256 devices in a mesh: req: 32 (over y, z_lo, core), tp: 8 (over x, z_hi).
Axes of the slice: x: 4, y: 4, z: 8 (z_hi: 2, z_lo: 4; z = z_hi * 4 + z_lo), core: 2. Of those that a mesh axis runs over, the one named last changes fastest.
Arguments:
- stream: bfloat16 [4096, 1792], P('req', 'tp'), may hold values from -6 to 6
- token_req: int32 [4096], P('req'), may hold values from 0 to 64, as said below
- request_leaf: int32 [64], replicated, may hold values from 10 to 31
- parent: int32 [32], replicated, may hold values from 0 to 9, as said below
- owner_map: int32 [32], replicated, may hold values from 0 to 31, each once
- node_state: bfloat16 [32, 16, 273, 112], P('req', 'tp')
- node_norm: bfloat16 [32, 16, 273], P('req', 'tp'), as said below
- node_tail: bfloat16 [32, 2, 1792], P('req', None, 'tp'), may hold values from -16 to 16
- mixer_gain: float32 [1792], replicated, may hold values from 0.5 to 1.5
- ffn_gain: float32 [1792], replicated, may hold values from 0.5 to 1.5
- query_weight: bfloat16 [1792, 256], P(None, 'tp'), may hold values from -0.125 to 0.125
- key_weight: bfloat16 [1792, 256], P(None, 'tp'), may hold values from -0.125 to 0.125
- value_weight: bfloat16 [1792, 1792], P(None, 'tp'), may hold values from -0.125 to 0.125
- conv_gate_weight: bfloat16 [1792, 1792], P(None, 'tp'), may hold values from -0.125 to 0.125
- conv_kernel: float32 [3, 1792], P(None, 'tp'), may hold values from -3 to 3
- out_weight: bfloat16 [1792, 1792], P('tp'), may hold values from -0.125 to 0.125
- ffn_gate: bfloat16 [1792, 4864], P(None, 'tp'), may hold values from -0.125 to 0.125
- ffn_up: bfloat16 [1792, 4864], P(None, 'tp'), may hold values from -0.125 to 0.125
- ffn_down: bfloat16 [4864, 1792], P('tp'), may hold values from -0.078125 to 0.078125
Outputs:
- layer_out: bfloat16 [4096, 1792], P('req', 'tp')
The draws below stay inside these ranges and needn't reach their ends.
Inputs may be any that keep to these rules, and one draw needn't show every extreme that they name: `token_req`: on the device at index d of req the slots hold, in order, the tokens of requests d * 2 to d * 2 + 1, each request 1 to 64 contiguous tokens, some request exactly that many, then padding slots with value 64; some device has padding. Nodes below 2 are roots and their own parents; nodes 2 to 9 have a root as parent; every other node has one of those as parent. `node_norm`: every row is a sum with positive weights of feature maps phi of key vectors.
All inputs are finite; a program needn't handle non-finite values.
Results may differ from the reference program's by a relative error of at most 0.019.
Values may be sent and summed in bfloat16 or wider, within the bound.
No kernel may reach another device: no remote copies, remote signals or barrier semaphores. Data moves between devices by JAX's collectives and lax.ppermute only.
A program may use at most 128 MiB of HBM per device.

```python
import math
import jax
import jax.numpy as jnp
from jax import lax

D = 1792
HEADS = 16
HD = 112
FD = 16
FEAT = 273
FF = 4864
KC = 3
TOK_DEV = 128
R_DEV = 2
NODE_DEV = 1
TOKENS = 4096
REQUESTS = 64
NODES = 32
ROOTS = 2
INNER = 8
N_REQ = 32


def draw_token_req(key, part):
    key_len, key_long, key_short = jax.random.split(jax.random.fold_in(key, 7), 3)
    longest = TOK_DEV // R_DEV
    total_req = N_REQ * R_DEV
    lengths = jax.random.randint(key_len, (total_req,), 1, longest + 1, dtype=jnp.int32)
    request_ids = jnp.arange(total_req, dtype=jnp.int32)
    long_device = jax.random.randint(key_long, (), 0, N_REQ, dtype=jnp.int32)
    short_device = (long_device + 1 + jax.random.randint(key_short, (), 0, N_REQ - 1, dtype=jnp.int32)) % N_REQ
    lengths = jnp.where(request_ids == long_device * R_DEV, longest, lengths)
    lengths = jnp.where(request_ids == short_device * R_DEV + R_DEV - 1, jnp.minimum(lengths, longest - 1), lengths)
    bounds = jnp.cumsum(lengths.reshape(N_REQ, R_DEV), axis=1)
    slot_ids = jnp.arange(TOK_DEV, dtype=jnp.int32)
    within = jnp.sum((slot_ids[None, :, None] >= bounds[:, None, :]).astype(jnp.int32), axis=2)
    firsts = (jnp.arange(N_REQ, dtype=jnp.int32) * R_DEV)[:, None]
    token_ids = jnp.where(within >= R_DEV, total_req, firsts + within)
    return token_ids.reshape(N_REQ * TOK_DEV).astype(jnp.int32)


def draw_parent(key, part):
    node_ids = jnp.arange(NODES, dtype=jnp.int32)
    key_upper, key_lower = jax.random.split(jax.random.fold_in(key, 5))
    upper_pick = jax.random.randint(key_upper, (NODES,), 0, ROOTS, dtype=jnp.int32)
    lower_pick = ROOTS + jax.random.randint(key_lower, (NODES,), 0, INNER, dtype=jnp.int32)
    return jnp.where(node_ids < ROOTS, node_ids, jnp.where(node_ids < ROOTS + INNER, upper_pick, lower_pick)).astype(jnp.int32)


def prefix_draw(key):
    key_mass, key_pseudo, key_state = jax.random.split(jax.random.fold_in(key, 11), 3)
    mass = jnp.exp(jax.random.uniform(key_mass, (NODES, HEADS, 4), jnp.float32, 0.0, math.log(16.0)))
    pseudo = jax.random.normal(key_pseudo, (NODES, HEADS, 4, FD), jnp.float32)
    unit_column = jnp.ones((NODES, HEADS, 4, 1), jnp.float32)
    square = (pseudo[:, :, :, :, None] * pseudo[:, :, :, None, :]).reshape(NODES, HEADS, 4, FD * FD) * (2.0 * FD) ** (-0.5)
    mapped = jnp.concatenate([unit_column, pseudo * FD ** (-0.25), square], axis=-1)
    norm_rows = jnp.sum(mass[:, :, :, None] * mapped, axis=2)
    spread = 0.2 * jnp.sum(mass, axis=2)
    state_rows = jax.random.normal(key_state, (NODES, HEADS, FEAT, HD), jnp.float32) * spread[:, :, None, None]
    return (state_rows, norm_rows)


def draw_node_state(key, part):
    state_rows, norm_rows = prefix_draw(key)
    return state_rows.astype(jnp.bfloat16)


def draw_node_norm(key, part):
    state_rows, norm_rows = prefix_draw(key)
    return norm_rows.astype(jnp.bfloat16)


def with_ends(array, key, smallest, top_value):
    dims = array.shape
    index_at = [jax.random.randint(jax.random.fold_in(key, axis), (), 0, dims[axis]) for axis in range(len(dims))]
    array = array.at[tuple(index_at)].set(smallest)
    longest = dims.index(max(dims))
    index_at[longest] = (index_at[longest] + 1) % dims[longest]
    return array.at[tuple(index_at)].set(top_value)


def steps_of(key, extent, pieces, low, top_value):
    def one(axis_at, shards_of):
        steps = jax.random.uniform(jax.random.fold_in(jax.random.fold_in(key, 6), axis_at), (shards_of,), jnp.float32, low / len(pieces), top_value / len(pieces))
        return jnp.repeat(jnp.exp(steps), extent[axis_at] // shards_of).reshape((-1,) + (1,) * (len(extent) - axis_at - 1))

    gain = one(*pieces[0])
    for cut in pieces[1:]:
        gain = gain * one(*cut)
    return gain


def noise(own_key, extent, deviation, most, pieces=(), kind=jnp.bfloat16):
    drawn = deviation * jax.random.normal(own_key, extent, jnp.float32)
    if pieces:
        drawn = drawn * steps_of(own_key, extent, pieces, -0.22, 0.18)
    return jnp.clip(drawn, -most, most).astype(kind)


def setup_inputs(seed: int = 0) -> dict:
    streams_of = jax.random.split(jax.random.key(seed), 20)
    stream = noise(streams_of[0], (TOKENS, D), 1.0, 6.0, ((0, 32), (1, 8)))
    token_req = draw_token_req(jax.random.fold_in(streams_of[19], 71), 0)
    request_leaf = with_ends(jax.random.randint(streams_of[2], (REQUESTS,), ROOTS + INNER, NODES), jax.random.fold_in(streams_of[2], 1), ROOTS + INNER, NODES - 1).astype(jnp.int32)
    parent = draw_parent(jax.random.fold_in(streams_of[19], 71), 0)
    owner_map = jax.random.permutation(streams_of[4], NODES).astype(jnp.int32)
    node_state = draw_node_state(jax.random.fold_in(streams_of[19], 71), 0)
    node_norm = draw_node_norm(jax.random.fold_in(streams_of[19], 71), 0)
    node_tail = noise(streams_of[7], (NODES, KC - 1, D), 4.0, 16.0, ((0, 32), (2, 8)))
    mixer_gain = jnp.clip(1.0 + 0.1 * jax.random.normal(streams_of[8], (D,), jnp.float32), 0.5, 1.5)
    ffn_gain = jnp.clip(1.0 + 0.1 * jax.random.normal(streams_of[9], (D,), jnp.float32), 0.5, 1.5)
    query_weight = noise(streams_of[10], (D, HEADS * FD), D ** -0.5, 0.125, ((1, 8),))
    key_weight = noise(streams_of[11], (D, HEADS * FD), D ** -0.5, 0.125, ((1, 8),))
    value_weight = noise(streams_of[12], (D, D), D ** -0.5, 0.125, ((1, 8),))
    conv_gate_weight = noise(streams_of[13], (D, D), D ** -0.5, 0.125, ((1, 8),))
    conv_kernel = noise(streams_of[14], (KC, D), 0.6, 3.0, ((1, 8),), jnp.float32)
    out_weight = noise(streams_of[15], (D, D), D ** -0.5, 0.125, ((0, 8),))
    ffn_gate = noise(streams_of[16], (D, FF), D ** -0.5, 0.125, ((1, 8),))
    ffn_up = noise(streams_of[17], (D, FF), D ** -0.5, 0.125, ((1, 8),))
    ffn_down = noise(streams_of[18], (FF, D), FF ** -0.5, 0.078125, ((0, 8),))
    return {"stream": stream, "token_req": token_req, "request_leaf": request_leaf, "parent": parent, "owner_map": owner_map, "node_state": node_state, "node_norm": node_norm, "node_tail": node_tail, "mixer_gain": mixer_gain, "ffn_gain": ffn_gain, "query_weight": query_weight, "key_weight": key_weight, "value_weight": value_weight, "conv_gate_weight": conv_gate_weight, "conv_kernel": conv_kernel, "out_weight": out_weight, "ffn_gate": ffn_gate, "ffn_up": ffn_up, "ffn_down": ffn_down}


EPSILON = 1e-05

def rms_scale(rows_in, gain_row):
    rows_in = rows_in.astype(jnp.float32)
    return rows_in * lax.rsqrt(lax.optimization_barrier(jnp.mean(rows_in * rows_in, axis=-1, keepdims=True)) + EPSILON) * gain_row

def taylor_map(projected, head_count):
    row_count = projected.shape[0]
    feature_dim = projected.shape[1] // head_count
    head_parts = projected.reshape(row_count, head_count, feature_dim)
    unit_column = jnp.ones((row_count, head_count, 1), jnp.float32)
    linear = head_parts * feature_dim ** (-0.25)
    square = (head_parts[:, :, :, None] * head_parts[:, :, None, :]).reshape(row_count, head_count, feature_dim * feature_dim) * (2.0 * feature_dim) ** (-0.5)
    return jnp.concatenate([unit_column, linear, square], axis=-1)

def token_layout(token_ids, first_request, per_device, total_req):
    row_count = token_ids.shape[0]
    slot_of_token = jnp.where(token_ids >= total_req, per_device, token_ids - first_request).astype(jnp.int32)
    slot_ids = jnp.arange(per_device + 1, dtype=jnp.int32)
    matches = slot_of_token[:, None] == slot_ids[None, :]
    amounts = lax.optimization_barrier(jnp.sum(matches.astype(jnp.int32), axis=0))
    starts = jnp.cumsum(amounts) - amounts
    offset = lax.optimization_barrier(jnp.sum(jnp.where(matches, starts[None, :], 0), axis=1))
    position = (jnp.arange(row_count, dtype=jnp.int32) - offset).astype(jnp.int32)
    return (slot_of_token, matches, position)

def path_rows(request_leaf, parent, owner_map, first_request, amount):
    leaf_nodes = lax.dynamic_slice_in_dim(request_leaf, first_request, amount)
    middle_nodes = parent[leaf_nodes]
    root_nodes = parent[middle_nodes]
    return (owner_map[leaf_nodes], owner_map[middle_nodes], owner_map[root_nodes])

def rounded_term(term):
    return lax.optimization_barrier(term.astype(jnp.bfloat16)).astype(jnp.float32)

def grouped_path_sum(table, leaf_rows, middle_rows, root_rows, per_group):
    first = table[leaf_rows].astype(jnp.float32)
    second = table[middle_rows].astype(jnp.float32)
    third = table[root_rows].astype(jnp.float32)
    shape_tail = (1,) * (first.ndim - 1)
    leaf_group = (leaf_rows // per_group).reshape((-1,) + shape_tail)
    middle_group = (middle_rows // per_group).reshape((-1,) + shape_tail)
    root_group = (root_rows // per_group).reshape((-1,) + shape_tail)
    zero = jnp.zeros_like(first)
    leaf_term = first + jnp.where(middle_group == leaf_group, second, zero) + jnp.where(root_group == leaf_group, third, zero)
    middle_term = jnp.where(middle_group != leaf_group, second + jnp.where(root_group == middle_group, third, zero), zero)
    root_term = jnp.where((root_group != leaf_group) & (root_group != middle_group), third, zero)
    return rounded_term(leaf_term) + rounded_term(middle_term) + rounded_term(root_term)

def short_conv(values, conv_gates, tail_rows, conv_kernel, slot_of_token, position, per_device):
    row_count, row_width = values.shape
    kernel_len = conv_kernel.shape[0]
    tail_ids = jnp.arange((per_device + 1) * (kernel_len - 1), dtype=jnp.int32)
    result = jnp.zeros((row_count, row_width), jnp.float32)
    for lag_index in range(kernel_len):
        if lag_index == 0:
            shifted = values
        else:
            shifted = jnp.concatenate([jnp.zeros((lag_index, row_width), values.dtype), values[:row_count - lag_index]], axis=0)
        back_pos = position - lag_index
        inside = back_pos >= 0
        tail_slot = slot_of_token * (kernel_len - 1) + (kernel_len - 1) + back_pos
        picker = ((tail_slot[:, None] == tail_ids[None, :]) & jnp.logical_not(inside)[:, None]).astype(jnp.bfloat16)
        from_tail = jnp.dot(picker, tail_rows, preferred_element_type=jnp.float32)
        tapped = jnp.where(inside[:, None], shifted.astype(jnp.float32), from_tail)
        result = result + conv_kernel[lag_index][None, :] * tapped
    return (result * jax.nn.silu(conv_gates)).astype(jnp.bfloat16)

def linear_attention(queries, keys_proj, mixed, prefix_state, prefix_norm, slot_of_token, matches, head_count):
    row_count = queries.shape[0]
    head_dim = mixed.shape[1] // head_count
    query_feat = taylor_map(queries, head_count).astype(jnp.bfloat16)
    key_feat = taylor_map(keys_proj, head_count).astype(jnp.bfloat16)
    scores = jnp.einsum('thf,shf->hts', query_feat.astype(jnp.float32), key_feat.astype(jnp.float32))
    row_ids = jnp.arange(row_count, dtype=jnp.int32)
    allowed = (slot_of_token[:, None] == slot_of_token[None, :]) & (row_ids[None, :] <= row_ids[:, None])
    masked = jnp.where(allowed[None, :, :], scores, 0.0)
    local_den = jnp.transpose(lax.optimization_barrier(jnp.sum(masked, axis=2)))
    value_heads = mixed.reshape(row_count, head_count, head_dim)
    local_num = jnp.einsum('hts,she->the', masked.astype(jnp.bfloat16).astype(jnp.float32), value_heads.astype(jnp.float32))
    selector = matches.astype(jnp.float32)
    prefix_all = jnp.einsum('thf,rhfe->thre', query_feat.astype(jnp.float32), prefix_state.astype(jnp.float32))
    prefix_num = jnp.einsum('thre,tr->the', prefix_all, selector, precision=lax.Precision.HIGHEST)
    norm_all = jnp.einsum('thf,rhf->thr', query_feat.astype(jnp.float32), prefix_norm, precision=lax.Precision.HIGHEST)
    prefix_den = jnp.einsum('thr,tr->th', norm_all, selector, precision=lax.Precision.HIGHEST)
    ratio = (local_num + prefix_num) / (local_den + prefix_den)[:, :, None]
    return ratio.astype(jnp.bfloat16).reshape(row_count, head_count * head_dim)

def reference(stream, token_req, request_leaf, parent, owner_map, node_state, node_norm, node_tail, mixer_gain, ffn_gain, query_weight, key_weight, value_weight, conv_gate_weight, conv_kernel, out_weight, ffn_gate, ffn_up, ffn_down):
    blocks_in = stream.reshape(N_REQ, TOK_DEV, D)
    ids_in = token_req.reshape(N_REQ, TOK_DEV)

    def one_block(packed):
        rows_in, ids_here, device = packed
        first_request = (device * R_DEV).astype(jnp.int32)
        leaf_rows, middle_rows, root_rows = path_rows(request_leaf, parent, owner_map, first_request, R_DEV)
        state_sum = grouped_path_sum(node_state, leaf_rows, middle_rows, root_rows, NODE_DEV)
        prefix_state = jnp.concatenate([state_sum.astype(jnp.bfloat16), jnp.zeros((1, HEADS, FEAT, HD), jnp.bfloat16)], axis=0)
        norm_sum = grouped_path_sum(node_norm, leaf_rows, middle_rows, root_rows, NODE_DEV)
        prefix_norm = jnp.concatenate([norm_sum, jnp.zeros((1, HEADS, FEAT), jnp.float32)], axis=0)
        tail_rows = jnp.concatenate([node_tail[leaf_rows], jnp.zeros((1, KC - 1, D), jnp.bfloat16)], axis=0).reshape((R_DEV + 1) * (KC - 1), D)
        slot_of_token, matches, position = token_layout(ids_here, first_request, R_DEV, REQUESTS)
        normed = rms_scale(rows_in, mixer_gain).astype(jnp.bfloat16)
        queries = jnp.dot(normed, query_weight, preferred_element_type=jnp.float32)
        keys_proj = jnp.dot(normed, key_weight, preferred_element_type=jnp.float32)
        values = jnp.dot(normed, value_weight, preferred_element_type=jnp.float32).astype(jnp.bfloat16)
        conv_gates = jnp.dot(normed, conv_gate_weight, preferred_element_type=jnp.float32)
        mixed = short_conv(values, conv_gates, tail_rows, conv_kernel, slot_of_token, position, R_DEV)
        attended = linear_attention(queries, keys_proj, mixed, prefix_state, prefix_norm, slot_of_token, matches, HEADS)
        partial_value = jnp.dot(attended, out_weight, preferred_element_type=jnp.float32)
        updated = (rows_in.astype(jnp.float32) + partial_value).astype(jnp.bfloat16)
        normed_two = rms_scale(updated, ffn_gain).astype(jnp.bfloat16)
        gate_part = jnp.dot(normed_two, ffn_gate, preferred_element_type=jnp.float32)
        up_part = jnp.dot(normed_two, ffn_up, preferred_element_type=jnp.float32)
        activated = (jax.nn.silu(gate_part) * up_part).astype(jnp.bfloat16)
        down_part = jnp.dot(activated, ffn_down, preferred_element_type=jnp.float32)
        return (updated.astype(jnp.float32) + down_part).astype(jnp.bfloat16)
    outputs = lax.map(one_block, (blocks_in, ids_in, jnp.arange(N_REQ, dtype=jnp.int32)))
    return outputs.reshape(TOKENS, D)
```

```python
import functools

import jax
import jax.numpy as jnp
import numpy as np
from jax import lax
from jax.experimental import pallas as pl
from jax.experimental.pallas import tpu as pltpu
from jax.sharding import PartitionSpec as P

EPSILON = 1e-05
ROWS = 160
LANES = 128
TAIL_ROW = 153
F32 = jnp.float32
BF16 = jnp.bfloat16

VMEM = pl.BlockSpec(memory_space=pltpu.VMEM)
SMEM = pl.BlockSpec(memory_space=pltpu.SMEM)
PARAMS = pltpu.CompilerParams(vmem_limit_bytes=48 * 1024 * 1024)


def call(kernel, out_shape, specs, args, scratch=(), name=None):
    single = not isinstance(out_shape, (list, tuple))
    return pl.pallas_call(
        kernel,
        out_shape=out_shape,
        in_specs=specs,
        out_specs=VMEM if single else [VMEM] * len(out_shape),
        scratch_shapes=list(scratch),
        compiler_params=PARAMS,
        name=name,
    )(*args)


def sds(shape, dtype):
    return jax.ShapeDtypeStruct(shape, dtype)


def fold_matrix(feat_dim, feat_count):
    fold = np.zeros((ROWS, feat_count), np.float32)
    row = 0
    for i in range(feat_dim):
        fold[row, 1 + i] = 1
        row += 1
    for gap in range(feat_dim // 2 + 1):
        for i in range(feat_dim if gap < feat_dim // 2 else feat_dim // 2):
            j = (i + gap) % feat_dim
            fold[row, 1 + feat_dim + feat_dim * i + j] = 1
            fold[row, 1 + feat_dim + feat_dim * j + i] = 1
            row += 1
    fold[row, 0] = 1
    return fold


def split_norm(total, head_dim):
    rounded = total.astype(BF16).astype(F32)
    lost = pltpu.roll(total - rounded, 1, axis=1)
    lane = lax.broadcasted_iota(jnp.int32, total.shape, 1)
    return jnp.where(lane == head_dim + 1, total + lost, total).astype(BF16)


def fold_kernel(fold_ref, state_ref, norm_ref, tail_ref, out_ref):
    heads, feats, head_dim = state_ref.shape
    fold = fold_ref[...]
    norms = lax.dot_general(fold, norm_ref[...], (((1,), (1,)), ((), ())), preferred_element_type=F32)
    lane = lax.broadcasted_iota(jnp.int32, (ROWS, LANES), 1)
    for h in range(heads):
        state = jnp.dot(fold, state_ref[h], preferred_element_type=F32)
        norm = jnp.broadcast_to(norms[:, h : h + 1], (ROWS, LANES))
        hi = norm.astype(BF16).astype(F32)
        cols = jnp.where(lane == head_dim, hi, jnp.where(lane == head_dim + 1, norm - hi, 0.0))
        out_ref[h] = cols.astype(BF16)
        out_ref[h, :, :head_dim] = state.astype(BF16)
        out_ref[h, TAIL_ROW : TAIL_ROW + 2, :head_dim] = tail_ref[h]


def select_kernel(groups, leaf_ref, parent_ref, owner_ref, dev_ref, mine_ref, other_ref, *rest):
    outs, pool = rest[:groups], rest[groups]
    held = mine_ref.shape[0]
    heads = mine_ref.shape[1]
    count = 2 * held
    for n in range(held):
        pool[n] = mine_ref[n]
        pool[held + n] = other_ref[n]
    pool[count] = jnp.zeros(pool.shape[1:], BF16)
    dev = dev_ref[0]
    total_dev = groups * count
    column = dev // count
    place = (dev % count) // 2
    core = dev % 2

    def slot(row):
        here = (row // count) == column
        at = (row % count) // 2
        k = lax.rem(place - at + held, held)
        k = k + jnp.where((row % 2) == core, 0, held)
        return jnp.where(here, k, count)

    per = leaf_ref.shape[0] // total_dev
    rows = lax.broadcasted_iota(jnp.int32, (ROWS, LANES), 0)
    is_tail = (rows >= TAIL_ROW) & (rows < TAIL_ROW + 2)
    for k in range(groups):
        target = lax.rem(dev + k * count, total_dev)
        for s in range(per):
            leaf = leaf_ref[target * per + s]
            middle = parent_ref[leaf]
            root = parent_ref[middle]
            at = [slot(owner_ref[n]) for n in (leaf, middle, root)]
            for h in range(heads):
                first, second, third = [pool[a, h].astype(F32) for a in at]
                total = first + jnp.where(is_tail, 0.0, second + third)
                outs[k][s, h] = split_norm(total, 112)


def place_blocks(scratch, blocks, half_ref):
    x = half_ref[0]
    z = half_ref[1]
    n = len(blocks)
    rows = blocks[0].shape[1]
    for k, block in enumerate(blocks):
        source = lax.rem(x - k + n, n)
        scratch[pl.ds(pl.multiple_of((2 * source + z) * rows, 32), rows), :] = block[0]
        scratch[pl.ds(pl.multiple_of((2 * source + 1 - z) * rows, 32), rows), :] = block[1]


def row_scale(scratch):
    rows = scratch[...].astype(F32)
    return lax.rsqrt(jnp.mean(rows * rows, axis=0, keepdims=True) + EPSILON)


def project_kernel(half_ref, own_ref, r1_ref, r2_ref, r3_ref, weight_ref, out_ref, scratch):
    place_blocks(scratch, [own_ref, r1_ref, r2_ref, r3_ref], half_ref)
    scale = row_scale(scratch)
    out_ref[...] = jnp.dot(weight_ref[...], scratch[...], preferred_element_type=F32) * scale


def silu(v):
    return v / (1.0 + jnp.exp(-v))


def mix_kernel(
    half_ref, first_ref, token_ref, proj_ref, taps_ref, p0_ref, p1_ref, p2_ref, p3_ref, out_weight_ref, *rest
):
    outs, attended_ref = rest[:4], rest[4]
    per, heads = p0_ref.shape[:2]
    head_dim = attended_ref.shape[0] // heads
    feat_dim = 16
    tokens = token_ref.shape[1]
    ids = token_ref[...]
    slot = jnp.where(ids >= first_ref[1], per, ids - first_ref[0])
    lane = lax.broadcasted_iota(jnp.int32, (1, tokens), 1)
    start = jnp.zeros((1, tokens), jnp.int32)
    for s in range(per):
        amount = jnp.sum((slot == s).astype(jnp.int32), axis=1, keepdims=True)
        start = start + jnp.where(slot > s, amount, 0)
    position = lane - start
    source = lax.broadcasted_iota(jnp.int32, (tokens, tokens), 0)
    target = lax.broadcasted_iota(jnp.int32, (tokens, tokens), 1)
    allowed = (source >= start) & (source <= target)
    width = heads * feat_dim
    payload_row = lax.broadcasted_iota(jnp.int32, (ROWS, tokens), 0)
    values_at = 2 * width
    gates_at = values_at + heads * head_dim
    for h in range(heads):
        query = proj_ref[h * feat_dim : (h + 1) * feat_dim, :]
        key = proj_ref[width + h * feat_dim : width + (h + 1) * feat_dim, :]
        value = proj_ref[values_at + h * head_dim : values_at + (h + 1) * head_dim, :].astype(BF16).astype(F32)
        gate = proj_ref[gates_at + h * head_dim : gates_at + (h + 1) * head_dim, :]
        linear = query * feat_dim ** (-0.25)
        blocks = [linear]
        for gap in range(feat_dim // 2):
            other = query if gap == 0 else pltpu.roll(query, feat_dim - gap, axis=0)
            blocks.append(query * other * (2.0 * feat_dim) ** (-0.5))
        half = feat_dim // 2
        blocks.append(query[:half] * query[half:] * (2.0 * feat_dim) ** (-0.5))
        one = (lax.broadcasted_iota(jnp.int32, (half, tokens), 0) == 0).astype(F32)
        blocks.append(one)
        feature = jnp.concatenate(blocks, axis=0)
        right = []
        states = []
        for s in range(per):
            total = (
                p0_ref[s, h].astype(F32) + p1_ref[s, h].astype(F32) + p2_ref[s, h].astype(F32) + p3_ref[s, h].astype(F32)
            )
            states.append(split_norm(total, head_dim))
            member = slot == s
            lag_one = (member & (position == 0) & (payload_row == TAIL_ROW + 1)).astype(F32)
            lag_two = (
                member
                & (
                    ((position == 0) & (payload_row == TAIL_ROW))
                    | ((position == 1) & (payload_row == TAIL_ROW + 1))
                )
            ).astype(F32)
            keep = jnp.where(member, feature, 0.0)
            right.append(jnp.concatenate([keep, lag_one, lag_two], axis=1).astype(BF16))
        state = jnp.concatenate(states, axis=0)
        reached = lax.dot_general(
            state, jnp.concatenate(right, axis=0), (((0,), (0,)), ((), ())), preferred_element_type=F32
        )
        prefix_num = reached[:head_dim, :tokens]
        prefix_den = reached[head_dim : head_dim + 1, :tokens] + reached[head_dim + 1 : head_dim + 2, :tokens]
        taps = taps_ref[h * head_dim : (h + 1) * head_dim, :]
        lagged_one = jnp.where(position >= 1, pltpu.roll(value, 1, axis=1), reached[:head_dim, tokens : 2 * tokens])
        lagged_two = jnp.where(
            position >= 2, pltpu.roll(value, 2, axis=1), reached[:head_dim, 2 * tokens : 3 * tokens]
        )
        conv = taps[:, 0:1] * value + taps[:, 1:2] * lagged_one + taps[:, 2:3] * lagged_two
        mixed = (conv * silu(gate)).astype(BF16)
        dots = lax.dot_general(
            key, query, (((0,), (0,)), ((), ())), preferred_element_type=F32, precision=lax.Precision.HIGHEST
        )
        scores = jnp.where(allowed, 1.0 + dots * feat_dim ** (-0.5) + dots * dots * (1.0 / (2.0 * feat_dim)), 0.0)
        local_den = jnp.sum(scores, axis=0, keepdims=True)
        local_num = jnp.dot(mixed, scores.astype(BF16), preferred_element_type=F32)
        attended_ref[h * head_dim : (h + 1) * head_dim, :] = (
            (local_num + prefix_num) / (local_den + prefix_den)
        ).astype(BF16)
    spread_blocks(outs, out_weight_ref, attended_ref[...], half_ref)


def spread_blocks(outs, weight_ref, right, half_ref):
    x = half_ref[0]
    z = half_ref[1]
    n = len(outs)
    rows = outs[0].shape[1]
    for k, out in enumerate(outs):
        to = lax.rem(x + k, n)
        for half, at in ((0, 2 * to + z), (1, 2 * to + 1 - z)):
            block = weight_ref[pl.ds(pl.multiple_of(at * rows, 32), rows), :]
            out[half] = jnp.dot(block, right, preferred_element_type=F32).astype(out.dtype)


def ffn_kernel(half_ref, own_ref, r1_ref, r2_ref, r3_ref, gate_ref, up_ref, down_ref, *rest):
    outs, scratch = rest[:4], rest[4]
    place_blocks(scratch, [own_ref, r1_ref, r2_ref, r3_ref], half_ref)
    scale = row_scale(scratch)
    gate = jnp.dot(gate_ref[...], scratch[...], preferred_element_type=F32) * scale
    up = jnp.dot(up_ref[...], scratch[...], preferred_element_type=F32) * scale
    spread_blocks(outs, down_ref, (silu(gate) * up).astype(BF16), half_ref)


def shards(
    stream, token_req, request_leaf, parent, owner_map, node_state, node_norm, node_tail, mixer_gain, ffn_gain,
    query_weight, key_weight, value_weight, conv_gate_weight, conv_kernel, out_weight, ffn_gate, ffn_up, ffn_down,
):
    tokens, width = stream.shape
    heads, feats, head_dim = node_state.shape[1:]
    feat_dim = query_weight.shape[1] // heads
    model = value_weight.shape[0]
    req_size = lax.axis_size("req")
    tp_size = lax.axis_size("tp")
    x_size = tp_size // 2
    y_size, z_size = 4, req_size // 8
    per = request_leaf.shape[0] // req_size
    dev = lax.axis_index("req")
    tp = lax.axis_index("tp")
    halves = jnp.stack([tp // 2, tp % 2]).astype(jnp.int32)

    def along_x(array, k):
        return lax.ppermute(array, "tp", [(i, ((i // 2 + k) % x_size) * 2 + i % 2) for i in range(tp_size)])

    def across_z(array):
        return lax.ppermute(array, "tp", [(i, i ^ 1) for i in range(tp_size)])

    def along_z(array, k):
        count = 2 * z_size
        return lax.ppermute(
            array, "req", [(i, (i // count) * count + (((i % count) // 2 + k) % z_size) * 2 + i % 2) for i in range(req_size)]
        )

    def across_core(array):
        return lax.ppermute(array, "req", [(i, i ^ 1) for i in range(req_size)])

    def along_y(array, k):
        return lax.ppermute(array, "req", [(i, (i + 2 * z_size * k) % req_size) for i in range(req_size)])

    order = (1, 3, 2)

    fold = jnp.asarray(fold_matrix(feat_dim, feats), BF16)
    tails = jnp.transpose(node_tail[0].reshape(2, heads, head_dim), (1, 0, 2))
    payload = call(
        fold_kernel, sds((heads, ROWS, LANES), BF16), [VMEM] * 4, (fold, node_state[0], node_norm[0], tails), name="fold"
    )
    from_z = {k: along_z(payload, k) for k in order}

    own = stream.T
    pair = jnp.stack([own, across_z(own)])

    mine = jnp.stack([payload, from_z[1], from_z[2], from_z[3]])
    other = across_core(mine)
    shares = call(
        functools.partial(select_kernel, y_size),
        [sds((per, heads, ROWS, LANES), BF16)] * y_size,
        [SMEM] * 4 + [VMEM] * 2,
        (request_leaf, parent, owner_map, dev.reshape(1), mine, other),
        scratch=[pltpu.VMEM((2 * z_size + 1, heads, ROWS, LANES), BF16)],
        name="select",
    )
    from_y = {k: along_y(shares[k], k) for k in order}

    rows = {k: along_x(pair, k) for k in order}
    weights = (
        jnp.concatenate([query_weight.T, key_weight.T, value_weight.T, conv_gate_weight.T], axis=0).astype(F32)
        * mixer_gain[None, :]
    ).astype(BF16)
    proj = call(
        project_kernel,
        sds((weights.shape[0], tokens), F32),
        [SMEM] + [VMEM] * 5,
        (halves, pair, rows[1], rows[2], rows[3], weights),
        scratch=[pltpu.VMEM((model, tokens), BF16)],
        name="project",
    )
    first = jnp.stack([dev * per, jnp.int32(request_leaf.shape[0])]).astype(jnp.int32)
    parts = call(
        mix_kernel,
        [sds((2, width, tokens), F32)] + [sds((2, width, tokens), BF16)] * (x_size - 1),
        [SMEM] * 2 + [VMEM] * 8,
        (
            halves, first, token_req.reshape(1, tokens), proj, conv_kernel.T,
            shares[0], from_y[1], from_y[2], from_y[3], out_weight.T,
        ),
        scratch=[pltpu.VMEM((width, tokens), BF16)],
        name="mix",
    )
    got = {k: along_x(parts[k], k) for k in order}
    share = parts[0] + got[1].astype(F32) + got[2].astype(F32) + got[3].astype(F32)
    share_peer = across_z(jnp.stack([share[1], share[0]]).astype(BF16))
    updated = (pair.astype(F32) + share + share_peer.astype(F32)).astype(BF16)

    wide = {k: along_x(updated, k) for k in order}
    gate_scaled = (ffn_gate.T.astype(F32) * ffn_gain[None, :]).astype(BF16)
    up_scaled = (ffn_up.T.astype(F32) * ffn_gain[None, :]).astype(BF16)
    downs = call(
        ffn_kernel,
        [sds((2, width, tokens), F32)] + [sds((2, width, tokens), BF16)] * (x_size - 1),
        [SMEM] + [VMEM] * 7,
        (halves, updated, wide[1], wide[2], wide[3], gate_scaled, up_scaled, ffn_down.T),
        scratch=[pltpu.VMEM((model, tokens), BF16)],
        name="ffn",
    )
    back = {k: along_x(downs[k], k) for k in order}
    down_share = downs[0] + back[1].astype(F32) + back[2].astype(F32) + back[3].astype(F32)
    down_peer = across_z(down_share[1].astype(BF16))
    result = updated[0].astype(F32) + down_share[0] + down_peer.astype(F32)
    return result.astype(BF16).T


def solution(mesh):
    in_specs = (
        P("req", "tp"), P("req"), P(), P(), P(), P("req", "tp", None, None), P("req", "tp", None), P("req", None, "tp"),
        P(), P(), P(None, "tp"), P(None, "tp"), P(None, "tp"), P(None, "tp"), P(None, "tp"), P("tp", None),
        P(None, "tp"), P(None, "tp"), P("tp", None),
    )
    return jax.shard_map(shards, mesh=mesh, in_specs=in_specs, out_specs=P("req", "tp"), check_vma=False)
```

```python
import functools

import jax
import jax.numpy as jnp
import numpy as np
from jax import lax
from jax.experimental import pallas as pl
from jax.experimental.pallas import tpu as pltpu
from jax.sharding import PartitionSpec as P

EPSILON = 1e-05
ROWS = 160
LANES = 128
TAIL_ROW = 153
F32 = jnp.float32
BF16 = jnp.bfloat16

VMEM = pl.BlockSpec(memory_space=pltpu.VMEM)
SMEM = pl.BlockSpec(memory_space=pltpu.SMEM)
PARAMS = pltpu.CompilerParams(vmem_limit_bytes=12 * 1024 * 1024)


def call(kernel, out_shape, specs, args, scratch=(), name=None):
    single = not isinstance(out_shape, (list, tuple))
    return pl.pallas_call(
        kernel,
        out_shape=out_shape,
        in_specs=specs,
        out_specs=VMEM if single else [VMEM] * len(out_shape),
        scratch_shapes=list(scratch),
        compiler_params=PARAMS,
        name=name,
    )(*args)


def sds(shape, dtype):
    return jax.ShapeDtypeStruct(shape, dtype)


def fold_matrix(feat_dim, feat_count):
    fold = np.zeros((ROWS, feat_count), np.float32)
    row = 0
    for i in range(feat_dim):
        fold[row, 1 + i] = 1
        row += 1
    for gap in range(feat_dim // 2 + 1):
        for i in range(feat_dim if gap < feat_dim // 2 else feat_dim // 2):
            j = (i + gap) % feat_dim
            fold[row, 1 + feat_dim + feat_dim * i + j] = 1
            fold[row, 1 + feat_dim + feat_dim * j + i] = 1
            row += 1
    fold[row, 0] = 1
    return fold


def split_norm(total, head_dim):
    rounded = total.astype(BF16).astype(F32)
    lost = pltpu.roll(total - rounded, 1, axis=1)
    lane = lax.broadcasted_iota(jnp.int32, total.shape, 1)
    return jnp.where(lane == head_dim + 1, total + lost, total).astype(BF16)


def fold_kernel(fold_ref, state_ref, norm_ref, tail_ref, out_ref):
    feats, heads, head_dim = state_ref.shape
    fold = fold_ref[...]
    norms = lax.dot_general(fold, norm_ref[...], (((1,), (1,)), ((), ())), preferred_element_type=F32)
    lane = lax.broadcasted_iota(jnp.int32, (ROWS, LANES), 1)
    for h in range(heads):
        state = jnp.dot(fold, state_ref[:, h, :], preferred_element_type=F32)
        norm = jnp.broadcast_to(norms[:, h : h + 1], (ROWS, LANES))
        hi = norm.astype(BF16).astype(F32)
        cols = jnp.where(lane == head_dim, hi, jnp.where(lane == head_dim + 1, norm - hi, 0.0))
        out_ref[h] = cols.astype(BF16)
        out_ref[h, :, :head_dim] = state.astype(BF16)
        out_ref[h, TAIL_ROW : TAIL_ROW + 2, :head_dim] = tail_ref[:, h * head_dim : (h + 1) * head_dim]


def select_kernel(groups, leaf_ref, parent_ref, owner_ref, dev_ref, mine_ref, other_ref, *rest):
    outs, pool = rest[:groups], rest[groups]
    held = mine_ref.shape[0]
    heads = mine_ref.shape[1]
    count = 2 * held
    for n in range(held):
        pool[n] = mine_ref[n]
        pool[held + n] = other_ref[n]
    pool[count] = jnp.zeros(pool.shape[1:], BF16)
    dev = dev_ref[0]
    total_dev = groups * count
    column = dev // count
    place = (dev % count) // 2
    core = dev % 2

    def slot(row):
        here = (row // count) == column
        at = (row % count) // 2
        k = lax.rem(place - at + held, held)
        k = k + jnp.where((row % 2) == core, 0, held)
        return jnp.where(here, k, count)

    per = leaf_ref.shape[0] // total_dev
    rows = lax.broadcasted_iota(jnp.int32, (ROWS, LANES), 0)
    is_tail = (rows >= TAIL_ROW) & (rows < TAIL_ROW + 2)
    for k in range(groups):
        target = lax.rem(dev + k * count, total_dev)
        for s in range(per):
            leaf = leaf_ref[target * per + s]
            middle = parent_ref[leaf]
            root = parent_ref[middle]
            at = [slot(owner_ref[n]) for n in (leaf, middle, root)]
            for h in range(heads):
                first, second, third = [pool[a, h].astype(F32) for a in at]
                total = first + jnp.where(is_tail, 0.0, second + third)
                outs[k][s, h] = split_norm(total, 112)


def place_blocks(scratch, blocks, half_ref):
    x = half_ref[0]
    z = half_ref[1]
    n = len(blocks)
    rows = blocks[0].shape[1]
    for k, block in enumerate(blocks):
        source = lax.rem(x - k + n, n)
        scratch[pl.ds(pl.multiple_of((2 * source + z) * rows, 32), rows), :] = block[0]
        scratch[pl.ds(pl.multiple_of((2 * source + 1 - z) * rows, 32), rows), :] = block[1]


def row_scale(scratch):
    rows = scratch[...].astype(F32)
    return lax.rsqrt(jnp.mean(rows * rows, axis=0, keepdims=True) + EPSILON)


def project_kernel(half_ref, own_ref, r1_ref, r2_ref, r3_ref, weight_ref, out_ref, scratch):
    place_blocks(scratch, [own_ref, r1_ref, r2_ref, r3_ref], half_ref)
    scale = row_scale(scratch)
    out_ref[...] = jnp.dot(weight_ref[...], scratch[...], preferred_element_type=F32) * scale


def silu(v):
    return v / (1.0 + jnp.exp(-v))


def mix_kernel(
    half_ref, first_ref, token_ref, proj_ref, taps_ref, p0_ref, p1_ref, p2_ref, p3_ref, out_weight_ref, *rest
):
    outs, attended_ref = rest[:4], rest[4]
    per, heads = p0_ref.shape[:2]
    head_dim = attended_ref.shape[0] // heads
    feat_dim = 16
    tokens = token_ref.shape[1]
    ids = token_ref[...]
    slot = jnp.where(ids >= first_ref[1], per, ids - first_ref[0])
    lane = lax.broadcasted_iota(jnp.int32, (1, tokens), 1)
    start = jnp.zeros((1, tokens), jnp.int32)
    for s in range(per):
        amount = jnp.sum((slot == s).astype(jnp.int32), axis=1, keepdims=True)
        start = start + jnp.where(slot > s, amount, 0)
    position = lane - start
    source = lax.broadcasted_iota(jnp.int32, (tokens, tokens), 0)
    target = lax.broadcasted_iota(jnp.int32, (tokens, tokens), 1)
    allowed = (source >= start) & (source <= target)
    width = heads * feat_dim
    payload_row = lax.broadcasted_iota(jnp.int32, (ROWS, tokens), 0)
    values_at = 2 * width
    gates_at = values_at + heads * head_dim
    for h in range(heads):
        query = proj_ref[h * feat_dim : (h + 1) * feat_dim, :]
        key = proj_ref[width + h * feat_dim : width + (h + 1) * feat_dim, :]
        value = proj_ref[values_at + h * head_dim : values_at + (h + 1) * head_dim, :].astype(BF16).astype(F32)
        gate = proj_ref[gates_at + h * head_dim : gates_at + (h + 1) * head_dim, :]
        linear = query * feat_dim ** (-0.25)
        blocks = [linear]
        for gap in range(feat_dim // 2):
            other = query if gap == 0 else pltpu.roll(query, feat_dim - gap, axis=0)
            blocks.append(query * other * (2.0 * feat_dim) ** (-0.5))
        half = feat_dim // 2
        blocks.append(query[:half] * query[half:] * (2.0 * feat_dim) ** (-0.5))
        one = (lax.broadcasted_iota(jnp.int32, (half, tokens), 0) == 0).astype(F32)
        blocks.append(one)
        feature = jnp.concatenate(blocks, axis=0)
        right = []
        states = []
        for s in range(per):
            total = (
                p0_ref[s, h].astype(F32) + p1_ref[s, h].astype(F32) + p2_ref[s, h].astype(F32) + p3_ref[s, h].astype(F32)
            )
            states.append(split_norm(total, head_dim))
            member = slot == s
            lag_one = (member & (position == 0) & (payload_row == TAIL_ROW + 1)).astype(F32)
            lag_two = (
                member
                & (
                    ((position == 0) & (payload_row == TAIL_ROW))
                    | ((position == 1) & (payload_row == TAIL_ROW + 1))
                )
            ).astype(F32)
            keep = jnp.where(member, feature, 0.0)
            right.append(jnp.concatenate([keep, lag_one, lag_two], axis=1).astype(BF16))
        state = jnp.concatenate(states, axis=0)
        reached = lax.dot_general(
            state, jnp.concatenate(right, axis=0), (((0,), (0,)), ((), ())), preferred_element_type=F32
        )
        prefix_num = reached[:head_dim, :tokens]
        prefix_den = reached[head_dim : head_dim + 1, :tokens] + reached[head_dim + 1 : head_dim + 2, :tokens]
        taps = taps_ref[h * head_dim : (h + 1) * head_dim, :]
        lagged_one = jnp.where(position >= 1, pltpu.roll(value, 1, axis=1), reached[:head_dim, tokens : 2 * tokens])
        lagged_two = jnp.where(
            position >= 2, pltpu.roll(value, 2, axis=1), reached[:head_dim, 2 * tokens : 3 * tokens]
        )
        conv = taps[:, 0:1] * value + taps[:, 1:2] * lagged_one + taps[:, 2:3] * lagged_two
        mixed = (conv * silu(gate)).astype(BF16)
        dots = lax.dot_general(
            key, query, (((0,), (0,)), ((), ())), preferred_element_type=F32, precision=lax.Precision.HIGHEST
        )
        scores = jnp.where(allowed, 1.0 + dots * feat_dim ** (-0.5) + dots * dots * (1.0 / (2.0 * feat_dim)), 0.0)
        local_den = jnp.sum(scores, axis=0, keepdims=True)
        local_num = jnp.dot(mixed, scores.astype(BF16), preferred_element_type=F32)
        attended_ref[h * head_dim : (h + 1) * head_dim, :] = (
            (local_num + prefix_num) / (local_den + prefix_den)
        ).astype(BF16)
    spread_blocks(outs, out_weight_ref, attended_ref[...], half_ref)


def spread_blocks(outs, weight_ref, right, half_ref):
    x = half_ref[0]
    z = half_ref[1]
    n = len(outs)
    rows = outs[0].shape[1]
    for k, out in enumerate(outs):
        to = lax.rem(x + k, n)
        for half, at in ((0, 2 * to + z), (1, 2 * to + 1 - z)):
            block = weight_ref[pl.ds(pl.multiple_of(at * rows, 32), rows), :]
            out[half] = jnp.dot(block, right, preferred_element_type=F32).astype(out.dtype)


def ffn_kernel(half_ref, own_ref, r1_ref, r2_ref, r3_ref, gate_ref, up_ref, down_ref, *rest):
    outs, scratch = rest[:4], rest[4]
    place_blocks(scratch, [own_ref, r1_ref, r2_ref, r3_ref], half_ref)
    scale = row_scale(scratch)
    gate = jnp.dot(gate_ref[...], scratch[...], preferred_element_type=F32) * scale
    up = jnp.dot(up_ref[...], scratch[...], preferred_element_type=F32) * scale
    spread_blocks(outs, down_ref, (silu(gate) * up).astype(BF16), half_ref)


def shards(
    stream, token_req, request_leaf, parent, owner_map, node_state, node_norm, node_tail, mixer_gain, ffn_gain,
    query_weight, key_weight, value_weight, conv_gate_weight, conv_kernel, out_weight, ffn_gate, ffn_up, ffn_down,
):
    tokens, width = stream.shape
    heads, feats, head_dim = node_state.shape[1:]
    feat_dim = query_weight.shape[1] // heads
    model = value_weight.shape[0]
    req_size = lax.axis_size("req")
    tp_size = lax.axis_size("tp")
    x_size = tp_size // 2
    y_size, z_size = 4, req_size // 8
    per = request_leaf.shape[0] // req_size
    dev = lax.axis_index("req")
    tp = lax.axis_index("tp")
    halves = jnp.stack([tp // 2, tp % 2]).astype(jnp.int32)

    def along_x(array, k):
        return lax.ppermute(array, "tp", [(i, ((i // 2 + k) % x_size) * 2 + i % 2) for i in range(tp_size)])

    def across_z(array):
        return lax.ppermute(array, "tp", [(i, i ^ 1) for i in range(tp_size)])

    def along_z(array, k):
        count = 2 * z_size
        return lax.ppermute(
            array, "req", [(i, (i // count) * count + (((i % count) // 2 + k) % z_size) * 2 + i % 2) for i in range(req_size)]
        )

    def across_core(array):
        return lax.ppermute(array, "req", [(i, i ^ 1) for i in range(req_size)])

    def along_y(array, k):
        return lax.ppermute(array, "req", [(i, (i + 2 * z_size * k) % req_size) for i in range(req_size)])

    order = (1, 3, 2)

    fold = jnp.asarray(fold_matrix(feat_dim, feats), BF16)
    whole = pl.BlockSpec()
    payload = call(
        fold_kernel,
        sds((heads, ROWS, LANES), BF16),
        [whole] * 4,
        (fold, jnp.transpose(node_state[0], (1, 0, 2)), node_norm[0], node_tail[0]),
        name="fold",
    )
    payload, own = lax.optimization_barrier((payload, stream.T))
    from_z = {k: along_z(payload, k) for k in order}

    pair = jnp.stack([own, across_z(own)])

    mine = jnp.stack([payload, from_z[1], from_z[2], from_z[3]])
    other = across_core(mine)
    shares = call(
        functools.partial(select_kernel, y_size),
        [sds((per, heads, ROWS, LANES), BF16)] * y_size,
        [SMEM] * 4 + [VMEM] * 2,
        (request_leaf, parent, owner_map, dev.reshape(1), mine, other),
        scratch=[pltpu.VMEM((2 * z_size + 1, heads, ROWS, LANES), BF16)],
        name="select",
    )
    from_y = {k: along_y(shares[k], k) for k in order}

    rows = {k: along_x(pair, k) for k in order}
    weights = (
        jnp.concatenate([query_weight.T, key_weight.T, value_weight.T, conv_gate_weight.T], axis=0).astype(F32)
        * mixer_gain[None, :]
    ).astype(BF16)
    proj = call(
        project_kernel,
        sds((weights.shape[0], tokens), F32),
        [SMEM] + [VMEM] * 5,
        (halves, pair, rows[1], rows[2], rows[3], weights),
        scratch=[pltpu.VMEM((model, tokens), BF16)],
        name="project",
    )
    first = jnp.stack([dev * per, jnp.int32(request_leaf.shape[0])]).astype(jnp.int32)
    parts = call(
        mix_kernel,
        [sds((2, width, tokens), F32)] + [sds((2, width, tokens), BF16)] * (x_size - 1),
        [SMEM] * 2 + [VMEM] * 8,
        (
            halves, first, token_req.reshape(1, tokens), proj, conv_kernel.T,
            shares[0], from_y[1], from_y[2], from_y[3], out_weight.T,
        ),
        scratch=[pltpu.VMEM((width, tokens), BF16)],
        name="mix",
    )
    got = {k: along_x(parts[k], k) for k in order}
    share = parts[0] + got[1].astype(F32) + got[2].astype(F32) + got[3].astype(F32)
    crossing, gate_in, up_in, down_in = lax.optimization_barrier(
        (jnp.stack([share[1], share[0]]).astype(BF16), ffn_gate, ffn_up, ffn_down)
    )
    share_peer = across_z(crossing)
    gate_scaled = (gate_in.T.astype(F32) * ffn_gain[None, :]).astype(BF16)
    up_scaled = (up_in.T.astype(F32) * ffn_gain[None, :]).astype(BF16)
    updated = (pair.astype(F32) + share + share_peer.astype(F32)).astype(BF16)
    updated, gate_scaled, up_scaled, down_turned = lax.optimization_barrier(
        (updated, gate_scaled, up_scaled, down_in.T)
    )

    wide = {k: along_x(updated, k) for k in order}
    downs = call(
        ffn_kernel,
        [sds((2, width, tokens), F32)] + [sds((2, width, tokens), BF16)] * (x_size - 1),
        [SMEM] + [VMEM] * 7,
        (halves, updated, wide[1], wide[2], wide[3], gate_scaled, up_scaled, down_turned),
        scratch=[pltpu.VMEM((model, tokens), BF16)],
        name="ffn",
    )
    back = {k: along_x(downs[k], k) for k in order}
    down_share = downs[0] + back[1].astype(F32) + back[2].astype(F32) + back[3].astype(F32)
    down_peer = across_z(down_share[1].astype(BF16))
    result = updated[0].astype(F32) + down_share[0] + down_peer.astype(F32)
    return result.astype(BF16).T


def solution(mesh):
    in_specs = (
        P("req", "tp"), P("req"), P(), P(), P(), P("req", "tp", None, None), P("req", "tp", None), P("req", None, "tp"),
        P(), P(), P(None, "tp"), P(None, "tp"), P(None, "tp"), P(None, "tp"), P(None, "tp"), P("tp", None),
        P(None, "tp"), P(None, "tp"), P("tp", None),
    )
    return jax.shard_map(shards, mesh=mesh, in_specs=in_specs, out_specs=P("req", "tp"), check_vma=False)
```

```python
import functools

import jax
import jax.numpy as jnp
import numpy as np
from jax import lax
from jax.experimental import pallas as pl
from jax.experimental.pallas import tpu as pltpu
from jax.sharding import PartitionSpec as P

EPSILON = 1e-05
ROWS = 160
LANES = 128
TAIL_ROW = 153
F32 = jnp.float32
BF16 = jnp.bfloat16

VMEM = pl.BlockSpec(memory_space=pltpu.VMEM)
SMEM = pl.BlockSpec(memory_space=pltpu.SMEM)
PARAMS = pltpu.CompilerParams(vmem_limit_bytes=12 * 1024 * 1024)


def call(kernel, out_shape, specs, args, scratch=(), name=None):
    single = not isinstance(out_shape, (list, tuple))
    return pl.pallas_call(
        kernel,
        out_shape=out_shape,
        in_specs=specs,
        out_specs=VMEM if single else [VMEM] * len(out_shape),
        scratch_shapes=list(scratch),
        compiler_params=PARAMS,
        name=name,
    )(*args)


def sds(shape, dtype):
    return jax.ShapeDtypeStruct(shape, dtype)


def fold_matrix(feat_dim, feat_count):
    fold = np.zeros((ROWS, feat_count), np.float32)
    row = 0
    for i in range(feat_dim):
        fold[row, 1 + i] = 1
        row += 1
    for gap in range(feat_dim // 2 + 1):
        for i in range(feat_dim if gap < feat_dim // 2 else feat_dim // 2):
            j = (i + gap) % feat_dim
            fold[row, 1 + feat_dim + feat_dim * i + j] = 1
            fold[row, 1 + feat_dim + feat_dim * j + i] = 1
            row += 1
    fold[row, 0] = 1
    return fold


def split_norm(total, head_dim):
    rounded = total.astype(BF16).astype(F32)
    lost = pltpu.roll(total - rounded, 1, axis=1)
    lane = lax.broadcasted_iota(jnp.int32, total.shape, 1)
    return jnp.where(lane == head_dim + 1, total + lost, total).astype(BF16)


def fold_kernel(fold_hbm, state_hbm, norm_hbm, tail_hbm, out_ref, fold_ref, state_ref, norm_ref, tail_ref, sems):
    pairs = ((state_hbm, state_ref), (fold_hbm, fold_ref), (norm_hbm, norm_ref), (tail_hbm, tail_ref))
    copies = [pltpu.make_async_copy(a, b, sems.at[i]) for i, (a, b) in enumerate(pairs)]
    for copy in copies:
        copy.start()
    for copy in copies:
        copy.wait()
    feats, heads, head_dim = state_ref.shape
    fold = fold_ref[...]
    norms = lax.dot_general(fold, norm_ref[...], (((1,), (1,)), ((), ())), preferred_element_type=F32)
    lane = lax.broadcasted_iota(jnp.int32, (ROWS, LANES), 1)
    for h in range(heads):
        state = jnp.dot(fold, state_ref[:, h, :], preferred_element_type=F32)
        norm = jnp.broadcast_to(norms[:, h : h + 1], (ROWS, LANES))
        hi = norm.astype(BF16).astype(F32)
        cols = jnp.where(lane == head_dim, hi, jnp.where(lane == head_dim + 1, norm - hi, 0.0))
        out_ref[h] = cols.astype(BF16)
        out_ref[h, :, :head_dim] = state.astype(BF16)
        out_ref[h, TAIL_ROW : TAIL_ROW + 2, :head_dim] = tail_ref[:, h * head_dim : (h + 1) * head_dim]


def select_kernel(groups, shifts, leaf_ref, parent_ref, owner_ref, mine_ref, other_ref, *rest):
    outs, pool = rest[:-1], rest[-1]
    held = mine_ref.shape[0]
    heads = mine_ref.shape[1]
    count = 2 * held
    for n in range(held):
        pool[n] = mine_ref[n]
        pool[held + n] = other_ref[n]
    pool[count] = jnp.zeros(pool.shape[1:], BF16)
    dev = lax.axis_index("req")
    total_dev = groups * count
    column = dev // count
    place = (dev % count) // 2
    core = dev % 2

    def slot(row):
        here = (row // count) == column
        at = (row % count) // 2
        k = lax.rem(place - at + held, held)
        k = k + jnp.where((row % 2) == core, 0, held)
        return jnp.where(here, k, count)

    per = leaf_ref.shape[0] // total_dev
    rows = lax.broadcasted_iota(jnp.int32, (ROWS, LANES), 0)
    is_tail = (rows >= TAIL_ROW) & (rows < TAIL_ROW + 2)
    for out, k in zip(outs, shifts):
        target = lax.rem(dev + k * count, total_dev)
        for s in range(per):
            leaf = leaf_ref[target * per + s]
            middle = parent_ref[leaf]
            root = parent_ref[middle]
            at = [slot(owner_ref[n]) for n in (leaf, middle, root)]
            for h in range(heads):
                first, second, third = [pool[a, h].astype(F32) for a in at]
                total = first + jnp.where(is_tail, 0.0, second + third)
                out[s, h] = split_norm(total, 112)


def tp_place():
    index = lax.axis_index("tp")
    return index >> 1, index & 1


def place_blocks(scratch, blocks):
    x, z = tp_place()
    n = len(blocks)
    rows = blocks[0].shape[1]
    for k, block in enumerate(blocks):
        source = lax.rem(x - k + n, n)
        scratch[pl.ds(pl.multiple_of((2 * source + z) * rows, 32), rows), :] = block[0]
        scratch[pl.ds(pl.multiple_of((2 * source + 1 - z) * rows, 32), rows), :] = block[1]


def scaled_rows(scratch, gain_ref):
    gain = gain_ref[...].T
    squares = jnp.zeros((LANES, scratch.shape[1]), F32)
    for j in range(scratch.shape[0] // LANES):
        rows = scratch[j * LANES : (j + 1) * LANES, :].astype(F32)
        squares = squares + rows * rows
        scratch[j * LANES : (j + 1) * LANES, :] = (rows * gain[:, j : j + 1]).astype(BF16)
    mean = jnp.sum(squares, axis=0, keepdims=True) / scratch.shape[0]
    return lax.rsqrt(mean + EPSILON)


def silu(v):
    return v / (1.0 + jnp.exp(-v))


def local_kernel(
    total_req, own_ref, r1_ref, r2_ref, r3_ref, gain_ref, token_ref, query_ref, key_ref, value_ref, gate_ref,
    taps_ref, conv_ref, silu_ref, scores_ref, den_ref, right_ref, turned_ref, scratch,
):
    place_blocks(scratch, [own_ref, r1_ref, r2_ref, r3_ref])
    scale = scaled_rows(scratch, gain_ref)
    rows = scratch[...]
    queries = jnp.dot(query_ref[...], rows, preferred_element_type=F32) * scale
    keys = jnp.dot(key_ref[...], rows, preferred_element_type=F32) * scale
    values = (jnp.dot(value_ref[...], rows, preferred_element_type=F32) * scale).astype(BF16).astype(F32)
    gates = jnp.dot(gate_ref[...], rows, preferred_element_type=F32) * scale
    heads = scores_ref.shape[0]
    per = right_ref.shape[1] // ROWS
    feat_dim = queries.shape[0] // heads
    tokens = token_ref.shape[1]
    ids = token_ref[...]
    slot = jnp.where(ids >= total_req, per, ids - lax.axis_index("req") * per)
    lane = lax.broadcasted_iota(jnp.int32, (1, tokens), 1)
    start = jnp.zeros((1, tokens), jnp.int32)
    for s in range(per):
        amount = jnp.sum((slot == s).astype(jnp.int32), axis=1, keepdims=True)
        start = start + jnp.where(slot > s, amount, 0)
    position = lane - start
    source = lax.broadcasted_iota(jnp.int32, (tokens, tokens), 0)
    target = lax.broadcasted_iota(jnp.int32, (tokens, tokens), 1)
    allowed = (source >= start) & (source <= target)
    turned = jnp.concatenate([taps_ref[...], jnp.zeros((5, taps_ref.shape[1]), F32)], axis=0).T
    turned_ref[...] = turned
    taps = turned
    conv_ref[...] = (
        taps[:, 0:1] * values
        + taps[:, 1:2] * jnp.where(position >= 1, pltpu.roll(values, 1, axis=1), 0.0)
        + taps[:, 2:3] * jnp.where(position >= 2, pltpu.roll(values, 2, axis=1), 0.0)
    )
    silu_ref[...] = silu(gates)
    payload_row = lax.broadcasted_iota(jnp.int32, (ROWS, tokens), 0)
    lag_one = (position == 0) & (payload_row == TAIL_ROW + 1)
    lag_two = ((position == 0) & (payload_row == TAIL_ROW)) | ((position == 1) & (payload_row == TAIL_ROW + 1))
    half = feat_dim // 2
    one = (lax.broadcasted_iota(jnp.int32, (half, tokens), 0) == 0).astype(F32)
    for h in range(heads):
        query = queries[h * feat_dim : (h + 1) * feat_dim]
        key = keys[h * feat_dim : (h + 1) * feat_dim]
        blocks = [query * feat_dim ** (-0.25)]
        for gap in range(half):
            other = query if gap == 0 else pltpu.roll(query, feat_dim - gap, axis=0)
            blocks.append(query * other * (2.0 * feat_dim) ** (-0.5))
        blocks.append(query[:half] * query[half:] * (2.0 * feat_dim) ** (-0.5))
        blocks.append(one)
        feature = jnp.concatenate(blocks, axis=0)
        for s in range(per):
            member = slot == s
            at = slice(s * ROWS, (s + 1) * ROWS)
            right_ref[h, at, :tokens] = jnp.where(member, feature, 0.0).astype(BF16)
            right_ref[h, at, tokens : 2 * tokens] = (member & lag_one).astype(F32).astype(BF16)
            right_ref[h, at, 2 * tokens :] = (member & lag_two).astype(F32).astype(BF16)
        dots = lax.dot_general(
            key, query, (((0,), (0,)), ((), ())), preferred_element_type=F32, precision=lax.Precision.HIGHEST
        )
        scores = jnp.where(allowed, 1.0 + dots * feat_dim ** (-0.5) + dots * dots * (1.0 / (2.0 * feat_dim)), 0.0)
        den_ref[h] = jnp.sum(scores, axis=0, keepdims=True)
        scores_ref[h] = scores.astype(BF16)


def turn_kernel(in_ref, out_ref):
    for j in range(out_ref.shape[0] // LANES):
        at = slice(j * LANES, (j + 1) * LANES)
        out_ref[at, :] = in_ref[:, at].T


def turn(weight, name):
    return call(turn_kernel, sds(weight.shape[::-1], weight.dtype), [VMEM], (weight,), name=name)


def mix_kernel(
    conv_ref, silu_ref, scores_ref, den_ref, right_ref, taps_ref, p0_ref, p1_ref, p2_ref, p3_ref,
    out_weight_ref, *rest,
):
    outs, attended_ref = rest[:4], rest[4]
    per, heads = p0_ref.shape[:2]
    head_dim = attended_ref.shape[0] // heads
    tokens = attended_ref.shape[1]
    for h in range(heads):
        states = []
        for s in range(per):
            total = (
                p0_ref[s, h].astype(F32) + p1_ref[s, h].astype(F32) + p2_ref[s, h].astype(F32) + p3_ref[s, h].astype(F32)
            )
            states.append(split_norm(total, head_dim))
        reached = lax.dot_general(
            jnp.concatenate(states, axis=0), right_ref[h], (((0,), (0,)), ((), ())), preferred_element_type=F32
        )
        prefix_num = reached[:head_dim, :tokens]
        prefix_den = reached[head_dim : head_dim + 1, :tokens] + reached[head_dim + 1 : head_dim + 2, :tokens]
        at = slice(h * head_dim, (h + 1) * head_dim)
        taps = taps_ref[at, :]
        conv = (
            conv_ref[at, :]
            + taps[:, 1:2] * reached[:head_dim, tokens : 2 * tokens]
            + taps[:, 2:3] * reached[:head_dim, 2 * tokens :]
        )
        mixed = (conv * silu_ref[at, :]).astype(BF16)
        local_num = jnp.dot(mixed, scores_ref[h], preferred_element_type=F32)
        attended_ref[at, :] = ((local_num + prefix_num) / (den_ref[h] + prefix_den)).astype(BF16)
    spread_blocks(outs, out_weight_ref, attended_ref[...])


def spread_blocks(outs, weight_ref, right):
    x, z = tp_place()
    n = len(outs)
    rows = outs[0].shape[1]
    for k, out in enumerate(outs):
        to = lax.rem(x + k, n)
        for half, at in ((0, 2 * to + z), (1, 2 * to + 1 - z)):
            block = weight_ref[pl.ds(pl.multiple_of(at * rows, 32), rows), :]
            out[half] = jnp.dot(block, right, preferred_element_type=F32).astype(out.dtype)


def ffn_kernel(own_ref, r1_ref, r2_ref, r3_ref, gain_ref, gate_ref, up_ref, down_ref, *rest):
    outs, scratch = rest[:4], rest[4]
    place_blocks(scratch, [own_ref, r1_ref, r2_ref, r3_ref])
    scale = scaled_rows(scratch, gain_ref)
    gate = jnp.dot(gate_ref[...], scratch[...], preferred_element_type=F32) * scale
    up = jnp.dot(up_ref[...], scratch[...], preferred_element_type=F32) * scale
    spread_blocks(outs, down_ref, (silu(gate) * up).astype(BF16))


def shards(
    stream, token_req, request_leaf, parent, owner_map, node_state, node_norm, node_tail, mixer_gain, ffn_gain,
    query_weight, key_weight, value_weight, conv_gate_weight, conv_kernel, out_weight, ffn_gate, ffn_up, ffn_down,
):
    tokens, width = stream.shape
    heads, feats, head_dim = node_state.shape[1:]
    feat_dim = query_weight.shape[1] // heads
    model = value_weight.shape[0]
    req_size = lax.axis_size("req")
    tp_size = lax.axis_size("tp")
    x_size = tp_size // 2
    y_size, z_size = 4, req_size // 8
    per = request_leaf.shape[0] // req_size

    def along_x(array, k):
        return lax.ppermute(array, "tp", [(i, ((i // 2 + k) % x_size) * 2 + i % 2) for i in range(tp_size)])

    def across_z(array):
        return lax.ppermute(array, "tp", [(i, i ^ 1) for i in range(tp_size)])

    def along_z(array, k):
        count = 2 * z_size
        return lax.ppermute(
            array, "req", [(i, (i // count) * count + (((i % count) // 2 + k) % z_size) * 2 + i % 2) for i in range(req_size)]
        )

    def across_core(array):
        return lax.ppermute(array, "req", [(i, i ^ 1) for i in range(req_size)])

    def along_y(array, k):
        return lax.ppermute(array, "req", [(i, (i + 2 * z_size * k) % req_size) for i in range(req_size)])

    order = (1, 3, 2)

    fold = jnp.asarray(fold_matrix(feat_dim, feats), BF16)
    hbm = pl.BlockSpec(memory_space=pltpu.MemorySpace.HBM)
    state_in = jnp.transpose(node_state[0], (1, 0, 2))
    payload = call(
        fold_kernel,
        sds((heads, ROWS, LANES), BF16),
        [hbm] * 4,
        (fold, state_in, node_norm[0], node_tail[0]),
        scratch=[
            pltpu.VMEM(fold.shape, BF16),
            pltpu.VMEM(state_in.shape, BF16),
            pltpu.VMEM(node_norm[0].shape, BF16),
            pltpu.VMEM(node_tail[0].shape, BF16),
            pltpu.SemaphoreType.DMA((4,)),
        ],
        name="fold",
    )
    payload, own = lax.optimization_barrier((payload, stream.T))
    from_z = {k: along_z(payload, k) for k in order}

    pair = jnp.stack([own, across_z(own)])

    mine = jnp.stack([payload, from_z[1], from_z[2], from_z[3]])
    other = across_core(mine)
    def select(shifts, held, name):
        return call(
            functools.partial(select_kernel, y_size, shifts),
            [sds((per, heads, ROWS, LANES), BF16)] * len(shifts),
            [SMEM] * 3 + [VMEM] * 2,
            (request_leaf, parent, owner_map, *held),
            scratch=[pltpu.VMEM((2 * z_size + 1, heads, ROWS, LANES), BF16)],
            name=name,
        )

    sent = dict(zip(order, select(order, (mine, other), "select_sent")))
    mine, other, sent = lax.optimization_barrier((mine, other, sent))
    [kept] = select((0,), (mine, other), "select_kept")
    from_y = {k: along_y(sent[k], k) for k in order}

    rows = {k: along_x(pair, k) for k in order}
    gain_rows = model // LANES

    def gain_block(gain):
        return jnp.pad(gain.reshape(gain_rows, LANES), ((0, -gain_rows % 8), (0, 0)))

    local = call(
        functools.partial(local_kernel, request_leaf.shape[0]),
        [
            sds((width, tokens), F32),
            sds((width, tokens), F32),
            sds((heads, tokens, tokens), BF16),
            sds((heads, 1, tokens), F32),
            sds((heads, per * ROWS, 3 * tokens), BF16),
            sds((width, 8), F32),
        ],
        [VMEM] * 11,
        (
            pair, rows[1], rows[2], rows[3], gain_block(mixer_gain), token_req.reshape(1, tokens),
            query_weight.T, key_weight.T, value_weight.T, conv_gate_weight.T, conv_kernel,
        ),
        scratch=[pltpu.VMEM((model, tokens), BF16)],
        name="local",
    )
    parts = call(
        mix_kernel,
        [sds((2, width, tokens), F32)] + [sds((2, width, tokens), BF16)] * (x_size - 1),
        [VMEM] * 11,
        (*local, kept, from_y[1], from_y[2], from_y[3], turn(out_weight, "turn_out")),
        scratch=[pltpu.VMEM((width, tokens), BF16)],
        name="mix",
    )
    got = {k: along_x(parts[k], k) for k in order}
    share = parts[0] + got[1].astype(F32) + got[2].astype(F32) + got[3].astype(F32)
    crossing, down_in = lax.optimization_barrier((jnp.stack([share[1], share[0]]).astype(BF16), ffn_down))
    share_peer = across_z(crossing)
    updated = (pair.astype(F32) + share + share_peer.astype(F32)).astype(BF16)
    updated, down_turned = lax.optimization_barrier((updated, turn(down_in, "turn_down")))

    wide = {k: along_x(updated, k) for k in order}
    downs = call(
        ffn_kernel,
        [sds((2, width, tokens), F32)] + [sds((2, width, tokens), BF16)] * (x_size - 1),
        [VMEM] * 8,
        (updated, wide[1], wide[2], wide[3], gain_block(ffn_gain), ffn_gate.T, ffn_up.T, down_turned),
        scratch=[pltpu.VMEM((model, tokens), BF16)],
        name="ffn",
    )
    back = {k: along_x(downs[k], k) for k in order}
    down_share = downs[0] + back[1].astype(F32) + back[2].astype(F32) + back[3].astype(F32)
    down_peer = across_z(down_share[1].astype(BF16))
    result = updated[0].astype(F32) + down_share[0] + down_peer.astype(F32)
    return result.astype(BF16).T


def solution(mesh):
    in_specs = (
        P("req", "tp"), P("req"), P(), P(), P(), P("req", "tp", None, None), P("req", "tp", None), P("req", None, "tp"),
        P(), P(), P(None, "tp"), P(None, "tp"), P(None, "tp"), P(None, "tp"), P(None, "tp"), P("tp", None),
        P(None, "tp"), P(None, "tp"), P("tp", None),
    )
    return jax.shard_map(shards, mesh=mesh, in_specs=in_specs, out_specs=P("req", "tp"), check_vma=False)
```

```python
import functools

import jax
import jax.numpy as jnp
import numpy as np
from jax import lax
from jax.experimental import pallas as pl
from jax.experimental.pallas import tpu as pltpu
from jax.sharding import PartitionSpec as P

EPSILON = 1e-05
ROWS = 160
LANES = 128
TAIL_ROW = 153
F32 = jnp.float32
BF16 = jnp.bfloat16

VMEM = pl.BlockSpec(memory_space=pltpu.VMEM)
SMEM = pl.BlockSpec(memory_space=pltpu.SMEM)
PARAMS = pltpu.CompilerParams(vmem_limit_bytes=12 * 1024 * 1024)


def call(kernel, out_shape, specs, args, scratch=(), name=None):
    single = not isinstance(out_shape, (list, tuple))
    return pl.pallas_call(
        kernel,
        out_shape=out_shape,
        in_specs=specs,
        out_specs=VMEM if single else [VMEM] * len(out_shape),
        scratch_shapes=list(scratch),
        compiler_params=PARAMS,
        name=name,
    )(*args)


def sds(shape, dtype):
    return jax.ShapeDtypeStruct(shape, dtype)


def fold_matrix(feat_dim, feat_count):
    fold = np.zeros((ROWS, feat_count), np.float32)
    row = 0
    for i in range(feat_dim):
        fold[row, 1 + i] = 1
        row += 1
    for gap in range(feat_dim // 2 + 1):
        for i in range(feat_dim if gap < feat_dim // 2 else feat_dim // 2):
            j = (i + gap) % feat_dim
            fold[row, 1 + feat_dim + feat_dim * i + j] = 1
            fold[row, 1 + feat_dim + feat_dim * j + i] = 1
            row += 1
    fold[row, 0] = 1
    return fold


def split_norm(total, head_dim):
    rounded = total.astype(BF16).astype(F32)
    lost = pltpu.roll(total - rounded, 1, axis=1)
    lane = lax.broadcasted_iota(jnp.int32, total.shape, 1)
    return jnp.where(lane == head_dim + 1, total + lost, total).astype(BF16)


def fold_kernel(groups, held, *refs):
    (fold_hbm, state_hbm, norm_hbm, tail_hbm, leaf_hbm, parent_hbm, owner_hbm, out_ref, slot_ref) = refs[:9]
    fold_ref, state_ref, norm_ref, tail_ref, leaf_ref, parent_ref, owner_ref, sems = refs[9:]
    pairs = (
        (state_hbm, state_ref), (fold_hbm, fold_ref), (norm_hbm, norm_ref), (tail_hbm, tail_ref),
        (leaf_hbm, leaf_ref), (parent_hbm, parent_ref), (owner_hbm, owner_ref),
    )
    copies = [pltpu.make_async_copy(a, b, sems.at[i]) for i, (a, b) in enumerate(pairs)]
    for copy in copies:
        copy.start()
    for copy in copies:
        copy.wait()
    feats, heads, head_dim = state_ref.shape
    fold = fold_ref[...]
    norms = lax.dot_general(fold, norm_ref[...], (((1,), (1,)), ((), ())), preferred_element_type=F32)
    lane = lax.broadcasted_iota(jnp.int32, (ROWS, LANES), 1)
    for h in range(heads):
        state = jnp.dot(fold, state_ref[:, h, :], preferred_element_type=F32)
        norm = jnp.broadcast_to(norms[:, h : h + 1], (ROWS, LANES))
        hi = norm.astype(BF16).astype(F32)
        cols = jnp.where(lane == head_dim, hi, jnp.where(lane == head_dim + 1, norm - hi, 0.0))
        out_ref[h] = cols.astype(BF16)
        out_ref[h, :, :head_dim] = state.astype(BF16)
        out_ref[h, TAIL_ROW : TAIL_ROW + 2, :head_dim] = tail_ref[:, h * head_dim : (h + 1) * head_dim]

    dev = lax.axis_index("req")
    count = 2 * held
    total_dev = groups * count
    column = dev // count
    place = (dev % count) // 2
    core = dev % 2
    per = leaf_ref.shape[0] // total_dev

    def slot(row):
        k = lax.rem(place - (row % count) // 2 + held, held)
        k = k + jnp.where((row % 2) == core, 0, held)
        return jnp.where((row // count) == column, k, count)

    for k in range(groups):
        target = lax.rem(dev + k * count, total_dev)
        for s in range(per):
            leaf = leaf_ref[target * per + s]
            middle = parent_ref[leaf]
            root = parent_ref[middle]
            for i, node in enumerate((leaf, middle, root)):
                slot_ref[(k * per + s) * 3 + i] = slot(owner_ref[node])


def select_kernel(shifts, slot_ref, mine_ref, other_ref, *rest):
    outs, pool = rest[:-1], rest[-1]
    held, heads = mine_ref.shape[:2]
    per = outs[0].shape[0]
    for n in range(held):
        pool[n] = mine_ref[n]
        pool[held + n] = other_ref[n]
    pool[2 * held] = jnp.zeros(pool.shape[1:], BF16)
    rows = lax.broadcasted_iota(jnp.int32, (ROWS, LANES), 0)
    is_tail = (rows >= TAIL_ROW) & (rows < TAIL_ROW + 2)
    for out, k in zip(outs, shifts):
        for s in range(per):
            at = [slot_ref[(k * per + s) * 3 + i] for i in range(3)]
            for h in range(heads):
                first, second, third = [pool[a, h].astype(F32) for a in at]
                total = first + jnp.where(is_tail, 0.0, second + third)
                out[s, h] = split_norm(total, 112)


def tp_place():
    index = lax.axis_index("tp")
    return index >> 1, index & 1


def place_blocks(scratch, blocks):
    x, z = tp_place()
    n = len(blocks)
    rows = blocks[0].shape[1]
    for k, block in enumerate(blocks):
        source = lax.rem(x - k + n, n)
        scratch[pl.ds(pl.multiple_of((2 * source + z) * rows, 32), rows), :] = block[0]
        scratch[pl.ds(pl.multiple_of((2 * source + 1 - z) * rows, 32), rows), :] = block[1]


def scaled_rows(scratch, gain_ref):
    gain = gain_ref[...].T
    squares = jnp.zeros((LANES, scratch.shape[1]), F32)
    for j in range(scratch.shape[0] // LANES):
        rows = scratch[j * LANES : (j + 1) * LANES, :].astype(F32)
        squares = squares + rows * rows
        scratch[j * LANES : (j + 1) * LANES, :] = (rows * gain[:, j : j + 1]).astype(BF16)
    mean = jnp.sum(squares, axis=0, keepdims=True) / scratch.shape[0]
    return lax.rsqrt(mean + EPSILON)


def silu(v):
    return v / (1.0 + jnp.exp(-v))


def local_kernel(
    total_req, own_ref, r1_ref, r2_ref, r3_ref, gain_ref, token_ref, query_ref, key_ref, value_ref, gate_ref,
    taps_ref, conv_ref, silu_ref, scores_ref, den_ref, right_ref, turned_ref, scratch,
):
    place_blocks(scratch, [own_ref, r1_ref, r2_ref, r3_ref])
    scale = scaled_rows(scratch, gain_ref)
    rows = scratch[...]
    queries = jnp.dot(query_ref[...], rows, preferred_element_type=F32) * scale
    keys = jnp.dot(key_ref[...], rows, preferred_element_type=F32) * scale
    values = (jnp.dot(value_ref[...], rows, preferred_element_type=F32) * scale).astype(BF16).astype(F32)
    gates = jnp.dot(gate_ref[...], rows, preferred_element_type=F32) * scale
    heads = scores_ref.shape[0]
    per = right_ref.shape[1] // ROWS
    feat_dim = queries.shape[0] // heads
    tokens = token_ref.shape[1]
    ids = token_ref[...]
    slot = jnp.where(ids >= total_req, per, ids - lax.axis_index("req") * per)
    lane = lax.broadcasted_iota(jnp.int32, (1, tokens), 1)
    start = jnp.zeros((1, tokens), jnp.int32)
    for s in range(per):
        amount = jnp.sum((slot == s).astype(jnp.int32), axis=1, keepdims=True)
        start = start + jnp.where(slot > s, amount, 0)
    position = lane - start
    source = lax.broadcasted_iota(jnp.int32, (tokens, tokens), 0)
    target = lax.broadcasted_iota(jnp.int32, (tokens, tokens), 1)
    allowed = (source >= start) & (source <= target)
    turned = jnp.concatenate([taps_ref[...], jnp.zeros((5, taps_ref.shape[1]), F32)], axis=0).T
    turned_ref[...] = turned
    taps = turned
    conv_ref[...] = (
        taps[:, 0:1] * values
        + taps[:, 1:2] * jnp.where(position >= 1, pltpu.roll(values, 1, axis=1), 0.0)
        + taps[:, 2:3] * jnp.where(position >= 2, pltpu.roll(values, 2, axis=1), 0.0)
    )
    silu_ref[...] = silu(gates)
    payload_row = lax.broadcasted_iota(jnp.int32, (ROWS, tokens), 0)
    lag_one = (position == 0) & (payload_row == TAIL_ROW + 1)
    lag_two = ((position == 0) & (payload_row == TAIL_ROW)) | ((position == 1) & (payload_row == TAIL_ROW + 1))
    half = feat_dim // 2
    one = (lax.broadcasted_iota(jnp.int32, (half, tokens), 0) == 0).astype(F32)
    for h in range(heads):
        query = queries[h * feat_dim : (h + 1) * feat_dim]
        key = keys[h * feat_dim : (h + 1) * feat_dim]
        blocks = [query * feat_dim ** (-0.25)]
        for gap in range(half):
            other = query if gap == 0 else pltpu.roll(query, feat_dim - gap, axis=0)
            blocks.append(query * other * (2.0 * feat_dim) ** (-0.5))
        blocks.append(query[:half] * query[half:] * (2.0 * feat_dim) ** (-0.5))
        blocks.append(one)
        feature = jnp.concatenate(blocks, axis=0)
        for s in range(per):
            member = slot == s
            at = slice(s * ROWS, (s + 1) * ROWS)
            right_ref[h, at, :tokens] = jnp.where(member, feature, 0.0).astype(BF16)
            right_ref[h, at, tokens : 2 * tokens] = (member & lag_one).astype(F32).astype(BF16)
            right_ref[h, at, 2 * tokens :] = (member & lag_two).astype(F32).astype(BF16)
        dots = lax.dot_general(
            key, query, (((0,), (0,)), ((), ())), preferred_element_type=F32, precision=lax.Precision.HIGHEST
        )
        scores = jnp.where(allowed, 1.0 + dots * feat_dim ** (-0.5) + dots * dots * (1.0 / (2.0 * feat_dim)), 0.0)
        den_ref[h] = jnp.sum(scores, axis=0, keepdims=True)
        scores_ref[h] = scores.astype(BF16)


def turn_kernel(in_ref, out_ref):
    for j in range(out_ref.shape[0] // LANES):
        at = slice(j * LANES, (j + 1) * LANES)
        out_ref[at, :] = in_ref[:, at].T


def turn(weight, name):
    return call(turn_kernel, sds(weight.shape[::-1], weight.dtype), [VMEM], (weight,), name=name)


def mix_kernel(
    conv_ref, silu_ref, scores_ref, den_ref, right_ref, taps_ref, p0_ref, p1_ref, p2_ref, p3_ref,
    out_weight_ref, *rest,
):
    outs, attended_ref = rest[:4], rest[4]
    per, heads = p0_ref.shape[:2]
    head_dim = attended_ref.shape[0] // heads
    tokens = attended_ref.shape[1]
    for h in range(heads):
        states = []
        for s in range(per):
            total = (
                p0_ref[s, h].astype(F32) + p1_ref[s, h].astype(F32) + p2_ref[s, h].astype(F32) + p3_ref[s, h].astype(F32)
            )
            states.append(split_norm(total, head_dim))
        reached = lax.dot_general(
            jnp.concatenate(states, axis=0), right_ref[h], (((0,), (0,)), ((), ())), preferred_element_type=F32
        )
        prefix_num = reached[:head_dim, :tokens]
        prefix_den = reached[head_dim : head_dim + 1, :tokens] + reached[head_dim + 1 : head_dim + 2, :tokens]
        at = slice(h * head_dim, (h + 1) * head_dim)
        taps = taps_ref[at, :]
        conv = (
            conv_ref[at, :]
            + taps[:, 1:2] * reached[:head_dim, tokens : 2 * tokens]
            + taps[:, 2:3] * reached[:head_dim, 2 * tokens :]
        )
        mixed = (conv * silu_ref[at, :]).astype(BF16)
        local_num = jnp.dot(mixed, scores_ref[h], preferred_element_type=F32)
        attended_ref[at, :] = ((local_num + prefix_num) / (den_ref[h] + prefix_den)).astype(BF16)
    spread_blocks(outs, out_weight_ref, attended_ref[...])


def spread_blocks(outs, weight_ref, right):
    x, z = tp_place()
    n = len(outs)
    rows = outs[0].shape[1]
    for k, out in enumerate(outs):
        to = lax.rem(x + k, n)
        for half, at in ((0, 2 * to + z), (1, 2 * to + 1 - z)):
            block = weight_ref[pl.ds(pl.multiple_of(at * rows, 32), rows), :]
            out[half] = jnp.dot(block, right, preferred_element_type=F32).astype(out.dtype)


def ffn_kernel(own_ref, r1_ref, r2_ref, r3_ref, gain_ref, gate_ref, up_ref, down_ref, *rest):
    outs, scratch = rest[:4], rest[4]
    place_blocks(scratch, [own_ref, r1_ref, r2_ref, r3_ref])
    scale = scaled_rows(scratch, gain_ref)
    gate = jnp.dot(gate_ref[...], scratch[...], preferred_element_type=F32) * scale
    up = jnp.dot(up_ref[...], scratch[...], preferred_element_type=F32) * scale
    spread_blocks(outs, down_ref, (silu(gate) * up).astype(BF16))


def shards(
    stream, token_req, request_leaf, parent, owner_map, node_state, node_norm, node_tail, mixer_gain, ffn_gain,
    query_weight, key_weight, value_weight, conv_gate_weight, conv_kernel, out_weight, ffn_gate, ffn_up, ffn_down,
):
    tokens, width = stream.shape
    heads, feats, head_dim = node_state.shape[1:]
    feat_dim = query_weight.shape[1] // heads
    model = value_weight.shape[0]
    req_size = lax.axis_size("req")
    tp_size = lax.axis_size("tp")
    x_size = tp_size // 2
    y_size, z_size = 4, req_size // 8
    per = request_leaf.shape[0] // req_size

    def along_x(array, k):
        return lax.ppermute(array, "tp", [(i, ((i // 2 + k) % x_size) * 2 + i % 2) for i in range(tp_size)])

    def across_z(array):
        return lax.ppermute(array, "tp", [(i, i ^ 1) for i in range(tp_size)])

    def along_z(array, k):
        count = 2 * z_size
        return lax.ppermute(
            array, "req", [(i, (i // count) * count + (((i % count) // 2 + k) % z_size) * 2 + i % 2) for i in range(req_size)]
        )

    def across_core(array):
        return lax.ppermute(array, "req", [(i, i ^ 1) for i in range(req_size)])

    def along_y(array, k):
        return lax.ppermute(array, "req", [(i, (i + 2 * z_size * k) % req_size) for i in range(req_size)])

    order = (1, 3, 2)

    fold = jnp.asarray(fold_matrix(feat_dim, feats), BF16)
    def in_hbm(array):
        return pltpu.with_memory_space_constraint(array, pltpu.HBM)

    state_in = jnp.transpose(node_state[0], (1, 0, 2))
    fold_in = (fold, state_in, node_norm[0], node_tail[0], request_leaf, parent, owner_map)
    payload, slots = pl.pallas_call(
        functools.partial(fold_kernel, y_size, z_size),
        out_shape=[sds((heads, ROWS, LANES), BF16), sds((y_size * per * 3,), jnp.int32)],
        in_specs=[pl.BlockSpec(memory_space=pltpu.HBM)] * len(fold_in),
        out_specs=[VMEM, SMEM],
        scratch_shapes=[pltpu.VMEM(a.shape, BF16) for a in fold_in[:4]]
        + [pltpu.SMEM(a.shape, jnp.int32) for a in fold_in[4:]]
        + [pltpu.SemaphoreType.DMA((len(fold_in),))],
        compiler_params=PARAMS,
        name="fold",
    )(*[in_hbm(a) for a in fold_in])
    from_z = {k: along_z(payload, k) for k in order}

    own = stream.T
    pair = jnp.stack([own, across_z(own)])

    held_pair, *arrived = lax.optimization_barrier((pair, from_z[1], from_z[2], from_z[3]))
    mine = jnp.stack([payload, *arrived])
    other = across_core(mine)
    def select(shifts, held, name):
        return call(
            functools.partial(select_kernel, shifts),
            [sds((per, heads, ROWS, LANES), BF16)] * len(shifts),
            [SMEM] + [VMEM] * 2,
            (slots, *held),
            scratch=[pltpu.VMEM((2 * z_size + 1, heads, ROWS, LANES), BF16)],
            name=name,
        )

    sent = dict(zip(order, select(order, (mine, other), "select_sent")))
    mine, other, sent = lax.optimization_barrier((mine, other, sent))
    [kept] = select((0,), (mine, other), "select_kept")
    from_y = {k: along_y(sent[k], k) for k in order}

    rows = {k: along_x(pair, k) for k in order}
    gain_rows = model // LANES

    def gain_block(gain):
        return jnp.pad(gain.reshape(gain_rows, LANES), ((0, -gain_rows % 8), (0, 0)))

    local = call(
        functools.partial(local_kernel, request_leaf.shape[0]),
        [
            sds((width, tokens), F32),
            sds((width, tokens), F32),
            sds((heads, tokens, tokens), BF16),
            sds((heads, 1, tokens), F32),
            sds((heads, per * ROWS, 3 * tokens), BF16),
            sds((width, 8), F32),
        ],
        [VMEM] * 11,
        (
            pair, rows[1], rows[2], rows[3], gain_block(mixer_gain), token_req.reshape(1, tokens),
            query_weight.T, key_weight.T, value_weight.T, conv_gate_weight.T, conv_kernel,
        ),
        scratch=[pltpu.VMEM((model, tokens), BF16)],
        name="local",
    )
    parts = call(
        mix_kernel,
        [sds((2, width, tokens), F32)] + [sds((2, width, tokens), BF16)] * (x_size - 1),
        [VMEM] * 11,
        (*local, kept, from_y[1], from_y[2], from_y[3], turn(out_weight, "turn_out")),
        scratch=[pltpu.VMEM((width, tokens), BF16)],
        name="mix",
    )
    got = {k: along_x(parts[k], k) for k in order}
    share = parts[0] + got[1].astype(F32) + got[2].astype(F32) + got[3].astype(F32)
    crossing, down_in = lax.optimization_barrier((jnp.stack([share[1], share[0]]).astype(BF16), ffn_down))
    share_peer = across_z(crossing)
    updated = (held_pair.astype(F32) + share + share_peer.astype(F32)).astype(BF16)
    updated, down_turned = lax.optimization_barrier((updated, turn(down_in, "turn_down")))

    wide = {k: along_x(updated, k) for k in order}
    downs = call(
        ffn_kernel,
        [sds((2, width, tokens), F32)] + [sds((2, width, tokens), BF16)] * (x_size - 1),
        [VMEM] * 8,
        (updated, wide[1], wide[2], wide[3], gain_block(ffn_gain), ffn_gate.T, ffn_up.T, down_turned),
        scratch=[pltpu.VMEM((model, tokens), BF16)],
        name="ffn",
    )
    back = {k: along_x(downs[k], k) for k in order}
    down_share = downs[0] + back[1].astype(F32) + back[2].astype(F32) + back[3].astype(F32)
    down_peer = across_z(down_share[1].astype(BF16))
    result = updated[0].astype(F32) + down_share[0] + down_peer.astype(F32)
    return result.astype(BF16).T


def solution(mesh):
    in_specs = (
        P("req", "tp"), P("req"), P(), P(), P(), P("req", "tp", None, None), P("req", "tp", None), P("req", None, "tp"),
        P(), P(), P(None, "tp"), P(None, "tp"), P(None, "tp"), P(None, "tp"), P(None, "tp"), P("tp", None),
        P(None, "tp"), P(None, "tp"), P("tp", None),
    )
    return jax.shard_map(shards, mesh=mesh, in_specs=in_specs, out_specs=P("req", "tp"), check_vma=False)
```

```python
import functools

import jax
import jax.numpy as jnp
import numpy as np
from jax import lax
from jax.experimental import pallas as pl
from jax.experimental.pallas import tpu as pltpu
from jax.sharding import PartitionSpec as P

EPSILON = 1e-05
ROWS = 160
LANES = 128
TAIL_ROW = 153
F32 = jnp.float32
BF16 = jnp.bfloat16

VMEM = pl.BlockSpec(memory_space=pltpu.VMEM)
SMEM = pl.BlockSpec(memory_space=pltpu.SMEM)
PARAMS = pltpu.CompilerParams(vmem_limit_bytes=12 * 1024 * 1024)


def call(kernel, out_shape, specs, args, scratch=(), name=None):
    single = not isinstance(out_shape, (list, tuple))
    return pl.pallas_call(
        kernel,
        out_shape=out_shape,
        in_specs=specs,
        out_specs=VMEM if single else [VMEM] * len(out_shape),
        scratch_shapes=list(scratch),
        compiler_params=PARAMS,
        name=name,
    )(*args)


def sds(shape, dtype):
    return jax.ShapeDtypeStruct(shape, dtype)


def fold_matrix(feat_dim, feat_count):
    fold = np.zeros((ROWS, feat_count), np.float32)
    row = 0
    for i in range(feat_dim):
        fold[row, 1 + i] = 1
        row += 1
    for gap in range(feat_dim // 2 + 1):
        for i in range(feat_dim if gap < feat_dim // 2 else feat_dim // 2):
            j = (i + gap) % feat_dim
            fold[row, 1 + feat_dim + feat_dim * i + j] = 1
            fold[row, 1 + feat_dim + feat_dim * j + i] = 1
            row += 1
    fold[row, 0] = 1
    return fold


def split_norm(total, head_dim):
    rounded = total.astype(BF16).astype(F32)
    lost = pltpu.roll(total - rounded, 1, axis=1)
    lane = lax.broadcasted_iota(jnp.int32, total.shape, 1)
    return jnp.where(lane == head_dim + 1, total + lost, total).astype(BF16)


def fold_kernel(groups, held, *refs):
    (fold_hbm, state_hbm, norm_hbm, tail_hbm, leaf_hbm, parent_hbm, owner_hbm, own_hbm) = refs[:8]
    out_ref, slot_ref, own_ref = refs[8:11]
    fold_ref, state_ref, norm_ref, tail_ref, leaf_ref, parent_ref, owner_ref, sems = refs[11:]
    pairs = (
        (state_hbm, state_ref), (fold_hbm, fold_ref), (norm_hbm, norm_ref), (tail_hbm, tail_ref),
        (leaf_hbm, leaf_ref), (parent_hbm, parent_ref), (owner_hbm, owner_ref), (own_hbm, own_ref),
    )
    copies = [pltpu.make_async_copy(a, b, sems.at[i]) for i, (a, b) in enumerate(pairs)]
    for copy in copies:
        copy.start()
    for copy in copies:
        copy.wait()
    feats, heads, head_dim = state_ref.shape
    fold = fold_ref[...]
    norms = lax.dot_general(fold, norm_ref[...], (((1,), (1,)), ((), ())), preferred_element_type=F32)
    lane = lax.broadcasted_iota(jnp.int32, (ROWS, LANES), 1)
    for h in range(heads):
        state = jnp.dot(fold, state_ref[:, h, :], preferred_element_type=F32)
        norm = jnp.broadcast_to(norms[:, h : h + 1], (ROWS, LANES))
        hi = norm.astype(BF16).astype(F32)
        cols = jnp.where(lane == head_dim, hi, jnp.where(lane == head_dim + 1, norm - hi, 0.0))
        out_ref[h] = cols.astype(BF16)
        out_ref[h, :, :head_dim] = state.astype(BF16)
        out_ref[h, TAIL_ROW : TAIL_ROW + 2, :head_dim] = tail_ref[:, h * head_dim : (h + 1) * head_dim]

    dev = lax.axis_index("req")
    count = 2 * held
    total_dev = groups * count
    column = dev // count
    place = (dev % count) // 2
    core = dev % 2
    per = leaf_ref.shape[0] // total_dev

    def slot(row):
        k = (place ^ ((row % count) // 2)) + jnp.where((row % 2) == core, 0, held)
        return jnp.where((row // count) == column, k, count)

    for k in range(groups):
        target = dev ^ (k * count)
        for s in range(per):
            leaf = leaf_ref[target * per + s]
            middle = parent_ref[leaf]
            root = parent_ref[middle]
            for i, node in enumerate((leaf, middle, root)):
                slot_ref[(k * per + s) * 3 + i] = slot(owner_ref[node])


def select_kernel(shifts, slot_ref, mine_ref, other_ref, *rest):
    outs, pool = rest[:-1], rest[-1]
    held, heads = mine_ref.shape[:2]
    per = outs[0].shape[0]
    for n in range(held):
        pool[n] = mine_ref[n]
        pool[held + n] = other_ref[n]
    pool[2 * held] = jnp.zeros(pool.shape[1:], BF16)
    rows = lax.broadcasted_iota(jnp.int32, (ROWS, LANES), 0)
    is_tail = (rows >= TAIL_ROW) & (rows < TAIL_ROW + 2)
    for out, k in zip(outs, shifts):
        for s in range(per):
            at = [slot_ref[(k * per + s) * 3 + i] for i in range(3)]
            for h in range(heads):
                first, second, third = [pool[a, h].astype(F32) for a in at]
                total = first + jnp.where(is_tail, 0.0, second + third)
                out[s, h] = split_norm(total, 112)


def tp_place():
    index = lax.axis_index("tp")
    return index >> 1, index & 1


def place_blocks(scratch, blocks):
    x, z = tp_place()
    rows = blocks[0].shape[1]
    for k, block in enumerate(blocks):
        source = x ^ k
        scratch[pl.ds(pl.multiple_of((2 * source + z) * rows, 32), rows), :] = block[0]
        scratch[pl.ds(pl.multiple_of((2 * source + 1 - z) * rows, 32), rows), :] = block[1]


def scaled_rows(scratch, gain_ref):
    gain = gain_ref[...].T
    squares = jnp.zeros((LANES, scratch.shape[1]), F32)
    for j in range(scratch.shape[0] // LANES):
        rows = scratch[j * LANES : (j + 1) * LANES, :].astype(F32)
        squares = squares + rows * rows
        scratch[j * LANES : (j + 1) * LANES, :] = (rows * gain[:, j : j + 1]).astype(BF16)
    mean = jnp.sum(squares, axis=0, keepdims=True) / scratch.shape[0]
    return lax.rsqrt(mean + EPSILON)


def silu(v):
    return v / (1.0 + jnp.exp(-v))


def local_kernel(
    total_req, own_ref, r1_ref, r2_ref, r3_ref, gain_ref, token_ref, query_ref, key_ref, value_ref, gate_ref,
    taps_ref, conv_ref, silu_ref, scores_ref, den_ref, right_ref, turned_ref, scratch,
):
    place_blocks(scratch, [own_ref, r1_ref, r2_ref, r3_ref])
    scale = scaled_rows(scratch, gain_ref)
    rows = scratch[...]
    queries = jnp.dot(query_ref[...], rows, preferred_element_type=F32) * scale
    keys = jnp.dot(key_ref[...], rows, preferred_element_type=F32) * scale
    values = (jnp.dot(value_ref[...], rows, preferred_element_type=F32) * scale).astype(BF16).astype(F32)
    gates = jnp.dot(gate_ref[...], rows, preferred_element_type=F32) * scale
    heads = scores_ref.shape[0]
    per = right_ref.shape[1] // ROWS
    feat_dim = queries.shape[0] // heads
    tokens = token_ref.shape[1]
    ids = token_ref[...]
    slot = jnp.where(ids >= total_req, per, ids - lax.axis_index("req") * per)
    lane = lax.broadcasted_iota(jnp.int32, (1, tokens), 1)
    start = jnp.zeros((1, tokens), jnp.int32)
    for s in range(per):
        amount = jnp.sum((slot == s).astype(jnp.int32), axis=1, keepdims=True)
        start = start + jnp.where(slot > s, amount, 0)
    position = lane - start
    source = lax.broadcasted_iota(jnp.int32, (tokens, tokens), 0)
    target = lax.broadcasted_iota(jnp.int32, (tokens, tokens), 1)
    allowed = (source >= start) & (source <= target)
    turned = jnp.concatenate([taps_ref[...], jnp.zeros((5, taps_ref.shape[1]), F32)], axis=0).T
    turned_ref[...] = turned
    taps = turned
    conv_ref[...] = (
        taps[:, 0:1] * values
        + taps[:, 1:2] * jnp.where(position >= 1, pltpu.roll(values, 1, axis=1), 0.0)
        + taps[:, 2:3] * jnp.where(position >= 2, pltpu.roll(values, 2, axis=1), 0.0)
    )
    silu_ref[...] = silu(gates)
    payload_row = lax.broadcasted_iota(jnp.int32, (ROWS, tokens), 0)
    lag_one = (position == 0) & (payload_row == TAIL_ROW + 1)
    lag_two = ((position == 0) & (payload_row == TAIL_ROW)) | ((position == 1) & (payload_row == TAIL_ROW + 1))
    half = feat_dim // 2
    one = (lax.broadcasted_iota(jnp.int32, (half, tokens), 0) == 0).astype(F32)
    for h in range(heads):
        query = queries[h * feat_dim : (h + 1) * feat_dim]
        key = keys[h * feat_dim : (h + 1) * feat_dim]
        blocks = [query * feat_dim ** (-0.25)]
        for gap in range(half):
            other = query if gap == 0 else pltpu.roll(query, feat_dim - gap, axis=0)
            blocks.append(query * other * (2.0 * feat_dim) ** (-0.5))
        blocks.append(query[:half] * query[half:] * (2.0 * feat_dim) ** (-0.5))
        blocks.append(one)
        feature = jnp.concatenate(blocks, axis=0)
        for s in range(per):
            member = slot == s
            at = slice(s * ROWS, (s + 1) * ROWS)
            right_ref[h, at, :tokens] = jnp.where(member, feature, 0.0).astype(BF16)
            right_ref[h, at, tokens : 2 * tokens] = (member & lag_one).astype(F32).astype(BF16)
            right_ref[h, at, 2 * tokens :] = (member & lag_two).astype(F32).astype(BF16)
        dots = lax.dot_general(
            key, query, (((0,), (0,)), ((), ())), preferred_element_type=F32, precision=lax.Precision.HIGHEST
        )
        scores = jnp.where(allowed, 1.0 + dots * feat_dim ** (-0.5) + dots * dots * (1.0 / (2.0 * feat_dim)), 0.0)
        den_ref[h] = jnp.sum(scores, axis=0, keepdims=True)
        scores_ref[h] = scores.astype(BF16)


def stack_kernel(first_ref, second_ref, out_ref):
    out_ref[0] = first_ref[...]
    out_ref[1] = second_ref[...]


def turn_kernel(in_ref, out_ref):
    for j in range(out_ref.shape[0] // LANES):
        at = slice(j * LANES, (j + 1) * LANES)
        out_ref[at, :] = in_ref[:, at].T


def turn(weight, name):
    return call(turn_kernel, sds(weight.shape[::-1], weight.dtype), [VMEM], (weight,), name=name)


def mix_kernel(
    conv_ref, silu_ref, scores_ref, den_ref, right_ref, taps_ref, p0_ref, p1_ref, p2_ref, p3_ref,
    out_weight_ref, *rest,
):
    outs, attended_ref = rest[:4], rest[4]
    per, heads = p0_ref.shape[:2]
    head_dim = attended_ref.shape[0] // heads
    tokens = attended_ref.shape[1]
    for h in range(heads):
        states = []
        for s in range(per):
            total = (
                p0_ref[s, h].astype(F32) + p1_ref[s, h].astype(F32) + p2_ref[s, h].astype(F32) + p3_ref[s, h].astype(F32)
            )
            states.append(split_norm(total, head_dim))
        reached = lax.dot_general(
            jnp.concatenate(states, axis=0), right_ref[h], (((0,), (0,)), ((), ())), preferred_element_type=F32
        )
        prefix_num = reached[:head_dim, :tokens]
        prefix_den = reached[head_dim : head_dim + 1, :tokens] + reached[head_dim + 1 : head_dim + 2, :tokens]
        at = slice(h * head_dim, (h + 1) * head_dim)
        taps = taps_ref[at, :]
        conv = (
            conv_ref[at, :]
            + taps[:, 1:2] * reached[:head_dim, tokens : 2 * tokens]
            + taps[:, 2:3] * reached[:head_dim, 2 * tokens :]
        )
        mixed = (conv * silu_ref[at, :]).astype(BF16)
        local_num = jnp.dot(mixed, scores_ref[h], preferred_element_type=F32)
        attended_ref[at, :] = ((local_num + prefix_num) / (den_ref[h] + prefix_den)).astype(BF16)
    spread_blocks(outs, out_weight_ref, attended_ref[...])


def spread_blocks(outs, weight_ref, right):
    x, z = tp_place()
    rows = outs[0].shape[1]
    for k, out in enumerate(outs):
        to = x ^ k
        for half, at in ((0, 2 * to + z), (1, 2 * to + 1 - z)):
            block = weight_ref[pl.ds(pl.multiple_of(at * rows, 32), rows), :]
            out[half] = jnp.dot(block, right, preferred_element_type=F32).astype(out.dtype)


def ffn_kernel(own_ref, r1_ref, r2_ref, r3_ref, gain_ref, gate_ref, up_ref, down_ref, *rest):
    outs, scratch = rest[:4], rest[4]
    place_blocks(scratch, [own_ref, r1_ref, r2_ref, r3_ref])
    scale = scaled_rows(scratch, gain_ref)
    gate = jnp.dot(gate_ref[...], scratch[...], preferred_element_type=F32) * scale
    up = jnp.dot(up_ref[...], scratch[...], preferred_element_type=F32) * scale
    spread_blocks(outs, down_ref, (silu(gate) * up).astype(BF16))


def shards(
    stream, token_req, request_leaf, parent, owner_map, node_state, node_norm, node_tail, mixer_gain, ffn_gain,
    query_weight, key_weight, value_weight, conv_gate_weight, conv_kernel, out_weight, ffn_gate, ffn_up, ffn_down,
):
    tokens, width = stream.shape
    heads, feats, head_dim = node_state.shape[1:]
    feat_dim = query_weight.shape[1] // heads
    model = value_weight.shape[0]
    req_size = lax.axis_size("req")
    tp_size = lax.axis_size("tp")
    y_size, z_size = 4, req_size // 8
    per = request_leaf.shape[0] // req_size

    def along_x(array, k):
        return lax.ppermute(array, "tp", [(i, i ^ (2 * k)) for i in range(tp_size)])

    def across_z(array):
        return lax.ppermute(array, "tp", [(i, i ^ 1) for i in range(tp_size)])

    def along_z(array, k):
        return lax.ppermute(array, "req", [(i, i ^ (2 * k)) for i in range(req_size)])

    def across_core(array):
        return lax.ppermute(array, "req", [(i, i ^ 1) for i in range(req_size)])

    def along_y(array, k):
        return lax.ppermute(array, "req", [(i, i ^ (2 * z_size * k)) for i in range(req_size)])

    order = (1, 3, 2)

    fold = jnp.asarray(fold_matrix(feat_dim, feats), BF16)
    def in_hbm(array):
        return pltpu.with_memory_space_constraint(array, pltpu.HBM)

    state_in = jnp.transpose(node_state[0], (1, 0, 2))
    own = stream.T
    fold_in = (fold, state_in, node_norm[0], node_tail[0], request_leaf, parent, owner_map, own)
    payload, slots, own_near = pl.pallas_call(
        functools.partial(fold_kernel, y_size, z_size),
        out_shape=[sds((heads, ROWS, LANES), BF16), sds((y_size * per * 3,), jnp.int32), sds(own.shape, BF16)],
        in_specs=[pl.BlockSpec(memory_space=pltpu.HBM)] * len(fold_in),
        out_specs=[VMEM, SMEM, VMEM],
        scratch_shapes=[pltpu.VMEM(a.shape, BF16) for a in fold_in[:4]]
        + [pltpu.SMEM(a.shape, jnp.int32) for a in fold_in[4:7]]
        + [pltpu.SemaphoreType.DMA((len(fold_in),))],
        compiler_params=PARAMS,
        name="fold",
    )(*[in_hbm(a) for a in fold_in])
    from_z = {k: along_z(payload, k) for k in order}

    pair = call(stack_kernel, sds((2, width, tokens), BF16), [VMEM] * 2, (own_near, across_z(own)), name="stack_pair")
    rows = {k: along_x(pair, k) for k in order}

    held_pair, *arrived = lax.optimization_barrier((pair, from_z[1], from_z[2], from_z[3]))
    mine = jnp.stack([payload, *arrived])
    other = across_core(mine)
    def select(shifts, held, name):
        return call(
            functools.partial(select_kernel, shifts),
            [sds((per, heads, ROWS, LANES), BF16)] * len(shifts),
            [SMEM] + [VMEM] * 2,
            (slots, *held),
            scratch=[pltpu.VMEM((2 * z_size + 1, heads, ROWS, LANES), BF16)],
            name=name,
        )

    sent = dict(zip(order, select(order, (mine, other), "select_sent")))
    mine, other, sent = lax.optimization_barrier((mine, other, sent))
    [kept] = select((0,), (mine, other), "select_kept")
    from_y = {k: along_y(sent[k], k) for k in order}

    gain_rows = model // LANES

    def gain_block(gain):
        return jnp.pad(gain.reshape(gain_rows, LANES), ((0, -gain_rows % 8), (0, 0)))

    local = call(
        functools.partial(local_kernel, request_leaf.shape[0]),
        [
            sds((width, tokens), F32),
            sds((width, tokens), F32),
            sds((heads, tokens, tokens), BF16),
            sds((heads, 1, tokens), F32),
            sds((heads, per * ROWS, 3 * tokens), BF16),
            sds((width, 8), F32),
        ],
        [VMEM] * 11,
        (
            pair, rows[1], rows[2], rows[3], gain_block(mixer_gain), token_req.reshape(1, tokens),
            query_weight.T, key_weight.T, value_weight.T, conv_gate_weight.T, conv_kernel,
        ),
        scratch=[pltpu.VMEM((model, tokens), BF16)],
        name="local",
    )
    parts = call(
        mix_kernel,
        [sds((2, width, tokens), F32)] + [sds((2, width, tokens), BF16)] * 3,
        [VMEM] * 11,
        (*local, kept, from_y[1], from_y[2], from_y[3], turn(out_weight, "turn_out")),
        scratch=[pltpu.VMEM((width, tokens), BF16)],
        name="mix",
    )
    got = {k: along_x(parts[k], k) for k in order}
    share = parts[0] + got[1].astype(F32) + got[2].astype(F32) + got[3].astype(F32)
    crossing, down_in = lax.optimization_barrier((jnp.stack([share[1], share[0]]).astype(BF16), ffn_down))
    share_peer = across_z(crossing)
    updated = (held_pair.astype(F32) + share + share_peer.astype(F32)).astype(BF16)
    updated, down_turned = lax.optimization_barrier((updated, turn(down_in, "turn_down")))

    wide = {k: along_x(updated, k) for k in order}
    downs = call(
        ffn_kernel,
        [sds((2, width, tokens), F32)] + [sds((2, width, tokens), BF16)] * 3,
        [VMEM] * 8,
        (updated, wide[1], wide[2], wide[3], gain_block(ffn_gain), ffn_gate.T, ffn_up.T, down_turned),
        scratch=[pltpu.VMEM((model, tokens), BF16)],
        name="ffn",
    )
    back = {k: along_x(downs[k], k) for k in order}
    down_share = downs[0] + back[1].astype(F32) + back[2].astype(F32) + back[3].astype(F32)
    down_peer = across_z(down_share[1].astype(BF16))
    result = updated[0].astype(F32) + down_share[0] + down_peer.astype(F32)
    return result.astype(BF16).T


def solution(mesh):
    in_specs = (
        P("req", "tp"), P("req"), P(), P(), P(), P("req", "tp", None, None), P("req", "tp", None), P("req", None, "tp"),
        P(), P(), P(None, "tp"), P(None, "tp"), P(None, "tp"), P(None, "tp"), P(None, "tp"), P("tp", None),
        P(None, "tp"), P(None, "tp"), P("tp", None),
    )
    return jax.shard_map(shards, mesh=mesh, in_specs=in_specs, out_specs=P("req", "tp"), check_vma=False)
```

```python
import functools

import jax
import jax.numpy as jnp
import numpy as np
from jax import lax
from jax.experimental import pallas as pl
from jax.experimental.pallas import tpu as pltpu
from jax.sharding import PartitionSpec as P

EPSILON = 1e-05
ROWS = 160
LANES = 128
TAIL_ROW = 153
F32 = jnp.float32
BF16 = jnp.bfloat16

VMEM = pl.BlockSpec(memory_space=pltpu.VMEM)
SMEM = pl.BlockSpec(memory_space=pltpu.SMEM)
PARAMS = pltpu.CompilerParams(vmem_limit_bytes=12 * 1024 * 1024)


def call(kernel, out_shape, specs, args, scratch=(), name=None):
    single = not isinstance(out_shape, (list, tuple))
    return pl.pallas_call(
        kernel,
        out_shape=out_shape,
        in_specs=specs,
        out_specs=VMEM if single else [VMEM] * len(out_shape),
        scratch_shapes=list(scratch),
        compiler_params=PARAMS,
        name=name,
    )(*args)


def sds(shape, dtype):
    return jax.ShapeDtypeStruct(shape, dtype)


def fold_matrix(feat_dim, feat_count):
    fold = np.zeros((ROWS, feat_count), np.float32)
    row = 0
    for i in range(feat_dim):
        fold[row, 1 + i] = 1
        row += 1
    for gap in range(feat_dim // 2 + 1):
        for i in range(feat_dim if gap < feat_dim // 2 else feat_dim // 2):
            j = (i + gap) % feat_dim
            fold[row, 1 + feat_dim + feat_dim * i + j] = 1
            fold[row, 1 + feat_dim + feat_dim * j + i] = 1
            row += 1
    fold[row, 0] = 1
    return fold


def split_norm(total, head_dim):
    rounded = total.astype(BF16).astype(F32)
    lost = pltpu.roll(total - rounded, 1, axis=1)
    lane = lax.broadcasted_iota(jnp.int32, total.shape, 1)
    return jnp.where(lane == head_dim + 1, total + lost, total).astype(BF16)


def fetch(pairs, sems):
    copies = [pltpu.make_async_copy(a, b, sems.at[i]) for i, (a, b) in enumerate(pairs)]
    for copy in copies:
        copy.start()
    return copies


def fold_kernel(
    fold_hbm, state_hbm, norm_hbm, tail_hbm, own_hbm, out_ref, own_ref, fold_ref, state_ref, norm_ref, tail_ref, sems
):
    copies = fetch(
        (
            (state_hbm, state_ref), (fold_hbm, fold_ref), (norm_hbm, norm_ref), (tail_hbm, tail_ref),
            (own_hbm, own_ref),
        ),
        sems,
    )
    for copy in copies[:4]:
        copy.wait()
    feats, heads, head_dim = state_ref.shape
    fold = fold_ref[...]
    norms = lax.dot_general(fold, norm_ref[...], (((1,), (1,)), ((), ())), preferred_element_type=F32)
    lane = lax.broadcasted_iota(jnp.int32, (ROWS, LANES), 1)
    for h in range(heads):
        state = jnp.dot(fold, state_ref[:, h, :], preferred_element_type=F32)
        norm = jnp.broadcast_to(norms[:, h : h + 1], (ROWS, LANES))
        hi = norm.astype(BF16).astype(F32)
        cols = jnp.where(lane == head_dim, hi, jnp.where(lane == head_dim + 1, norm - hi, 0.0))
        out_ref[h] = cols.astype(BF16)
        out_ref[h, :, :head_dim] = state.astype(BF16)
        out_ref[h, TAIL_ROW : TAIL_ROW + 2, :head_dim] = tail_ref[:, h * head_dim : (h + 1) * head_dim]
    copies[4].wait()


def turn_block(in_ref, out_ref):
    for j in range(out_ref.shape[0] // LANES):
        at = slice(j * LANES, (j + 1) * LANES)
        out_ref[at, :] = in_ref[:, at].T


def turn_kernel(in_ref, out_ref):
    turn_block(in_ref, out_ref)


def turn_and_slots_kernel(
    groups, held, in_hbm, leaf_hbm, parent_hbm, owner_hbm, out_ref, slot_ref, in_ref, leaf_ref, parent_ref, owner_ref, sems
):
    copies = fetch(
        ((in_hbm, in_ref), (leaf_hbm, leaf_ref), (parent_hbm, parent_ref), (owner_hbm, owner_ref)), sems
    )
    for copy in copies:
        copy.wait()
    dev = lax.axis_index("req")
    count = 2 * held
    total_dev = groups * count
    column = dev // count
    place = (dev % count) // 2
    core = dev % 2
    per = leaf_ref.shape[0] // total_dev

    def slot(row):
        k = (place ^ ((row % count) // 2)) + jnp.where((row % 2) == core, 0, held)
        return jnp.where((row // count) == column, k, count)

    for k in range(groups):
        target = dev ^ (k * count)
        for s in range(per):
            leaf = leaf_ref[target * per + s]
            middle = parent_ref[leaf]
            root = parent_ref[middle]
            for i, node in enumerate((leaf, middle, root)):
                slot_ref[(k * per + s) * 3 + i] = slot(owner_ref[node])
    turn_block(in_ref, out_ref)


def select_kernel(shifts, slot_ref, mine_ref, other_ref, *rest):
    outs, pool = rest[:-1], rest[-1]
    held, heads = mine_ref.shape[:2]
    per = outs[0].shape[0]
    for n in range(held):
        pool[n] = mine_ref[n]
        pool[held + n] = other_ref[n]
    pool[2 * held] = jnp.zeros(pool.shape[1:], BF16)
    rows = lax.broadcasted_iota(jnp.int32, (ROWS, LANES), 0)
    is_tail = (rows >= TAIL_ROW) & (rows < TAIL_ROW + 2)
    for out, k in zip(outs, shifts):
        for s in range(per):
            at = [slot_ref[(k * per + s) * 3 + i] for i in range(3)]
            for h in range(heads):
                first, second, third = [pool[a, h].astype(F32) for a in at]
                total = first + jnp.where(is_tail, 0.0, second + third)
                out[s, h] = split_norm(total, 112)


def tp_place():
    index = lax.axis_index("tp")
    return index >> 1, index & 1


def place_blocks(scratch, blocks):
    x, z = tp_place()
    rows = blocks[0].shape[1]
    for k, block in enumerate(blocks):
        source = x ^ k
        scratch[pl.ds(pl.multiple_of((2 * source + z) * rows, 32), rows), :] = block[0]
        scratch[pl.ds(pl.multiple_of((2 * source + 1 - z) * rows, 32), rows), :] = block[1]


def scaled_rows(scratch, gain_ref):
    gain = gain_ref[...].T
    squares = jnp.zeros((LANES, scratch.shape[1]), F32)
    for j in range(scratch.shape[0] // LANES):
        rows = scratch[j * LANES : (j + 1) * LANES, :].astype(F32)
        squares = squares + rows * rows
        scratch[j * LANES : (j + 1) * LANES, :] = (rows * gain[:, j : j + 1]).astype(BF16)
    mean = jnp.sum(squares, axis=0, keepdims=True) / scratch.shape[0]
    return lax.rsqrt(mean + EPSILON)


def silu(v):
    return v / (1.0 + jnp.exp(-v))


def local_kernel(
    total_req, own_ref, r1_ref, r2_ref, r3_ref, gain_ref, token_ref, query_ref, key_ref, value_ref, gate_ref,
    taps_ref, conv_ref, silu_ref, scores_ref, den_ref, right_ref, turned_ref, scratch,
):
    place_blocks(scratch, [own_ref, r1_ref, r2_ref, r3_ref])
    scale = scaled_rows(scratch, gain_ref)
    rows = scratch[...]
    queries = jnp.dot(query_ref[...], rows, preferred_element_type=F32) * scale
    keys = jnp.dot(key_ref[...], rows, preferred_element_type=F32) * scale
    values = (jnp.dot(value_ref[...], rows, preferred_element_type=F32) * scale).astype(BF16).astype(F32)
    gates = jnp.dot(gate_ref[...], rows, preferred_element_type=F32) * scale
    heads = scores_ref.shape[0]
    per = right_ref.shape[1] // ROWS
    feat_dim = queries.shape[0] // heads
    tokens = token_ref.shape[1]
    ids = token_ref[...]
    slot = jnp.where(ids >= total_req, per, ids - lax.axis_index("req") * per)
    lane = lax.broadcasted_iota(jnp.int32, (1, tokens), 1)
    start = jnp.zeros((1, tokens), jnp.int32)
    for s in range(per):
        amount = jnp.sum((slot == s).astype(jnp.int32), axis=1, keepdims=True)
        start = start + jnp.where(slot > s, amount, 0)
    position = lane - start
    source = lax.broadcasted_iota(jnp.int32, (tokens, tokens), 0)
    target = lax.broadcasted_iota(jnp.int32, (tokens, tokens), 1)
    allowed = (source >= start) & (source <= target)
    turned = jnp.concatenate([taps_ref[...], jnp.zeros((5, taps_ref.shape[1]), F32)], axis=0).T
    turned_ref[...] = turned
    taps = turned
    conv_ref[...] = (
        taps[:, 0:1] * values
        + taps[:, 1:2] * jnp.where(position >= 1, pltpu.roll(values, 1, axis=1), 0.0)
        + taps[:, 2:3] * jnp.where(position >= 2, pltpu.roll(values, 2, axis=1), 0.0)
    )
    silu_ref[...] = silu(gates)
    payload_row = lax.broadcasted_iota(jnp.int32, (ROWS, tokens), 0)
    lag_one = (position == 0) & (payload_row == TAIL_ROW + 1)
    lag_two = ((position == 0) & (payload_row == TAIL_ROW)) | ((position == 1) & (payload_row == TAIL_ROW + 1))
    half = feat_dim // 2
    one = (lax.broadcasted_iota(jnp.int32, (half, tokens), 0) == 0).astype(F32)
    for h in range(heads):
        query = queries[h * feat_dim : (h + 1) * feat_dim]
        key = keys[h * feat_dim : (h + 1) * feat_dim]
        blocks = [query * feat_dim ** (-0.25)]
        for gap in range(half):
            other = query if gap == 0 else pltpu.roll(query, feat_dim - gap, axis=0)
            blocks.append(query * other * (2.0 * feat_dim) ** (-0.5))
        blocks.append(query[:half] * query[half:] * (2.0 * feat_dim) ** (-0.5))
        blocks.append(one)
        feature = jnp.concatenate(blocks, axis=0)
        for s in range(per):
            member = slot == s
            at = slice(s * ROWS, (s + 1) * ROWS)
            right_ref[h, at, :tokens] = jnp.where(member, feature, 0.0).astype(BF16)
            right_ref[h, at, tokens : 2 * tokens] = (member & lag_one).astype(F32).astype(BF16)
            right_ref[h, at, 2 * tokens :] = (member & lag_two).astype(F32).astype(BF16)
        dots = lax.dot_general(
            key, query, (((0,), (0,)), ((), ())), preferred_element_type=F32, precision=lax.Precision.HIGHEST
        )
        scores = jnp.where(allowed, 1.0 + dots * feat_dim ** (-0.5) + dots * dots * (1.0 / (2.0 * feat_dim)), 0.0)
        den_ref[h] = jnp.sum(scores, axis=0, keepdims=True)
        scores_ref[h] = scores.astype(BF16)


def stack_kernel(first_ref, second_ref, out_ref):
    out_ref[0] = first_ref[...]
    out_ref[1] = second_ref[...]


def mix_kernel(
    conv_ref, silu_ref, scores_ref, den_ref, right_ref, taps_ref, p0_ref, p1_ref, p2_ref, p3_ref,
    out_weight_ref, *rest,
):
    outs, attended_ref = rest[:4], rest[4]
    per, heads = p0_ref.shape[:2]
    head_dim = attended_ref.shape[0] // heads
    tokens = attended_ref.shape[1]
    for h in range(heads):
        states = []
        for s in range(per):
            total = (
                p0_ref[s, h].astype(F32) + p1_ref[s, h].astype(F32) + p2_ref[s, h].astype(F32) + p3_ref[s, h].astype(F32)
            )
            states.append(split_norm(total, head_dim))
        reached = lax.dot_general(
            jnp.concatenate(states, axis=0), right_ref[h], (((0,), (0,)), ((), ())), preferred_element_type=F32
        )
        prefix_num = reached[:head_dim, :tokens]
        prefix_den = reached[head_dim : head_dim + 1, :tokens] + reached[head_dim + 1 : head_dim + 2, :tokens]
        at = slice(h * head_dim, (h + 1) * head_dim)
        taps = taps_ref[at, :]
        conv = (
            conv_ref[at, :]
            + taps[:, 1:2] * reached[:head_dim, tokens : 2 * tokens]
            + taps[:, 2:3] * reached[:head_dim, 2 * tokens :]
        )
        mixed = (conv * silu_ref[at, :]).astype(BF16)
        local_num = jnp.dot(mixed, scores_ref[h], preferred_element_type=F32)
        attended_ref[at, :] = ((local_num + prefix_num) / (den_ref[h] + prefix_den)).astype(BF16)
    spread_blocks(outs, out_weight_ref, attended_ref[...])


def spread_blocks(outs, weight_ref, right):
    x, z = tp_place()
    rows = outs[0].shape[1]
    for k, out in enumerate(outs):
        to = x ^ k
        for half, at in ((0, 2 * to + z), (1, 2 * to + 1 - z)):
            block = weight_ref[pl.ds(pl.multiple_of(at * rows, 32), rows), :]
            out[half] = jnp.dot(block, right, preferred_element_type=F32).astype(out.dtype)


def ffn_kernel(own_ref, r1_ref, r2_ref, r3_ref, gain_ref, gate_ref, up_ref, down_ref, *rest):
    outs, scratch = rest[:4], rest[4]
    place_blocks(scratch, [own_ref, r1_ref, r2_ref, r3_ref])
    scale = scaled_rows(scratch, gain_ref)
    gate = jnp.dot(gate_ref[...], scratch[...], preferred_element_type=F32) * scale
    up = jnp.dot(up_ref[...], scratch[...], preferred_element_type=F32) * scale
    spread_blocks(outs, down_ref, (silu(gate) * up).astype(BF16))


def shards(
    stream, token_req, request_leaf, parent, owner_map, node_state, node_norm, node_tail, mixer_gain, ffn_gain,
    query_weight, key_weight, value_weight, conv_gate_weight, conv_kernel, out_weight, ffn_gate, ffn_up, ffn_down,
):
    tokens, width = stream.shape
    heads, feats, head_dim = node_state.shape[1:]
    feat_dim = query_weight.shape[1] // heads
    model = value_weight.shape[0]
    req_size = lax.axis_size("req")
    tp_size = lax.axis_size("tp")
    y_size, z_size = 4, req_size // 8
    per = request_leaf.shape[0] // req_size

    def along_x(array, k):
        return lax.ppermute(array, "tp", [(i, i ^ (2 * k)) for i in range(tp_size)])

    def across_z(array):
        return lax.ppermute(array, "tp", [(i, i ^ 1) for i in range(tp_size)])

    def along_z(array, k):
        return lax.ppermute(array, "req", [(i, i ^ (2 * k)) for i in range(req_size)])

    def across_core(array):
        return lax.ppermute(array, "req", [(i, i ^ 1) for i in range(req_size)])

    def along_y(array, k):
        return lax.ppermute(array, "req", [(i, i ^ (2 * z_size * k)) for i in range(req_size)])

    order = (1, 3, 2)

    fold = jnp.asarray(fold_matrix(feat_dim, feats), BF16)
    def in_hbm(array):
        return pltpu.with_memory_space_constraint(array, pltpu.HBM)

    state_in = jnp.transpose(node_state[0], (1, 0, 2))
    own = stream.T
    hbm = pl.BlockSpec(memory_space=pltpu.HBM)
    fold_in = (fold, state_in, node_norm[0], node_tail[0], own)
    payload, own_near = pl.pallas_call(
        fold_kernel,
        out_shape=[sds((heads, ROWS, LANES), BF16), sds(own.shape, BF16)],
        in_specs=[hbm] * len(fold_in),
        out_specs=[VMEM] * 2,
        scratch_shapes=[pltpu.VMEM(a.shape, BF16) for a in fold_in[:4]] + [pltpu.SemaphoreType.DMA((len(fold_in),))],
        compiler_params=PARAMS,
        name="fold",
    )(*[in_hbm(a) for a in fold_in])
    path_in = (out_weight, request_leaf, parent, owner_map)
    out_turned, slots = pl.pallas_call(
        functools.partial(turn_and_slots_kernel, y_size, z_size),
        out_shape=[sds(out_weight.shape[::-1], BF16), sds((y_size * per * 3,), jnp.int32)],
        in_specs=[hbm] * len(path_in),
        out_specs=[VMEM, SMEM],
        scratch_shapes=[pltpu.VMEM(out_weight.shape, BF16)]
        + [pltpu.SMEM(a.shape, jnp.int32) for a in path_in[1:]]
        + [pltpu.SemaphoreType.DMA((len(path_in),))],
        compiler_params=PARAMS,
        name="turn_out",
    )(*[in_hbm(a) for a in path_in])
    from_z = {k: along_z(payload, k) for k in order}

    pair = call(stack_kernel, sds((2, width, tokens), BF16), [VMEM] * 2, (own_near, across_z(own)), name="stack_pair")
    rows = {k: along_x(pair, k) for k in order}

    held_pair, out_turned, *arrived = lax.optimization_barrier(
        (pair, out_turned, from_z[1], from_z[2], from_z[3])
    )
    mine = jnp.stack([payload, *arrived])
    other = across_core(mine)
    def select(shifts, held, name):
        return call(
            functools.partial(select_kernel, shifts),
            [sds((per, heads, ROWS, LANES), BF16)] * len(shifts),
            [SMEM] + [VMEM] * 2,
            (slots, *held),
            scratch=[pltpu.VMEM((2 * z_size + 1, heads, ROWS, LANES), BF16)],
            name=name,
        )

    sent = dict(zip(order, select(order, (mine, other), "select_sent")))
    mine, other, sent = lax.optimization_barrier((mine, other, sent))
    [kept] = select((0,), (mine, other), "select_kept")
    from_y = {k: along_y(sent[k], k) for k in order}

    gain_rows = model // LANES

    def gain_block(gain):
        return jnp.pad(gain.reshape(gain_rows, LANES), ((0, -gain_rows % 8), (0, 0)))

    kept, mixer_rows = lax.optimization_barrier((kept, gain_block(mixer_gain)))
    local = call(
        functools.partial(local_kernel, request_leaf.shape[0]),
        [
            sds((width, tokens), F32),
            sds((width, tokens), F32),
            sds((heads, tokens, tokens), BF16),
            sds((heads, 1, tokens), F32),
            sds((heads, per * ROWS, 3 * tokens), BF16),
            sds((width, 8), F32),
        ],
        [VMEM] * 11,
        (
            pair, rows[1], rows[2], rows[3], mixer_rows, token_req.reshape(1, tokens),
            query_weight.T, key_weight.T, value_weight.T, conv_gate_weight.T, conv_kernel,
        ),
        scratch=[pltpu.VMEM((model, tokens), BF16)],
        name="local",
    )
    parts = call(
        mix_kernel,
        [sds((2, width, tokens), F32)] + [sds((2, width, tokens), BF16)] * 3,
        [VMEM] * 11,
        (*local, kept, from_y[1], from_y[2], from_y[3], out_turned),
        scratch=[pltpu.VMEM((width, tokens), BF16)],
        name="mix",
    )
    got = {k: along_x(parts[k], k) for k in order}
    share = parts[0] + got[1].astype(F32) + got[2].astype(F32) + got[3].astype(F32)
    crossing, down_in = lax.optimization_barrier((jnp.stack([share[1], share[0]]).astype(BF16), ffn_down))
    share_peer = across_z(crossing)
    updated = (held_pair.astype(F32) + share + share_peer.astype(F32)).astype(BF16)
    turned_down = call(turn_kernel, sds(down_in.shape[::-1], BF16), [VMEM], (down_in,), name="turn_down")
    updated, down_turned = lax.optimization_barrier((updated, turned_down))

    wide = {k: along_x(updated, k) for k in order}
    downs = call(
        ffn_kernel,
        [sds((2, width, tokens), F32)] + [sds((2, width, tokens), BF16)] * 3,
        [VMEM] * 8,
        (updated, wide[1], wide[2], wide[3], gain_block(ffn_gain), ffn_gate.T, ffn_up.T, down_turned),
        scratch=[pltpu.VMEM((model, tokens), BF16)],
        name="ffn",
    )
    back = {k: along_x(downs[k], k) for k in order}
    down_share = downs[0] + back[1].astype(F32) + back[2].astype(F32) + back[3].astype(F32)
    down_peer = across_z(down_share[1].astype(BF16))
    result = updated[0].astype(F32) + down_share[0] + down_peer.astype(F32)
    return result.astype(BF16).T


def solution(mesh):
    in_specs = (
        P("req", "tp"), P("req"), P(), P(), P(), P("req", "tp", None, None), P("req", "tp", None), P("req", None, "tp"),
        P(), P(), P(None, "tp"), P(None, "tp"), P(None, "tp"), P(None, "tp"), P(None, "tp"), P("tp", None),
        P(None, "tp"), P(None, "tp"), P("tp", None),
    )
    return jax.shard_map(shards, mesh=mesh, in_specs=in_specs, out_specs=P("req", "tp"), check_vma=False)
```

```python
import functools

import jax
import jax.numpy as jnp
import numpy as np
from jax import lax
from jax.experimental import pallas as pl
from jax.experimental.pallas import tpu as pltpu
from jax.sharding import PartitionSpec as P

EPSILON = 1e-05
ROWS = 160
LANES = 128
TAIL_ROW = 153
F32 = jnp.float32
BF16 = jnp.bfloat16

VMEM = pl.BlockSpec(memory_space=pltpu.VMEM)
SMEM = pl.BlockSpec(memory_space=pltpu.SMEM)
PARAMS = pltpu.CompilerParams(vmem_limit_bytes=12 * 1024 * 1024)


def call(kernel, out_shape, specs, args, scratch=(), name=None):
    single = not isinstance(out_shape, (list, tuple))
    return pl.pallas_call(
        kernel,
        out_shape=out_shape,
        in_specs=specs,
        out_specs=VMEM if single else [VMEM] * len(out_shape),
        scratch_shapes=list(scratch),
        compiler_params=PARAMS,
        name=name,
    )(*args)


def sds(shape, dtype):
    return jax.ShapeDtypeStruct(shape, dtype)


def fold_matrix(feat_dim, feat_count):
    fold = np.zeros((ROWS, feat_count), np.float32)
    row = 0
    for i in range(feat_dim):
        fold[row, 1 + i] = 1
        row += 1
    for gap in range(feat_dim // 2 + 1):
        for i in range(feat_dim if gap < feat_dim // 2 else feat_dim // 2):
            j = (i + gap) % feat_dim
            fold[row, 1 + feat_dim + feat_dim * i + j] = 1
            fold[row, 1 + feat_dim + feat_dim * j + i] = 1
            row += 1
    fold[row, 0] = 1
    return fold


def split_norm(total, head_dim):
    rounded = total.astype(BF16).astype(F32)
    lost = pltpu.roll(total - rounded, 1, axis=1)
    lane = lax.broadcasted_iota(jnp.int32, total.shape, 1)
    return jnp.where(lane == head_dim + 1, total + lost, total).astype(BF16)


def fetch(pairs, sems):
    copies = [pltpu.make_async_copy(a, b, sems.at[i]) for i, (a, b) in enumerate(pairs)]
    for copy in copies:
        copy.start()
    return copies


def fold_kernel(
    fold_hbm, state_hbm, norm_hbm, tail_hbm, own_hbm, out_ref, own_ref, fold_ref, state_ref, norm_ref, tail_ref, sems
):
    copies = fetch(
        (
            (state_hbm, state_ref), (fold_hbm, fold_ref), (norm_hbm, norm_ref), (tail_hbm, tail_ref),
            (own_hbm, own_ref),
        ),
        sems,
    )
    for copy in copies[:4]:
        copy.wait()
    feats, heads, head_dim = state_ref.shape
    fold = fold_ref[...]
    norms = lax.dot_general(fold, norm_ref[...], (((1,), (1,)), ((), ())), preferred_element_type=F32)
    lane = lax.broadcasted_iota(jnp.int32, (ROWS, LANES), 1)
    for h in range(heads):
        state = jnp.dot(fold, state_ref[:, h, :], preferred_element_type=F32)
        norm = jnp.broadcast_to(norms[:, h : h + 1], (ROWS, LANES))
        hi = norm.astype(BF16).astype(F32)
        cols = jnp.where(lane == head_dim, hi, jnp.where(lane == head_dim + 1, norm - hi, 0.0))
        out_ref[h] = cols.astype(BF16)
        out_ref[h, :, :head_dim] = state.astype(BF16)
        out_ref[h, TAIL_ROW : TAIL_ROW + 2, :head_dim] = tail_ref[:, h * head_dim : (h + 1) * head_dim]
    copies[4].wait()


def turn_block(in_ref, out_ref):
    for j in range(out_ref.shape[0] // LANES):
        at = slice(j * LANES, (j + 1) * LANES)
        out_ref[at, :] = in_ref[:, at].T


def turn_kernel(in_ref, out_ref):
    turn_block(in_ref, out_ref)


def turn_and_slots_kernel(
    groups, held, in_hbm, leaf_hbm, parent_hbm, owner_hbm, out_ref, slot_ref, in_ref, leaf_ref, parent_ref, owner_ref, sems
):
    copies = fetch(
        ((in_hbm, in_ref), (leaf_hbm, leaf_ref), (parent_hbm, parent_ref), (owner_hbm, owner_ref)), sems
    )
    for copy in copies:
        copy.wait()
    dev = lax.axis_index("req")
    count = 2 * held
    total_dev = groups * count
    column = dev // count
    place = (dev % count) // 2
    core = dev % 2
    per = leaf_ref.shape[0] // total_dev

    def slot(row):
        k = (place ^ ((row % count) // 2)) + jnp.where((row % 2) == core, 0, held)
        return jnp.where((row // count) == column, k, count)

    for k in range(groups):
        target = dev ^ (k * count)
        for s in range(per):
            leaf = leaf_ref[target * per + s]
            middle = parent_ref[leaf]
            root = parent_ref[middle]
            for i, node in enumerate((leaf, middle, root)):
                slot_ref[(k * per + s) * 3 + i] = slot(owner_ref[node])
    turn_block(in_ref, out_ref)


def select_kernel(shifts, slot_ref, mine_ref, other_ref, *rest):
    outs, pool = rest[:-1], rest[-1]
    held, heads = mine_ref.shape[:2]
    per = outs[0].shape[0]
    for n in range(held):
        pool[n] = mine_ref[n]
        pool[held + n] = other_ref[n]
    pool[2 * held] = jnp.zeros(pool.shape[1:], BF16)
    rows = lax.broadcasted_iota(jnp.int32, (ROWS, LANES), 0)
    is_tail = (rows >= TAIL_ROW) & (rows < TAIL_ROW + 2)
    for out, k in zip(outs, shifts):
        for s in range(per):
            at = [slot_ref[(k * per + s) * 3 + i] for i in range(3)]
            for h in range(heads):
                first, second, third = [pool[a, h].astype(F32) for a in at]
                total = first + jnp.where(is_tail, 0.0, second + third)
                out[s, h] = split_norm(total, 112)


def tp_place():
    index = lax.axis_index("tp")
    return index >> 1, index & 1


def place_blocks(scratch, blocks):
    x, z = tp_place()
    rows = blocks[0].shape[1]
    for k, block in enumerate(blocks):
        source = x ^ k
        scratch[pl.ds(pl.multiple_of((2 * source + z) * rows, 32), rows), :] = block[0]
        scratch[pl.ds(pl.multiple_of((2 * source + 1 - z) * rows, 32), rows), :] = block[1]


def scaled_rows(scratch, gain_ref):
    gain = gain_ref[...].T
    squares = jnp.zeros((LANES, scratch.shape[1]), F32)
    for j in range(scratch.shape[0] // LANES):
        rows = scratch[j * LANES : (j + 1) * LANES, :].astype(F32)
        squares = squares + rows * rows
        scratch[j * LANES : (j + 1) * LANES, :] = (rows * gain[:, j : j + 1]).astype(BF16)
    mean = jnp.sum(squares, axis=0, keepdims=True) / scratch.shape[0]
    return lax.rsqrt(mean + EPSILON)


def silu(v):
    return v / (1.0 + jnp.exp(-v))


def local_kernel(
    total_req, own_ref, r1_ref, r3_ref, r2_ref, gain_ref, token_ref, query_ref, key_ref, value_ref, gate_ref,
    taps_ref, conv_ref, silu_ref, scores_ref, den_ref, right_ref, turned_ref, scratch,
):
    place_blocks(scratch, [own_ref, r1_ref, r2_ref, r3_ref])
    scale = scaled_rows(scratch, gain_ref)
    rows = scratch[...]
    queries = jnp.dot(query_ref[...], rows, preferred_element_type=F32) * scale
    keys = jnp.dot(key_ref[...], rows, preferred_element_type=F32) * scale
    values = (jnp.dot(value_ref[...], rows, preferred_element_type=F32) * scale).astype(BF16).astype(F32)
    gates = jnp.dot(gate_ref[...], rows, preferred_element_type=F32) * scale
    heads = scores_ref.shape[0]
    per = right_ref.shape[1] // ROWS
    feat_dim = queries.shape[0] // heads
    tokens = token_ref.shape[1]
    ids = token_ref[...]
    slot = jnp.where(ids >= total_req, per, ids - lax.axis_index("req") * per)
    lane = lax.broadcasted_iota(jnp.int32, (1, tokens), 1)
    start = jnp.zeros((1, tokens), jnp.int32)
    for s in range(per):
        amount = jnp.sum((slot == s).astype(jnp.int32), axis=1, keepdims=True)
        start = start + jnp.where(slot > s, amount, 0)
    position = lane - start
    source = lax.broadcasted_iota(jnp.int32, (tokens, tokens), 0)
    target = lax.broadcasted_iota(jnp.int32, (tokens, tokens), 1)
    allowed = (source >= start) & (source <= target)
    turned = jnp.concatenate([taps_ref[...], jnp.zeros((5, taps_ref.shape[1]), F32)], axis=0).T
    turned_ref[...] = turned
    taps = turned
    conv_ref[...] = (
        taps[:, 0:1] * values
        + taps[:, 1:2] * jnp.where(position >= 1, pltpu.roll(values, 1, axis=1), 0.0)
        + taps[:, 2:3] * jnp.where(position >= 2, pltpu.roll(values, 2, axis=1), 0.0)
    )
    silu_ref[...] = silu(gates)
    payload_row = lax.broadcasted_iota(jnp.int32, (ROWS, tokens), 0)
    lag_one = (position == 0) & (payload_row == TAIL_ROW + 1)
    lag_two = ((position == 0) & (payload_row == TAIL_ROW)) | ((position == 1) & (payload_row == TAIL_ROW + 1))
    half = feat_dim // 2
    one = (lax.broadcasted_iota(jnp.int32, (half, tokens), 0) == 0).astype(F32)
    for h in range(heads):
        query = queries[h * feat_dim : (h + 1) * feat_dim]
        key = keys[h * feat_dim : (h + 1) * feat_dim]
        blocks = [query * feat_dim ** (-0.25)]
        for gap in range(half):
            other = query if gap == 0 else pltpu.roll(query, feat_dim - gap, axis=0)
            blocks.append(query * other * (2.0 * feat_dim) ** (-0.5))
        blocks.append(query[:half] * query[half:] * (2.0 * feat_dim) ** (-0.5))
        blocks.append(one)
        feature = jnp.concatenate(blocks, axis=0)
        for s in range(per):
            member = slot == s
            at = slice(s * ROWS, (s + 1) * ROWS)
            right_ref[h, at, :tokens] = jnp.where(member, feature, 0.0).astype(BF16)
            right_ref[h, at, tokens : 2 * tokens] = (member & lag_one).astype(F32).astype(BF16)
            right_ref[h, at, 2 * tokens :] = (member & lag_two).astype(F32).astype(BF16)
        dots = lax.dot_general(
            key, query, (((0,), (0,)), ((), ())), preferred_element_type=F32, precision=lax.Precision.HIGHEST
        )
        scores = jnp.where(allowed, 1.0 + dots * feat_dim ** (-0.5) + dots * dots * (1.0 / (2.0 * feat_dim)), 0.0)
        den_ref[h] = jnp.sum(scores, axis=0, keepdims=True)
        scores_ref[h] = scores.astype(BF16)


def stack_kernel(first_ref, second_ref, out_ref):
    out_ref[0] = first_ref[...]
    out_ref[1] = second_ref[...]


def mix_kernel(
    conv_ref, silu_ref, scores_ref, den_ref, right_ref, taps_ref, p0_ref, p1_ref, p2_ref, p3_ref,
    out_weight_ref, *rest,
):
    outs, attended_ref = rest[:4], rest[4]
    per, heads = p0_ref.shape[:2]
    head_dim = attended_ref.shape[0] // heads
    tokens = attended_ref.shape[1]
    for h in range(heads):
        states = []
        for s in range(per):
            total = (
                p0_ref[s, h].astype(F32) + p1_ref[s, h].astype(F32) + p2_ref[s, h].astype(F32) + p3_ref[s, h].astype(F32)
            )
            states.append(split_norm(total, head_dim))
        reached = lax.dot_general(
            jnp.concatenate(states, axis=0), right_ref[h], (((0,), (0,)), ((), ())), preferred_element_type=F32
        )
        prefix_num = reached[:head_dim, :tokens]
        prefix_den = reached[head_dim : head_dim + 1, :tokens] + reached[head_dim + 1 : head_dim + 2, :tokens]
        at = slice(h * head_dim, (h + 1) * head_dim)
        taps = taps_ref[at, :]
        conv = (
            conv_ref[at, :]
            + taps[:, 1:2] * reached[:head_dim, tokens : 2 * tokens]
            + taps[:, 2:3] * reached[:head_dim, 2 * tokens :]
        )
        mixed = (conv * silu_ref[at, :]).astype(BF16)
        local_num = jnp.dot(mixed, scores_ref[h], preferred_element_type=F32)
        attended_ref[at, :] = ((local_num + prefix_num) / (den_ref[h] + prefix_den)).astype(BF16)
    spread_blocks(outs, out_weight_ref, attended_ref[...])


def spread_blocks(outs, weight_ref, right):
    x, z = tp_place()
    rows = outs[0].shape[1]
    for k, out in enumerate(outs):
        to = x ^ k
        for half, at in ((0, 2 * to + z), (1, 2 * to + 1 - z)):
            block = weight_ref[pl.ds(pl.multiple_of(at * rows, 32), rows), :]
            out[half] = jnp.dot(block, right, preferred_element_type=F32).astype(out.dtype)


def ffn_kernel(own_ref, r1_ref, r2_ref, r3_ref, gain_ref, gate_ref, up_ref, down_ref, *rest):
    outs, scratch = rest[:4], rest[4]
    place_blocks(scratch, [own_ref, r1_ref, r2_ref, r3_ref])
    scale = scaled_rows(scratch, gain_ref)
    gate = jnp.dot(gate_ref[...], scratch[...], preferred_element_type=F32) * scale
    up = jnp.dot(up_ref[...], scratch[...], preferred_element_type=F32) * scale
    spread_blocks(outs, down_ref, (silu(gate) * up).astype(BF16))


def shards(
    stream, token_req, request_leaf, parent, owner_map, node_state, node_norm, node_tail, mixer_gain, ffn_gain,
    query_weight, key_weight, value_weight, conv_gate_weight, conv_kernel, out_weight, ffn_gate, ffn_up, ffn_down,
):
    tokens, width = stream.shape
    heads, feats, head_dim = node_state.shape[1:]
    feat_dim = query_weight.shape[1] // heads
    model = value_weight.shape[0]
    req_size = lax.axis_size("req")
    tp_size = lax.axis_size("tp")
    y_size, z_size = 4, req_size // 8
    per = request_leaf.shape[0] // req_size

    def along_x(array, k):
        return lax.ppermute(array, "tp", [(i, i ^ (2 * k)) for i in range(tp_size)])

    def across_z(array):
        return lax.ppermute(array, "tp", [(i, i ^ 1) for i in range(tp_size)])

    def along_z(array, k):
        return lax.ppermute(array, "req", [(i, i ^ (2 * k)) for i in range(req_size)])

    def across_core(array):
        return lax.ppermute(array, "req", [(i, i ^ 1) for i in range(req_size)])

    def along_y(array, k):
        return lax.ppermute(array, "req", [(i, i ^ (2 * z_size * k)) for i in range(req_size)])

    order = (2, 1, 3)

    fold = jnp.asarray(fold_matrix(feat_dim, feats), BF16)
    def in_hbm(array):
        return pltpu.with_memory_space_constraint(array, pltpu.HBM)

    state_in = jnp.transpose(node_state[0], (1, 0, 2))
    own = stream.T
    hbm = pl.BlockSpec(memory_space=pltpu.HBM)
    fold_in = (fold, state_in, node_norm[0], node_tail[0], own)
    payload, own_near = pl.pallas_call(
        fold_kernel,
        out_shape=[sds((heads, ROWS, LANES), BF16), sds(own.shape, BF16)],
        in_specs=[hbm] * len(fold_in),
        out_specs=[VMEM] * 2,
        scratch_shapes=[pltpu.VMEM(a.shape, BF16) for a in fold_in[:4]] + [pltpu.SemaphoreType.DMA((len(fold_in),))],
        compiler_params=PARAMS,
        name="fold",
    )(*[in_hbm(a) for a in fold_in])
    path_in = (out_weight, request_leaf, parent, owner_map)
    out_turned, slots = pl.pallas_call(
        functools.partial(turn_and_slots_kernel, y_size, z_size),
        out_shape=[sds(out_weight.shape[::-1], BF16), sds((y_size * per * 3,), jnp.int32)],
        in_specs=[hbm] * len(path_in),
        out_specs=[VMEM, SMEM],
        scratch_shapes=[pltpu.VMEM(out_weight.shape, BF16)]
        + [pltpu.SMEM(a.shape, jnp.int32) for a in path_in[1:]]
        + [pltpu.SemaphoreType.DMA((len(path_in),))],
        compiler_params=PARAMS,
        name="turn_out",
    )(*[in_hbm(a) for a in path_in])
    from_z = {k: along_z(payload, k) for k in order}

    pair = call(stack_kernel, sds((2, width, tokens), BF16), [VMEM] * 2, (own_near, across_z(own)), name="stack_pair")
    rows = {k: along_x(pair, k) for k in order}

    held_pair, out_turned, *arrived = lax.optimization_barrier(
        (pair, out_turned, from_z[1], from_z[2], from_z[3])
    )
    mine = jnp.stack([payload, *arrived])
    other = across_core(mine)
    def select(shifts, held, name):
        return call(
            functools.partial(select_kernel, shifts),
            [sds((per, heads, ROWS, LANES), BF16)] * len(shifts),
            [SMEM] + [VMEM] * 2,
            (slots, *held),
            scratch=[pltpu.VMEM((2 * z_size + 1, heads, ROWS, LANES), BF16)],
            name=name,
        )

    sent = dict(zip(order, select(order, (mine, other), "select_sent")))
    mine, other, sent = lax.optimization_barrier((mine, other, sent))
    [kept] = select((0,), (mine, other), "select_kept")
    from_y = {k: along_y(sent[k], k) for k in order}

    gain_rows = model // LANES

    def gain_block(gain):
        return jnp.pad(gain.reshape(gain_rows, LANES), ((0, -gain_rows % 8), (0, 0)))

    kept, mixer_rows = lax.optimization_barrier((kept, gain_block(mixer_gain)))
    local = call(
        functools.partial(local_kernel, request_leaf.shape[0]),
        [
            sds((width, tokens), F32),
            sds((width, tokens), F32),
            sds((heads, tokens, tokens), BF16),
            sds((heads, 1, tokens), F32),
            sds((heads, per * ROWS, 3 * tokens), BF16),
            sds((width, 8), F32),
        ],
        [VMEM] * 11,
        (
            pair, rows[1], rows[3], rows[2], mixer_rows, token_req.reshape(1, tokens),
            query_weight.T, key_weight.T, value_weight.T, conv_gate_weight.T, conv_kernel,
        ),
        scratch=[pltpu.VMEM((model, tokens), BF16)],
        name="local",
    )
    parts = call(
        mix_kernel,
        [sds((2, width, tokens), F32)] + [sds((2, width, tokens), BF16)] * 3,
        [VMEM] * 11,
        (*local, kept, from_y[2], from_y[1], from_y[3], out_turned),
        scratch=[pltpu.VMEM((width, tokens), BF16)],
        name="mix",
    )
    got = {k: along_x(parts[k], k) for k in order}
    share = parts[0] + got[2].astype(F32) + got[1].astype(F32) + got[3].astype(F32)
    crossing, down_in = lax.optimization_barrier((jnp.stack([share[1], share[0]]).astype(BF16), ffn_down))
    share_peer = across_z(crossing)
    updated = (held_pair.astype(F32) + share + share_peer.astype(F32)).astype(BF16)
    turned_down = call(turn_kernel, sds(down_in.shape[::-1], BF16), [VMEM], (down_in,), name="turn_down")
    updated, down_turned = lax.optimization_barrier((updated, turned_down))

    wide = {k: along_x(updated, k) for k in order}
    downs = call(
        ffn_kernel,
        [sds((2, width, tokens), F32)] + [sds((2, width, tokens), BF16)] * 3,
        [VMEM] * 8,
        (updated, wide[1], wide[2], wide[3], gain_block(ffn_gain), ffn_gate.T, ffn_up.T, down_turned),
        scratch=[pltpu.VMEM((model, tokens), BF16)],
        name="ffn",
    )
    back = {k: along_x(downs[k], k) for k in order}
    down_share = downs[0] + back[2].astype(F32) + back[1].astype(F32) + back[3].astype(F32)
    down_peer = across_z(down_share[1].astype(BF16))
    result = updated[0].astype(F32) + down_share[0] + down_peer.astype(F32)
    return result.astype(BF16).T


def solution(mesh):
    in_specs = (
        P("req", "tp"), P("req"), P(), P(), P(), P("req", "tp", None, None), P("req", "tp", None), P("req", None, "tp"),
        P(), P(), P(None, "tp"), P(None, "tp"), P(None, "tp"), P(None, "tp"), P(None, "tp"), P("tp", None),
        P(None, "tp"), P(None, "tp"), P("tp", None),
    )
    return jax.shard_map(shards, mesh=mesh, in_specs=in_specs, out_specs=P("req", "tp"), check_vma=False)
```

```python
import functools

import jax
import jax.numpy as jnp
import numpy as np
from jax import lax
from jax.experimental import pallas as pl
from jax.experimental.pallas import tpu as pltpu
from jax.sharding import PartitionSpec as P

EPSILON = 1e-05
ROWS = 160
LANES = 128
TAIL_ROW = 153
F32 = jnp.float32
BF16 = jnp.bfloat16

VMEM = pl.BlockSpec(memory_space=pltpu.VMEM)
SMEM = pl.BlockSpec(memory_space=pltpu.SMEM)
PARAMS = pltpu.CompilerParams(vmem_limit_bytes=12 * 1024 * 1024)


def call(kernel, out_shape, specs, args, scratch=(), name=None):
    single = not isinstance(out_shape, (list, tuple))
    return pl.pallas_call(
        kernel,
        out_shape=out_shape,
        in_specs=specs,
        out_specs=VMEM if single else [VMEM] * len(out_shape),
        scratch_shapes=list(scratch),
        compiler_params=PARAMS,
        name=name,
    )(*args)


def sds(shape, dtype):
    return jax.ShapeDtypeStruct(shape, dtype)


def fold_matrix(feat_dim, feat_count):
    fold = np.zeros((ROWS, feat_count), np.float32)
    row = 0
    for i in range(feat_dim):
        fold[row, 1 + i] = 1
        row += 1
    for gap in range(feat_dim // 2 + 1):
        for i in range(feat_dim if gap < feat_dim // 2 else feat_dim // 2):
            j = (i + gap) % feat_dim
            fold[row, 1 + feat_dim + feat_dim * i + j] = 1
            fold[row, 1 + feat_dim + feat_dim * j + i] = 1
            row += 1
    fold[row, 0] = 1
    return fold


def split_norm(total, head_dim):
    rounded = total.astype(BF16).astype(F32)
    lost = pltpu.roll(total - rounded, 1, axis=1)
    lane = lax.broadcasted_iota(jnp.int32, total.shape, 1)
    return jnp.where(lane == head_dim + 1, total + lost, total).astype(BF16)


def fetch(pairs, sems):
    copies = [pltpu.make_async_copy(a, b, sems.at[i]) for i, (a, b) in enumerate(pairs)]
    for copy in copies:
        copy.start()
    return copies


def fold_kernel(
    fold_hbm, state_hbm, norm_hbm, tail_hbm, own_hbm, out_ref, own_ref, fold_ref, state_ref, norm_ref, tail_ref, sems
):
    copies = fetch(
        (
            (state_hbm, state_ref), (fold_hbm, fold_ref), (norm_hbm, norm_ref), (tail_hbm, tail_ref),
            (own_hbm, own_ref),
        ),
        sems,
    )
    for copy in copies[:4]:
        copy.wait()
    feats, heads, head_dim = state_ref.shape
    fold = fold_ref[...]
    norms = lax.dot_general(fold, norm_ref[...], (((1,), (1,)), ((), ())), preferred_element_type=F32)
    lane = lax.broadcasted_iota(jnp.int32, (ROWS, LANES), 1)
    for h in range(heads):
        state = jnp.dot(fold, state_ref[:, h, :], preferred_element_type=F32)
        norm = jnp.broadcast_to(norms[:, h : h + 1], (ROWS, LANES))
        hi = norm.astype(BF16).astype(F32)
        cols = jnp.where(lane == head_dim, hi, jnp.where(lane == head_dim + 1, norm - hi, 0.0))
        out_ref[h] = cols.astype(BF16)
        out_ref[h, :, :head_dim] = state.astype(BF16)
        out_ref[h, TAIL_ROW : TAIL_ROW + 2, :head_dim] = tail_ref[:, h * head_dim : (h + 1) * head_dim]
    copies[4].wait()


def turn_block(in_ref, out_ref):
    for j in range(out_ref.shape[0] // LANES):
        at = slice(j * LANES, (j + 1) * LANES)
        out_ref[at, :] = in_ref[:, at].T


def scale_block(in_ref, gain_ref, out_ref):
    for j in range(in_ref.shape[1] // LANES):
        at = slice(j * LANES, (j + 1) * LANES)
        out_ref[:, at] = (in_ref[:, at].astype(F32) * gain_ref[j : j + 1, :]).astype(BF16)


def ffn_weights_kernel(down_ref, gate_ref, up_ref, gain_ref, turned_ref, gate_out_ref, up_out_ref):
    turn_block(down_ref, turned_ref)
    scale_block(gate_ref, gain_ref, gate_out_ref)
    scale_block(up_ref, gain_ref, up_out_ref)


def mixer_weights_kernel(groups, held, *refs):
    out_ref, slot_ref, wide_ref = refs[9:12]
    copies = fetch(tuple(zip(refs[:9], refs[12:21])), refs[21])
    in_ref, leaf_ref, parent_ref, owner_ref, query_ref, key_ref, value_ref, gate_ref, gain_ref = refs[12:21]
    for copy in copies:
        copy.wait()
    row = 0
    for part in (query_ref, key_ref, value_ref, gate_ref):
        scale_block(part, gain_ref, wide_ref.at[row : row + part.shape[0]])
        row += part.shape[0]
    dev = lax.axis_index("req")
    count = 2 * held
    total_dev = groups * count
    column = dev // count
    place = (dev % count) // 2
    core = dev % 2
    per = leaf_ref.shape[0] // total_dev

    def slot(row):
        k = (place ^ ((row % count) // 2)) + jnp.where((row % 2) == core, 0, held)
        return jnp.where((row // count) == column, k, count)

    for k in range(groups):
        target = dev ^ (k * count)
        for s in range(per):
            leaf = leaf_ref[target * per + s]
            middle = parent_ref[leaf]
            root = parent_ref[middle]
            for i, node in enumerate((leaf, middle, root)):
                slot_ref[(k * per + s) * 3 + i] = slot(owner_ref[node])
    turn_block(in_ref, out_ref)


def select_kernel(shifts, slot_ref, mine_ref, other_ref, *rest):
    outs, pool = rest[:-1], rest[-1]
    held, heads = mine_ref.shape[:2]
    per = outs[0].shape[0]
    for n in range(held):
        pool[n] = mine_ref[n]
        pool[held + n] = other_ref[n]
    pool[2 * held] = jnp.zeros(pool.shape[1:], BF16)
    rows = lax.broadcasted_iota(jnp.int32, (ROWS, LANES), 0)
    is_tail = (rows >= TAIL_ROW) & (rows < TAIL_ROW + 2)
    for out, k in zip(outs, shifts):
        for s in range(per):
            at = [slot_ref[(k * per + s) * 3 + i] for i in range(3)]
            for h in range(heads):
                first, second, third = [pool[a, h].astype(F32) for a in at]
                total = first + jnp.where(is_tail, 0.0, second + third)
                out[s, h] = split_norm(total, 112)


def tp_place():
    index = lax.axis_index("tp")
    return index >> 1, index & 1


def place_blocks(scratch, blocks):
    x, z = tp_place()
    rows = blocks[0].shape[1]
    for k, block in enumerate(blocks):
        source = x ^ k
        scratch[pl.ds(pl.multiple_of((2 * source + z) * rows, 32), rows), :] = block[0]
        scratch[pl.ds(pl.multiple_of((2 * source + 1 - z) * rows, 32), rows), :] = block[1]


def row_scale(scratch):
    squares = jnp.zeros((LANES, scratch.shape[1]), F32)
    for j in range(scratch.shape[0] // LANES):
        rows = scratch[j * LANES : (j + 1) * LANES, :].astype(F32)
        squares = squares + rows * rows
    mean = jnp.sum(squares, axis=0, keepdims=True) / scratch.shape[0]
    return lax.rsqrt(mean + EPSILON)


def silu(v):
    return v / (1.0 + jnp.exp(-v))


def local_kernel(
    total_req, own_ref, r1_ref, r3_ref, r2_ref, token_ref, weight_ref, kept_ref,
    taps_ref, conv_ref, silu_ref, scores_ref, den_ref, right_ref, turned_ref, scratch,
):
    place_blocks(scratch, [own_ref, r1_ref, r2_ref, r3_ref])
    del kept_ref
    scale = row_scale(scratch)
    heads = scores_ref.shape[0]
    proj = jnp.dot(weight_ref[...], scratch[...], preferred_element_type=F32) * scale
    value_dim = conv_ref.shape[0]
    narrow = (proj.shape[0] - 2 * value_dim) // 2
    queries = proj[:narrow]
    keys = proj[narrow : 2 * narrow]
    values = proj[2 * narrow : 2 * narrow + value_dim].astype(BF16).astype(F32)
    gates = proj[2 * narrow + value_dim :]
    per = right_ref.shape[1] // ROWS
    feat_dim = queries.shape[0] // heads
    tokens = token_ref.shape[1]
    ids = token_ref[...]
    slot = jnp.where(ids >= total_req, per, ids - lax.axis_index("req") * per)
    lane = lax.broadcasted_iota(jnp.int32, (1, tokens), 1)
    start = jnp.zeros((1, tokens), jnp.int32)
    for s in range(per):
        amount = jnp.sum((slot == s).astype(jnp.int32), axis=1, keepdims=True)
        start = start + jnp.where(slot > s, amount, 0)
    position = lane - start
    source = lax.broadcasted_iota(jnp.int32, (tokens, tokens), 0)
    target = lax.broadcasted_iota(jnp.int32, (tokens, tokens), 1)
    allowed = (source >= start) & (source <= target)
    turned = jnp.concatenate([taps_ref[...], jnp.zeros((5, taps_ref.shape[1]), F32)], axis=0).T
    turned_ref[...] = turned
    taps = turned
    conv_ref[...] = (
        taps[:, 0:1] * values
        + taps[:, 1:2] * jnp.where(position >= 1, pltpu.roll(values, 1, axis=1), 0.0)
        + taps[:, 2:3] * jnp.where(position >= 2, pltpu.roll(values, 2, axis=1), 0.0)
    )
    silu_ref[...] = silu(gates)
    payload_row = lax.broadcasted_iota(jnp.int32, (ROWS, tokens), 0)
    lag_one = (position == 0) & (payload_row == TAIL_ROW + 1)
    lag_two = ((position == 0) & (payload_row == TAIL_ROW)) | ((position == 1) & (payload_row == TAIL_ROW + 1))
    half = feat_dim // 2
    one = (lax.broadcasted_iota(jnp.int32, (half, tokens), 0) == 0).astype(F32)
    for h in range(heads):
        query = queries[h * feat_dim : (h + 1) * feat_dim]
        key = keys[h * feat_dim : (h + 1) * feat_dim]
        blocks = [query * feat_dim ** (-0.25)]
        for gap in range(half):
            other = query if gap == 0 else pltpu.roll(query, feat_dim - gap, axis=0)
            blocks.append(query * other * (2.0 * feat_dim) ** (-0.5))
        blocks.append(query[:half] * query[half:] * (2.0 * feat_dim) ** (-0.5))
        blocks.append(one)
        feature = jnp.concatenate(blocks, axis=0)
        for s in range(per):
            member = slot == s
            at = slice(s * ROWS, (s + 1) * ROWS)
            right_ref[h, at, :tokens] = jnp.where(member, feature, 0.0).astype(BF16)
            right_ref[h, at, tokens : 2 * tokens] = (member & lag_one).astype(F32).astype(BF16)
            right_ref[h, at, 2 * tokens :] = (member & lag_two).astype(F32).astype(BF16)
        dots = lax.dot_general(
            key, query, (((0,), (0,)), ((), ())), preferred_element_type=F32, precision=lax.Precision.HIGHEST
        )
        scores = jnp.where(allowed, 1.0 + dots * feat_dim ** (-0.5) + dots * dots * (1.0 / (2.0 * feat_dim)), 0.0)
        den_ref[h] = jnp.sum(scores, axis=0, keepdims=True)
        scores_ref[h] = scores.astype(BF16)


def stack_kernel(first_ref, second_ref, out_ref):
    out_ref[0] = first_ref[...]
    out_ref[1] = second_ref[...]


def mix_kernel(
    conv_ref, silu_ref, scores_ref, den_ref, right_ref, taps_ref, p0_ref, p1_ref, p2_ref, p3_ref,
    out_weight_ref, *rest,
):
    outs, attended_ref = rest[:4], rest[4]
    per, heads = p0_ref.shape[:2]
    head_dim = attended_ref.shape[0] // heads
    tokens = attended_ref.shape[1]
    for h in range(heads):
        states = []
        for s in range(per):
            total = (
                p0_ref[s, h].astype(F32) + p1_ref[s, h].astype(F32) + p2_ref[s, h].astype(F32) + p3_ref[s, h].astype(F32)
            )
            states.append(split_norm(total, head_dim))
        reached = lax.dot_general(
            jnp.concatenate(states, axis=0), right_ref[h], (((0,), (0,)), ((), ())), preferred_element_type=F32
        )
        prefix_num = reached[:head_dim, :tokens]
        prefix_den = reached[head_dim : head_dim + 1, :tokens] + reached[head_dim + 1 : head_dim + 2, :tokens]
        at = slice(h * head_dim, (h + 1) * head_dim)
        taps = taps_ref[at, :]
        conv = (
            conv_ref[at, :]
            + taps[:, 1:2] * reached[:head_dim, tokens : 2 * tokens]
            + taps[:, 2:3] * reached[:head_dim, 2 * tokens :]
        )
        mixed = (conv * silu_ref[at, :]).astype(BF16)
        local_num = jnp.dot(mixed, scores_ref[h], preferred_element_type=F32)
        attended_ref[at, :] = ((local_num + prefix_num) / (den_ref[h] + prefix_den)).astype(BF16)
    spread_blocks(outs, out_weight_ref, attended_ref[...])


def spread_blocks(outs, weight_ref, right):
    x, z = tp_place()
    rows = outs[0].shape[1]
    for k, out in enumerate(outs):
        to = x ^ k
        for half, at in ((0, 2 * to + z), (1, 2 * to + 1 - z)):
            block = weight_ref[pl.ds(pl.multiple_of(at * rows, 32), rows), :]
            out[half] = jnp.dot(block, right, preferred_element_type=F32).astype(out.dtype)


def ffn_kernel(own_ref, r1_ref, r3_ref, r2_ref, gate_ref, up_ref, down_ref, *rest):
    outs, scratch = rest[:4], rest[4]
    place_blocks(scratch, [own_ref, r1_ref, r2_ref, r3_ref])
    scale = row_scale(scratch)
    gate = jnp.dot(gate_ref[...], scratch[...], preferred_element_type=F32) * scale
    up = jnp.dot(up_ref[...], scratch[...], preferred_element_type=F32) * scale
    spread_blocks(outs, down_ref, (silu(gate) * up).astype(BF16))


def shards(
    stream, token_req, request_leaf, parent, owner_map, node_state, node_norm, node_tail, mixer_gain, ffn_gain,
    query_weight, key_weight, value_weight, conv_gate_weight, conv_kernel, out_weight, ffn_gate, ffn_up, ffn_down,
):
    tokens, width = stream.shape
    heads, feats, head_dim = node_state.shape[1:]
    feat_dim = query_weight.shape[1] // heads
    model = value_weight.shape[0]
    req_size = lax.axis_size("req")
    tp_size = lax.axis_size("tp")
    y_size, z_size = 4, req_size // 8
    per = request_leaf.shape[0] // req_size

    def along_x(array, k):
        return lax.ppermute(array, "tp", [(i, i ^ (2 * k)) for i in range(tp_size)])

    def across_z(array):
        return lax.ppermute(array, "tp", [(i, i ^ 1) for i in range(tp_size)])

    def along_z(array, k):
        return lax.ppermute(array, "req", [(i, i ^ (2 * k)) for i in range(req_size)])

    def across_core(array):
        return lax.ppermute(array, "req", [(i, i ^ 1) for i in range(req_size)])

    def along_y(array, k):
        return lax.ppermute(array, "req", [(i, i ^ (2 * z_size * k)) for i in range(req_size)])

    order = (2, 1, 3)

    fold = jnp.asarray(fold_matrix(feat_dim, feats), BF16)
    def in_hbm(array):
        return pltpu.with_memory_space_constraint(array, pltpu.HBM)

    state_in = jnp.transpose(node_state[0], (1, 0, 2))
    own = stream.T
    hbm = pl.BlockSpec(memory_space=pltpu.HBM)
    fold_in = (fold, state_in, node_norm[0], node_tail[0], own)
    payload, own_near = pl.pallas_call(
        fold_kernel,
        out_shape=[sds((heads, ROWS, LANES), BF16), sds(own.shape, BF16)],
        in_specs=[hbm] * len(fold_in),
        out_specs=[VMEM] * 2,
        scratch_shapes=[pltpu.VMEM(a.shape, BF16) for a in fold_in[:4]] + [pltpu.SemaphoreType.DMA((len(fold_in),))],
        compiler_params=PARAMS,
        name="fold",
    )(*[in_hbm(a) for a in fold_in])
    gain_rows = model // LANES

    def gain_block(gain):
        return jnp.pad(gain.reshape(gain_rows, LANES), ((0, -gain_rows % 8), (0, 0)))

    narrow = (query_weight.T, key_weight.T, value_weight.T, conv_gate_weight.T)
    ready_in = (out_weight, request_leaf, parent, owner_map, *narrow, gain_block(mixer_gain))
    out_turned, slots, wide_weight = pl.pallas_call(
        functools.partial(mixer_weights_kernel, y_size, z_size),
        out_shape=[
            sds(out_weight.shape[::-1], BF16),
            sds((y_size * per * 3,), jnp.int32),
            sds((sum(a.shape[0] for a in narrow), model), BF16),
        ],
        in_specs=[hbm] * len(ready_in),
        out_specs=[VMEM, SMEM, VMEM],
        scratch_shapes=[
            pltpu.SMEM(a.shape, a.dtype) if a.dtype == jnp.int32 else pltpu.VMEM(a.shape, a.dtype) for a in ready_in
        ]
        + [pltpu.SemaphoreType.DMA((len(ready_in),))],
        compiler_params=PARAMS,
        name="mixer_weights",
    )(*[in_hbm(a) for a in ready_in])
    from_z = {k: along_z(payload, k) for k in order}

    pair = call(stack_kernel, sds((2, width, tokens), BF16), [VMEM] * 2, (own_near, across_z(own)), name="stack_pair")
    rows = {k: along_x(pair, k) for k in order}

    held_pair, out_turned, *arrived = lax.optimization_barrier(
        (pair, out_turned, from_z[1], from_z[2], from_z[3])
    )
    mine = jnp.stack([payload, *arrived])
    other = across_core(mine)
    def select(shifts, held, name):
        return call(
            functools.partial(select_kernel, shifts),
            [sds((per, heads, ROWS, LANES), BF16)] * len(shifts),
            [SMEM] + [VMEM] * 2,
            (slots, *held),
            scratch=[pltpu.VMEM((2 * z_size + 1, heads, ROWS, LANES), BF16)],
            name=name,
        )

    sent = dict(zip(order, select(order, (mine, other), "select_sent")))
    mine, other, sent = lax.optimization_barrier((mine, other, sent))
    [kept] = select((0,), (mine, other), "select_kept")
    from_y = {k: along_y(sent[k], k) for k in order}

    local = call(
        functools.partial(local_kernel, request_leaf.shape[0]),
        [
            sds((width, tokens), F32),
            sds((width, tokens), F32),
            sds((heads, tokens, tokens), BF16),
            sds((heads, 1, tokens), F32),
            sds((heads, per * ROWS, 3 * tokens), BF16),
            sds((width, 8), F32),
        ],
        [VMEM] * 6 + [pl.BlockSpec(memory_space=pl.ANY), VMEM],
        (
            pair, rows[1], rows[3], rows[2], token_req.reshape(1, tokens), wide_weight, kept, conv_kernel,
        ),
        scratch=[pltpu.VMEM((model, tokens), BF16)],
        name="local",
    )
    parts = call(
        mix_kernel,
        [sds((2, width, tokens), F32)] + [sds((2, width, tokens), BF16)] * 3,
        [VMEM] * 11,
        (*local, kept, from_y[2], from_y[1], from_y[3], out_turned),
        scratch=[pltpu.VMEM((width, tokens), BF16)],
        name="mix",
    )
    got = {k: along_x(parts[k], k) for k in order}
    share = parts[0] + got[2].astype(F32) + got[1].astype(F32) + got[3].astype(F32)
    crossing, down_in = lax.optimization_barrier((jnp.stack([share[1], share[0]]).astype(BF16), ffn_down))
    share_peer = across_z(crossing)
    ffn_shape = ffn_gate.shape[::-1]
    ready = call(
        ffn_weights_kernel,
        [sds(down_in.shape[::-1], BF16), sds(ffn_shape, BF16), sds(ffn_shape, BF16)],
        [VMEM] * 4,
        (down_in, ffn_gate.T, ffn_up.T, gain_block(ffn_gain)),
        name="ffn_weights",
    )
    updated = (held_pair.astype(F32) + share + share_peer.astype(F32)).astype(BF16)
    updated, down_turned, gate_scaled, up_scaled = lax.optimization_barrier((updated, *ready))

    wide = {k: along_x(updated, k) for k in order}
    downs = call(
        ffn_kernel,
        [sds((2, width, tokens), F32)] + [sds((2, width, tokens), BF16)] * 3,
        [VMEM] * 7,
        (updated, wide[1], wide[3], wide[2], gate_scaled, up_scaled, down_turned),
        scratch=[pltpu.VMEM((model, tokens), BF16)],
        name="ffn",
    )
    back = {k: along_x(downs[k], k) for k in order}
    down_share = downs[0] + back[2].astype(F32) + back[1].astype(F32) + back[3].astype(F32)
    down_peer = across_z(down_share[1].astype(BF16))
    result = updated[0].astype(F32) + down_share[0] + down_peer.astype(F32)
    return result.astype(BF16).T


def solution(mesh):
    in_specs = (
        P("req", "tp"), P("req"), P(), P(), P(), P("req", "tp", None, None), P("req", "tp", None), P("req", None, "tp"),
        P(), P(), P(None, "tp"), P(None, "tp"), P(None, "tp"), P(None, "tp"), P(None, "tp"), P("tp", None),
        P(None, "tp"), P(None, "tp"), P("tp", None),
    )
    return jax.shard_map(shards, mesh=mesh, in_specs=in_specs, out_specs=P("req", "tp"), check_vma=False)
```

```python
import functools

import jax
import jax.numpy as jnp
import numpy as np
from jax import lax
from jax.experimental import pallas as pl
from jax.experimental.pallas import tpu as pltpu
from jax.sharding import PartitionSpec as P

EPSILON = 1e-05
ROWS = 160
LANES = 128
TAIL_ROW = 153
F32 = jnp.float32
BF16 = jnp.bfloat16

VMEM = pl.BlockSpec(memory_space=pltpu.VMEM)
SMEM = pl.BlockSpec(memory_space=pltpu.SMEM)
PARAMS = pltpu.CompilerParams(vmem_limit_bytes=12 * 1024 * 1024)


def call(kernel, out_shape, specs, args, scratch=(), name=None):
    single = not isinstance(out_shape, (list, tuple))
    return pl.pallas_call(
        kernel,
        out_shape=out_shape,
        in_specs=specs,
        out_specs=VMEM if single else [VMEM] * len(out_shape),
        scratch_shapes=list(scratch),
        compiler_params=PARAMS,
        name=name,
    )(*args)


def sds(shape, dtype):
    return jax.ShapeDtypeStruct(shape, dtype)


def fold_matrix(feat_dim, feat_count):
    fold = np.zeros((ROWS, feat_count), np.float32)
    row = 0
    for i in range(feat_dim):
        fold[row, 1 + i] = 1
        row += 1
    for gap in range(feat_dim // 2 + 1):
        for i in range(feat_dim if gap < feat_dim // 2 else feat_dim // 2):
            j = (i + gap) % feat_dim
            fold[row, 1 + feat_dim + feat_dim * i + j] = 1
            fold[row, 1 + feat_dim + feat_dim * j + i] = 1
            row += 1
    fold[row, 0] = 1
    return fold


def split_norm(total, head_dim):
    rounded = total.astype(BF16).astype(F32)
    lost = pltpu.roll(total - rounded, 1, axis=1)
    lane = lax.broadcasted_iota(jnp.int32, total.shape, 1)
    return jnp.where(lane == head_dim + 1, total + lost, total).astype(BF16)


def fetch(pairs, sems):
    copies = [pltpu.make_async_copy(a, b, sems.at[i]) for i, (a, b) in enumerate(pairs)]
    for copy in copies:
        copy.start()
    return copies


def fold_kernel(
    fold_hbm, state_hbm, norm_hbm, tail_hbm, own_hbm, out_ref, own_ref, fold_ref, state_ref, norm_ref, tail_ref, sems
):
    copies = fetch(
        (
            (state_hbm, state_ref), (fold_hbm, fold_ref), (norm_hbm, norm_ref), (tail_hbm, tail_ref),
            (own_hbm, own_ref),
        ),
        sems,
    )
    for copy in copies[:4]:
        copy.wait()
    feats, heads, head_dim = state_ref.shape
    fold = fold_ref[...]
    norms = lax.dot_general(fold, norm_ref[...], (((1,), (1,)), ((), ())), preferred_element_type=F32)
    lane = lax.broadcasted_iota(jnp.int32, (ROWS, LANES), 1)
    for h in range(heads):
        state = jnp.dot(fold, state_ref[:, h, :], preferred_element_type=F32)
        norm = jnp.broadcast_to(norms[:, h : h + 1], (ROWS, LANES))
        hi = norm.astype(BF16).astype(F32)
        cols = jnp.where(lane == head_dim, hi, jnp.where(lane == head_dim + 1, norm - hi, 0.0))
        out_ref[h] = cols.astype(BF16)
        out_ref[h, :, :head_dim] = state.astype(BF16)
        out_ref[h, TAIL_ROW : TAIL_ROW + 2, :head_dim] = tail_ref[:, h * head_dim : (h + 1) * head_dim]
    copies[4].wait()


def turn_block(in_ref, out_ref):
    for j in range(out_ref.shape[0] // LANES):
        at = slice(j * LANES, (j + 1) * LANES)
        out_ref[at, :] = in_ref[:, at].T


def scale_block(in_ref, gain_ref, out_ref):
    for j in range(in_ref.shape[1] // LANES):
        at = slice(j * LANES, (j + 1) * LANES)
        out_ref[:, at] = (in_ref[:, at].astype(F32) * gain_ref[j : j + 1, :]).astype(BF16)


def ffn_weights_kernel(down_ref, gate_ref, up_ref, gain_ref, turned_ref, both_ref):
    hidden = gate_ref.shape[0]
    turn_block(down_ref, turned_ref)
    scale_block(gate_ref, gain_ref, both_ref.at[:hidden])
    scale_block(up_ref, gain_ref, both_ref.at[hidden:])


def mixer_weights_kernel(groups, held, *refs):
    out_ref, slot_ref, wide_ref = refs[9:12]
    copies = fetch(tuple(zip(refs[:9], refs[12:21])), refs[21])
    in_ref, leaf_ref, parent_ref, owner_ref, query_ref, key_ref, value_ref, gate_ref, gain_ref = refs[12:21]
    for copy in copies:
        copy.wait()
    row = 0
    for part in (query_ref, key_ref, value_ref, gate_ref):
        scale_block(part, gain_ref, wide_ref.at[row : row + part.shape[0]])
        row += part.shape[0]
    dev = lax.axis_index("req")
    count = 2 * held
    total_dev = groups * count
    column = dev // count
    place = (dev % count) // 2
    core = dev % 2
    per = leaf_ref.shape[0] // total_dev

    def slot(row):
        k = (place ^ ((row % count) // 2)) + jnp.where((row % 2) == core, 0, held)
        return jnp.where((row // count) == column, k, count)

    for k in range(groups):
        target = dev ^ (k * count)
        for s in range(per):
            leaf = leaf_ref[target * per + s]
            middle = parent_ref[leaf]
            root = parent_ref[middle]
            for i, node in enumerate((leaf, middle, root)):
                slot_ref[(k * per + s) * 3 + i] = slot(owner_ref[node])
    turn_block(in_ref, out_ref)


def select_kernel(shifts, slot_ref, mine_ref, other_ref, *rest):
    outs, pool = rest[:-1], rest[-1]
    held, heads = mine_ref.shape[:2]
    per = outs[0].shape[0]
    for n in range(held):
        pool[n] = mine_ref[n]
        pool[held + n] = other_ref[n]
    pool[2 * held] = jnp.zeros(pool.shape[1:], BF16)
    rows = lax.broadcasted_iota(jnp.int32, (ROWS, LANES), 0)
    is_tail = (rows >= TAIL_ROW) & (rows < TAIL_ROW + 2)
    for out, k in zip(outs, shifts):
        for s in range(per):
            at = [slot_ref[(k * per + s) * 3 + i] for i in range(3)]
            for h in range(heads):
                first, second, third = [pool[a, h].astype(F32) for a in at]
                total = first + jnp.where(is_tail, 0.0, second + third)
                out[s, h] = split_norm(total, 112)


def tp_place():
    index = lax.axis_index("tp")
    return index >> 1, index & 1


def place_blocks(scratch, blocks):
    x, z = tp_place()
    rows = blocks[0].shape[1]
    for k, block in enumerate(blocks):
        source = x ^ k
        scratch[pl.ds(pl.multiple_of((2 * source + z) * rows, 32), rows), :] = block[0]
        scratch[pl.ds(pl.multiple_of((2 * source + 1 - z) * rows, 32), rows), :] = block[1]


def row_scale(scratch):
    squares = jnp.zeros((LANES, scratch.shape[1]), F32)
    for j in range(scratch.shape[0] // LANES):
        rows = scratch[j * LANES : (j + 1) * LANES, :].astype(F32)
        squares = squares + rows * rows
    mean = jnp.sum(squares, axis=0, keepdims=True) / scratch.shape[0]
    return lax.rsqrt(mean + EPSILON)


def silu(v):
    return v / (1.0 + jnp.exp(-v))


def local_kernel(
    total_req, own_ref, r1_ref, r3_ref, r2_ref, token_ref, weight_ref, kept_ref,
    taps_ref, conv_ref, silu_ref, scores_ref, den_ref, right_ref, turned_ref, scratch,
):
    place_blocks(scratch, [own_ref, r1_ref, r2_ref, r3_ref])
    del kept_ref
    scale = row_scale(scratch)
    heads = scores_ref.shape[0]
    proj = jnp.dot(weight_ref[...], scratch[...], preferred_element_type=F32) * scale
    value_dim = conv_ref.shape[0]
    narrow = (proj.shape[0] - 2 * value_dim) // 2
    queries = proj[:narrow]
    keys = proj[narrow : 2 * narrow]
    values = proj[2 * narrow : 2 * narrow + value_dim].astype(BF16).astype(F32)
    gates = proj[2 * narrow + value_dim :]
    per = right_ref.shape[1] // ROWS
    feat_dim = queries.shape[0] // heads
    tokens = token_ref.shape[1]
    ids = token_ref[...]
    slot = jnp.where(ids >= total_req, per, ids - lax.axis_index("req") * per)
    lane = lax.broadcasted_iota(jnp.int32, (1, tokens), 1)
    start = jnp.zeros((1, tokens), jnp.int32)
    for s in range(per):
        amount = jnp.sum((slot == s).astype(jnp.int32), axis=1, keepdims=True)
        start = start + jnp.where(slot > s, amount, 0)
    position = lane - start
    source = lax.broadcasted_iota(jnp.int32, (tokens, tokens), 0)
    target = lax.broadcasted_iota(jnp.int32, (tokens, tokens), 1)
    allowed = (source >= start) & (source <= target)
    turned = jnp.concatenate([taps_ref[...], jnp.zeros((5, taps_ref.shape[1]), F32)], axis=0).T
    turned_ref[...] = turned
    taps = turned
    conv_ref[...] = (
        taps[:, 0:1] * values
        + taps[:, 1:2] * jnp.where(position >= 1, pltpu.roll(values, 1, axis=1), 0.0)
        + taps[:, 2:3] * jnp.where(position >= 2, pltpu.roll(values, 2, axis=1), 0.0)
    )
    silu_ref[...] = silu(gates)
    payload_row = lax.broadcasted_iota(jnp.int32, (ROWS, tokens), 0)
    lag_one = (position == 0) & (payload_row == TAIL_ROW + 1)
    lag_two = ((position == 0) & (payload_row == TAIL_ROW)) | ((position == 1) & (payload_row == TAIL_ROW + 1))
    half = feat_dim // 2
    one = (lax.broadcasted_iota(jnp.int32, (half, tokens), 0) == 0).astype(F32)
    for h in range(heads):
        query = queries[h * feat_dim : (h + 1) * feat_dim]
        key = keys[h * feat_dim : (h + 1) * feat_dim]
        blocks = [query * feat_dim ** (-0.25)]
        for gap in range(half):
            other = query if gap == 0 else pltpu.roll(query, feat_dim - gap, axis=0)
            blocks.append(query * other * (2.0 * feat_dim) ** (-0.5))
        blocks.append(query[:half] * query[half:] * (2.0 * feat_dim) ** (-0.5))
        blocks.append(one)
        feature = jnp.concatenate(blocks, axis=0)
        for s in range(per):
            member = slot == s
            at = slice(s * ROWS, (s + 1) * ROWS)
            right_ref[h, at, :tokens] = jnp.where(member, feature, 0.0).astype(BF16)
            right_ref[h, at, tokens : 2 * tokens] = (member & lag_one).astype(F32).astype(BF16)
            right_ref[h, at, 2 * tokens :] = (member & lag_two).astype(F32).astype(BF16)
        dots = lax.dot_general(
            key, query, (((0,), (0,)), ((), ())), preferred_element_type=F32, precision=lax.Precision.HIGHEST
        )
        scores = jnp.where(allowed, 1.0 + dots * feat_dim ** (-0.5) + dots * dots * (1.0 / (2.0 * feat_dim)), 0.0)
        den_ref[h] = jnp.sum(scores, axis=0, keepdims=True)
        scores_ref[h] = scores.astype(BF16)


def stack_kernel(first_ref, second_ref, out_ref):
    out_ref[0] = first_ref[...]
    out_ref[1] = second_ref[...]


def mix_kernel(
    conv_ref, silu_ref, scores_ref, den_ref, right_ref, taps_ref, p0_ref, p1_ref, p2_ref, p3_ref,
    out_weight_ref, *rest,
):
    outs, attended_ref = rest[:4], rest[4]
    per, heads = p0_ref.shape[:2]
    head_dim = attended_ref.shape[0] // heads
    tokens = attended_ref.shape[1]
    for h in range(heads):
        states = []
        for s in range(per):
            total = (
                p0_ref[s, h].astype(F32) + p1_ref[s, h].astype(F32) + p2_ref[s, h].astype(F32) + p3_ref[s, h].astype(F32)
            )
            states.append(split_norm(total, head_dim))
        reached = lax.dot_general(
            jnp.concatenate(states, axis=0), right_ref[h], (((0,), (0,)), ((), ())), preferred_element_type=F32
        )
        prefix_num = reached[:head_dim, :tokens]
        prefix_den = reached[head_dim : head_dim + 1, :tokens] + reached[head_dim + 1 : head_dim + 2, :tokens]
        at = slice(h * head_dim, (h + 1) * head_dim)
        taps = taps_ref[at, :]
        conv = (
            conv_ref[at, :]
            + taps[:, 1:2] * reached[:head_dim, tokens : 2 * tokens]
            + taps[:, 2:3] * reached[:head_dim, 2 * tokens :]
        )
        mixed = (conv * silu_ref[at, :]).astype(BF16)
        local_num = jnp.dot(mixed, scores_ref[h], preferred_element_type=F32)
        attended_ref[at, :] = ((local_num + prefix_num) / (den_ref[h] + prefix_den)).astype(BF16)
    spread_blocks(outs, out_weight_ref, attended_ref[...])


def spread_blocks(outs, weight_ref, right):
    x, z = tp_place()
    rows = outs[0].shape[1]
    for k, out in enumerate(outs):
        to = x ^ k
        for half, at in ((0, 2 * to + z), (1, 2 * to + 1 - z)):
            block = weight_ref[pl.ds(pl.multiple_of(at * rows, 32), rows), :]
            out[half] = jnp.dot(block, right, preferred_element_type=F32).astype(out.dtype)


def ffn_kernel(own_ref, r1_ref, r3_ref, r2_ref, both_ref, down_ref, *rest):
    outs, scratch = rest[:4], rest[4]
    place_blocks(scratch, [own_ref, r1_ref, r2_ref, r3_ref])
    scale = row_scale(scratch)
    hidden = both_ref.shape[0] // 2
    both = jnp.dot(both_ref[...], scratch[...], preferred_element_type=F32) * scale
    gate, up = both[:hidden], both[hidden:]
    spread_blocks(outs, down_ref, (silu(gate) * up).astype(BF16))


def shards(
    stream, token_req, request_leaf, parent, owner_map, node_state, node_norm, node_tail, mixer_gain, ffn_gain,
    query_weight, key_weight, value_weight, conv_gate_weight, conv_kernel, out_weight, ffn_gate, ffn_up, ffn_down,
):
    tokens, width = stream.shape
    heads, feats, head_dim = node_state.shape[1:]
    feat_dim = query_weight.shape[1] // heads
    model = value_weight.shape[0]
    req_size = lax.axis_size("req")
    tp_size = lax.axis_size("tp")
    y_size, z_size = 4, req_size // 8
    per = request_leaf.shape[0] // req_size

    def along_x(array, k):
        return lax.ppermute(array, "tp", [(i, i ^ (2 * k)) for i in range(tp_size)])

    def across_z(array):
        return lax.ppermute(array, "tp", [(i, i ^ 1) for i in range(tp_size)])

    def along_z(array, k):
        return lax.ppermute(array, "req", [(i, i ^ (2 * k)) for i in range(req_size)])

    def across_core(array):
        return lax.ppermute(array, "req", [(i, i ^ 1) for i in range(req_size)])

    def along_y(array, k):
        return lax.ppermute(array, "req", [(i, i ^ (2 * z_size * k)) for i in range(req_size)])

    order = (2, 1, 3)

    fold = jnp.asarray(fold_matrix(feat_dim, feats), BF16)
    def in_hbm(array):
        return pltpu.with_memory_space_constraint(array, pltpu.HBM)

    state_in = jnp.transpose(node_state[0], (1, 0, 2))
    own = stream.T
    hbm = pl.BlockSpec(memory_space=pltpu.HBM)
    fold_in = (fold, state_in, node_norm[0], node_tail[0], own)
    payload, own_near = pl.pallas_call(
        fold_kernel,
        out_shape=[sds((heads, ROWS, LANES), BF16), sds(own.shape, BF16)],
        in_specs=[hbm] * len(fold_in),
        out_specs=[VMEM] * 2,
        scratch_shapes=[pltpu.VMEM(a.shape, BF16) for a in fold_in[:4]] + [pltpu.SemaphoreType.DMA((len(fold_in),))],
        compiler_params=PARAMS,
        name="fold",
    )(*[in_hbm(a) for a in fold_in])
    gain_rows = model // LANES

    def gain_block(gain):
        return jnp.pad(gain.reshape(gain_rows, LANES), ((0, -gain_rows % 8), (0, 0)))

    narrow = (query_weight.T, key_weight.T, value_weight.T, conv_gate_weight.T)
    ready_in = (out_weight, request_leaf, parent, owner_map, *narrow, gain_block(mixer_gain))
    out_turned, slots, wide_weight = pl.pallas_call(
        functools.partial(mixer_weights_kernel, y_size, z_size),
        out_shape=[
            sds(out_weight.shape[::-1], BF16),
            sds((y_size * per * 3,), jnp.int32),
            sds((sum(a.shape[0] for a in narrow), model), BF16),
        ],
        in_specs=[hbm] * len(ready_in),
        out_specs=[VMEM, SMEM, VMEM],
        scratch_shapes=[
            pltpu.SMEM(a.shape, a.dtype) if a.dtype == jnp.int32 else pltpu.VMEM(a.shape, a.dtype) for a in ready_in
        ]
        + [pltpu.SemaphoreType.DMA((len(ready_in),))],
        compiler_params=PARAMS,
        name="mixer_weights",
    )(*[in_hbm(a) for a in ready_in])
    from_z = {k: along_z(payload, k) for k in order}

    pair = call(stack_kernel, sds((2, width, tokens), BF16), [VMEM] * 2, (own_near, across_z(own)), name="stack_pair")
    rows = {k: along_x(pair, k) for k in order}

    held_pair, out_turned, *arrived = lax.optimization_barrier(
        (pair, out_turned, from_z[1], from_z[2], from_z[3])
    )
    mine = jnp.stack([payload, *arrived])
    other = across_core(mine)
    def select(shifts, held, name):
        return call(
            functools.partial(select_kernel, shifts),
            [sds((per, heads, ROWS, LANES), BF16)] * len(shifts),
            [SMEM] + [VMEM] * 2,
            (slots, *held),
            scratch=[pltpu.VMEM((2 * z_size + 1, heads, ROWS, LANES), BF16)],
            name=name,
        )

    sent = dict(zip(order, select(order, (mine, other), "select_sent")))
    mine, other, sent = lax.optimization_barrier((mine, other, sent))
    [kept] = select((0,), (mine, other), "select_kept")
    from_y = {k: along_y(sent[k], k) for k in order}

    local = call(
        functools.partial(local_kernel, request_leaf.shape[0]),
        [
            sds((width, tokens), F32),
            sds((width, tokens), F32),
            sds((heads, tokens, tokens), BF16),
            sds((heads, 1, tokens), F32),
            sds((heads, per * ROWS, 3 * tokens), BF16),
            sds((width, 8), F32),
        ],
        [VMEM] * 6 + [pl.BlockSpec(memory_space=pl.ANY), VMEM],
        (
            pair, rows[1], rows[3], rows[2], token_req.reshape(1, tokens), wide_weight, kept, conv_kernel,
        ),
        scratch=[pltpu.VMEM((model, tokens), BF16)],
        name="local",
    )
    parts = call(
        mix_kernel,
        [sds((2, width, tokens), F32)] + [sds((2, width, tokens), BF16)] * 3,
        [VMEM] * 11,
        (*local, kept, from_y[2], from_y[1], from_y[3], out_turned),
        scratch=[pltpu.VMEM((width, tokens), BF16)],
        name="mix",
    )
    got = {k: along_x(parts[k], k) for k in order}
    share = parts[0] + got[2].astype(F32) + got[1].astype(F32) + got[3].astype(F32)
    crossing, down_in = lax.optimization_barrier((jnp.stack([share[1], share[0]]).astype(BF16), ffn_down))
    share_peer = across_z(crossing)
    ffn_shape = ffn_gate.shape[::-1]
    ready = call(
        ffn_weights_kernel,
        [sds(down_in.shape[::-1], BF16), sds((2 * ffn_shape[0], ffn_shape[1]), BF16)],
        [VMEM] * 4,
        (down_in, ffn_gate.T, ffn_up.T, gain_block(ffn_gain)),
        name="ffn_weights",
    )
    updated = (held_pair.astype(F32) + share + share_peer.astype(F32)).astype(BF16)
    updated, down_turned, gate_up = lax.optimization_barrier((updated, *ready))

    wide = {k: along_x(updated, k) for k in order}
    downs = call(
        ffn_kernel,
        [sds((2, width, tokens), F32)] + [sds((2, width, tokens), BF16)] * 3,
        [VMEM] * 6,
        (updated, wide[1], wide[3], wide[2], gate_up, down_turned),
        scratch=[pltpu.VMEM((model, tokens), BF16)],
        name="ffn",
    )
    back = {k: along_x(downs[k], k) for k in order}
    down_share = downs[0] + back[2].astype(F32) + back[1].astype(F32) + back[3].astype(F32)
    down_peer = across_z(down_share[1].astype(BF16))
    result = updated[0].astype(F32) + down_share[0] + down_peer.astype(F32)
    return result.astype(BF16).T


def solution(mesh):
    in_specs = (
        P("req", "tp"), P("req"), P(), P(), P(), P("req", "tp", None, None), P("req", "tp", None), P("req", None, "tp"),
        P(), P(), P(None, "tp"), P(None, "tp"), P(None, "tp"), P(None, "tp"), P(None, "tp"), P("tp", None),
        P(None, "tp"), P(None, "tp"), P("tp", None),
    )
    return jax.shard_map(shards, mesh=mesh, in_specs=in_specs, out_specs=P("req", "tp"), check_vma=False)
```

```python
import functools

import jax
import jax.numpy as jnp
import numpy as np
from jax import lax
from jax.experimental import pallas as pl
from jax.experimental.pallas import tpu as pltpu
from jax.sharding import PartitionSpec as P

EPSILON = 1e-05
ROWS = 160
LANES = 128
TAIL_ROW = 153
F32 = jnp.float32
BF16 = jnp.bfloat16

VMEM = pl.BlockSpec(memory_space=pltpu.VMEM)
SMEM = pl.BlockSpec(memory_space=pltpu.SMEM)
PARAMS = pltpu.CompilerParams(vmem_limit_bytes=12 * 1024 * 1024)


def call(kernel, out_shape, specs, args, scratch=(), name=None):
    single = not isinstance(out_shape, (list, tuple))
    return pl.pallas_call(
        kernel,
        out_shape=out_shape,
        in_specs=specs,
        out_specs=VMEM if single else [VMEM] * len(out_shape),
        scratch_shapes=list(scratch),
        compiler_params=PARAMS,
        name=name,
    )(*args)


def sds(shape, dtype):
    return jax.ShapeDtypeStruct(shape, dtype)


def fold_matrix(feat_dim, feat_count):
    fold = np.zeros((ROWS, feat_count), np.float32)
    row = 0
    for i in range(feat_dim):
        fold[row, 1 + i] = 1
        row += 1
    for gap in range(feat_dim // 2 + 1):
        for i in range(feat_dim if gap < feat_dim // 2 else feat_dim // 2):
            j = (i + gap) % feat_dim
            fold[row, 1 + feat_dim + feat_dim * i + j] = 1
            fold[row, 1 + feat_dim + feat_dim * j + i] = 1
            row += 1
    fold[row, 0] = 1
    return fold


def split_norm(total, head_dim):
    rounded = total.astype(BF16).astype(F32)
    lost = pltpu.roll(total - rounded, 1, axis=1)
    lane = lax.broadcasted_iota(jnp.int32, total.shape, 1)
    return jnp.where(lane == head_dim + 1, total + lost, total).astype(BF16)


def fetch(pairs, sems):
    copies = [pltpu.make_async_copy(a, b, sems.at[i]) for i, (a, b) in enumerate(pairs)]
    for copy in copies:
        copy.start()
    return copies


def fold_kernel(
    fold_hbm, state_hbm, norm_hbm, tail_hbm, own_hbm, out_ref, own_ref, fold_ref, state_ref, norm_ref, tail_ref, sems
):
    copies = fetch(
        (
            (state_hbm, state_ref), (fold_hbm, fold_ref), (norm_hbm, norm_ref), (tail_hbm, tail_ref),
            (own_hbm, own_ref),
        ),
        sems,
    )
    for copy in copies[:4]:
        copy.wait()
    feats, heads, head_dim = state_ref.shape
    fold = fold_ref[...]
    norms = lax.dot_general(fold, norm_ref[...], (((1,), (1,)), ((), ())), preferred_element_type=F32)
    lane = lax.broadcasted_iota(jnp.int32, (ROWS, LANES), 1)
    for h in range(heads):
        state = jnp.dot(fold, state_ref[:, h, :], preferred_element_type=F32)
        norm = jnp.broadcast_to(norms[:, h : h + 1], (ROWS, LANES))
        hi = norm.astype(BF16).astype(F32)
        cols = jnp.where(lane == head_dim, hi, jnp.where(lane == head_dim + 1, norm - hi, 0.0))
        out_ref[h] = cols.astype(BF16)
        out_ref[h, :, :head_dim] = state.astype(BF16)
        out_ref[h, TAIL_ROW : TAIL_ROW + 2, :head_dim] = tail_ref[:, h * head_dim : (h + 1) * head_dim]
    copies[4].wait()


def turn_block(in_ref, out_ref):
    for j in range(out_ref.shape[0] // LANES):
        at = slice(j * LANES, (j + 1) * LANES)
        out_ref[at, :] = in_ref[:, at].T


def scale_block(in_ref, gain_ref, out_ref):
    for j in range(in_ref.shape[1] // LANES):
        at = slice(j * LANES, (j + 1) * LANES)
        out_ref[:, at] = (in_ref[:, at].astype(F32) * gain_ref[j : j + 1, :]).astype(BF16)


def ffn_weights_kernel(down_ref, gate_ref, up_ref, gain_ref, turned_ref, gate_out_ref, up_out_ref):
    turn_block(down_ref, turned_ref)
    scale_block(gate_ref, gain_ref, gate_out_ref)
    scale_block(up_ref, gain_ref, up_out_ref)


def mixer_weights_kernel(groups, held, *refs):
    out_ref, slot_ref, wide_ref = refs[9:12]
    copies = fetch(tuple(zip(refs[:9], refs[12:21])), refs[21])
    in_ref, leaf_ref, parent_ref, owner_ref, query_ref, key_ref, value_ref, gate_ref, gain_ref = refs[12:21]
    for copy in copies:
        copy.wait()
    row = 0
    for part in (query_ref, key_ref, value_ref, gate_ref):
        scale_block(part, gain_ref, wide_ref.at[row : row + part.shape[0]])
        row += part.shape[0]
    dev = lax.axis_index("req")
    count = 2 * held
    total_dev = groups * count
    column = dev // count
    place = (dev % count) // 2
    core = dev % 2
    per = leaf_ref.shape[0] // total_dev

    def slot(row):
        k = (place ^ ((row % count) // 2)) + jnp.where((row % 2) == core, 0, held)
        return jnp.where((row // count) == column, k, count)

    for k in range(groups):
        target = dev ^ (k * count)
        for s in range(per):
            leaf = leaf_ref[target * per + s]
            middle = parent_ref[leaf]
            root = parent_ref[middle]
            for i, node in enumerate((leaf, middle, root)):
                slot_ref[(k * per + s) * 3 + i] = slot(owner_ref[node])
    turn_block(in_ref, out_ref)


def select_kernel(shifts, slot_ref, mine_ref, other_ref, *rest):
    outs, pool = rest[:-1], rest[-1]
    held, heads = mine_ref.shape[:2]
    per = outs[0].shape[0]
    for n in range(held):
        pool[n] = mine_ref[n]
        pool[held + n] = other_ref[n]
    pool[2 * held] = jnp.zeros(pool.shape[1:], BF16)
    rows = lax.broadcasted_iota(jnp.int32, (ROWS, LANES), 0)
    is_tail = (rows >= TAIL_ROW) & (rows < TAIL_ROW + 2)
    for out, k in zip(outs, shifts):
        for s in range(per):
            at = [slot_ref[(k * per + s) * 3 + i] for i in range(3)]
            for h in range(heads):
                first, second, third = [pool[a, h].astype(F32) for a in at]
                total = first + jnp.where(is_tail, 0.0, second + third)
                out[s, h] = split_norm(total, 112)


def tp_place():
    index = lax.axis_index("tp")
    return index >> 1, index & 1


def place_blocks(scratch, blocks):
    x, z = tp_place()
    rows = blocks[0].shape[1]
    for k, block in enumerate(blocks):
        source = x ^ k
        scratch[pl.ds(pl.multiple_of((2 * source + z) * rows, 32), rows), :] = block[0]
        scratch[pl.ds(pl.multiple_of((2 * source + 1 - z) * rows, 32), rows), :] = block[1]


def row_scale(scratch):
    squares = jnp.zeros((LANES, scratch.shape[1]), F32)
    for j in range(scratch.shape[0] // LANES):
        rows = scratch[j * LANES : (j + 1) * LANES, :].astype(F32)
        squares = squares + rows * rows
    mean = jnp.sum(squares, axis=0, keepdims=True) / scratch.shape[0]
    return lax.rsqrt(mean + EPSILON)


def silu(v):
    return v / (1.0 + jnp.exp(-v))


def local_kernel(
    total_req, own_ref, r1_ref, r3_ref, r2_ref, token_ref, weight_ref, kept_ref,
    taps_ref, conv_ref, silu_ref, scores_ref, den_ref, right_ref, turned_ref, scratch,
):
    place_blocks(scratch, [own_ref, r1_ref, r2_ref, r3_ref])
    del kept_ref
    scale = row_scale(scratch)
    heads = scores_ref.shape[0]
    proj = jnp.dot(weight_ref[...], scratch[...], preferred_element_type=F32) * scale
    value_dim = conv_ref.shape[0]
    narrow = (proj.shape[0] - 2 * value_dim) // 2
    queries = proj[:narrow]
    keys = proj[narrow : 2 * narrow]
    values = proj[2 * narrow : 2 * narrow + value_dim].astype(BF16).astype(F32)
    gates = proj[2 * narrow + value_dim :]
    per = right_ref.shape[1] // ROWS
    feat_dim = queries.shape[0] // heads
    tokens = token_ref.shape[1]
    ids = token_ref[...]
    slot = jnp.where(ids >= total_req, per, ids - lax.axis_index("req") * per)
    lane = lax.broadcasted_iota(jnp.int32, (1, tokens), 1)
    start = jnp.zeros((1, tokens), jnp.int32)
    for s in range(per):
        amount = jnp.sum((slot == s).astype(jnp.int32), axis=1, keepdims=True)
        start = start + jnp.where(slot > s, amount, 0)
    position = lane - start
    source = lax.broadcasted_iota(jnp.int32, (tokens, tokens), 0)
    target = lax.broadcasted_iota(jnp.int32, (tokens, tokens), 1)
    allowed = (source >= start) & (source <= target)
    turned = jnp.concatenate([taps_ref[...], jnp.zeros((5, taps_ref.shape[1]), F32)], axis=0).T
    turned_ref[...] = turned
    taps = turned
    conv_ref[...] = (
        taps[:, 0:1] * values
        + taps[:, 1:2] * jnp.where(position >= 1, pltpu.roll(values, 1, axis=1), 0.0)
        + taps[:, 2:3] * jnp.where(position >= 2, pltpu.roll(values, 2, axis=1), 0.0)
    )
    silu_ref[...] = silu(gates)
    payload_row = lax.broadcasted_iota(jnp.int32, (ROWS, tokens), 0)
    lag_one = (position == 0) & (payload_row == TAIL_ROW + 1)
    lag_two = ((position == 0) & (payload_row == TAIL_ROW)) | ((position == 1) & (payload_row == TAIL_ROW + 1))
    half = feat_dim // 2
    one = (lax.broadcasted_iota(jnp.int32, (half, tokens), 0) == 0).astype(F32)
    for h in range(heads):
        query = queries[h * feat_dim : (h + 1) * feat_dim]
        key = keys[h * feat_dim : (h + 1) * feat_dim]
        blocks = [query * feat_dim ** (-0.25)]
        for gap in range(half):
            other = query if gap == 0 else pltpu.roll(query, feat_dim - gap, axis=0)
            blocks.append(query * other * (2.0 * feat_dim) ** (-0.5))
        blocks.append(query[:half] * query[half:] * (2.0 * feat_dim) ** (-0.5))
        blocks.append(one)
        feature = jnp.concatenate(blocks, axis=0)
        for s in range(per):
            member = slot == s
            at = slice(s * ROWS, (s + 1) * ROWS)
            right_ref[h, at, :tokens] = jnp.where(member, feature, 0.0).astype(BF16)
            right_ref[h, at, tokens : 2 * tokens] = (member & lag_one).astype(F32).astype(BF16)
            right_ref[h, at, 2 * tokens :] = (member & lag_two).astype(F32).astype(BF16)
        dots = lax.dot_general(
            key, query, (((0,), (0,)), ((), ())), preferred_element_type=F32, precision=lax.Precision.HIGHEST
        )
        scores = jnp.where(allowed, 1.0 + dots * feat_dim ** (-0.5) + dots * dots * (1.0 / (2.0 * feat_dim)), 0.0)
        den_ref[h] = jnp.sum(scores, axis=0, keepdims=True)
        scores_ref[h] = scores.astype(BF16)


def stack_kernel(first_ref, second_ref, out_ref):
    out_ref[0] = first_ref[...]
    out_ref[1] = second_ref[...]


def mix_kernel(
    conv_ref, silu_ref, scores_ref, den_ref, right_ref, taps_ref, p0_ref, p1_ref, p2_ref, p3_ref,
    out_weight_ref, *rest,
):
    outs, attended_ref = rest[:4], rest[4]
    per, heads = p0_ref.shape[:2]
    head_dim = attended_ref.shape[0] // heads
    tokens = attended_ref.shape[1]
    for h in range(heads):
        states = []
        for s in range(per):
            total = (
                p0_ref[s, h].astype(F32) + p1_ref[s, h].astype(F32) + p2_ref[s, h].astype(F32) + p3_ref[s, h].astype(F32)
            )
            states.append(split_norm(total, head_dim))
        reached = lax.dot_general(
            jnp.concatenate(states, axis=0), right_ref[h], (((0,), (0,)), ((), ())), preferred_element_type=F32
        )
        prefix_num = reached[:head_dim, :tokens]
        prefix_den = reached[head_dim : head_dim + 1, :tokens] + reached[head_dim + 1 : head_dim + 2, :tokens]
        at = slice(h * head_dim, (h + 1) * head_dim)
        taps = taps_ref[at, :]
        conv = (
            conv_ref[at, :]
            + taps[:, 1:2] * reached[:head_dim, tokens : 2 * tokens]
            + taps[:, 2:3] * reached[:head_dim, 2 * tokens :]
        )
        mixed = (conv * silu_ref[at, :]).astype(BF16)
        local_num = jnp.dot(mixed, scores_ref[h], preferred_element_type=F32)
        attended_ref[at, :] = ((local_num + prefix_num) / (den_ref[h] + prefix_den)).astype(BF16)
    spread_blocks(outs, out_weight_ref, attended_ref[...])


def spread_blocks(outs, weight_ref, right):
    x, z = tp_place()
    rows = outs[0].shape[1]
    for k, out in enumerate(outs):
        to = x ^ k
        for half, at in ((0, 2 * to + z), (1, 2 * to + 1 - z)):
            block = weight_ref[pl.ds(pl.multiple_of(at * rows, 32), rows), :]
            out[half] = jnp.dot(block, right, preferred_element_type=F32).astype(out.dtype)


def ffn_kernel(own_ref, r1_ref, r3_ref, r2_ref, gate_ref, up_ref, down_ref, *rest):
    outs, scratch, active = rest[:4], rest[4], rest[5]
    place_blocks(scratch, [own_ref, r1_ref, r2_ref, r3_ref])
    scale = row_scale(scratch)
    rows = gate_ref.shape[0] // 2
    for half in range(2):
        at = slice(half * rows, (half + 1) * rows)
        gate = jnp.dot(gate_ref[at, :], scratch[...], preferred_element_type=F32) * scale
        up = jnp.dot(up_ref[at, :], scratch[...], preferred_element_type=F32) * scale
        active[at, :] = (silu(gate) * up).astype(BF16)
    spread_blocks(outs, down_ref, active[...])


def shards(
    stream, token_req, request_leaf, parent, owner_map, node_state, node_norm, node_tail, mixer_gain, ffn_gain,
    query_weight, key_weight, value_weight, conv_gate_weight, conv_kernel, out_weight, ffn_gate, ffn_up, ffn_down,
):
    tokens, width = stream.shape
    heads, feats, head_dim = node_state.shape[1:]
    feat_dim = query_weight.shape[1] // heads
    model = value_weight.shape[0]
    req_size = lax.axis_size("req")
    tp_size = lax.axis_size("tp")
    y_size, z_size = 4, req_size // 8
    per = request_leaf.shape[0] // req_size

    def along_x(array, k):
        return lax.ppermute(array, "tp", [(i, i ^ (2 * k)) for i in range(tp_size)])

    def across_z(array):
        return lax.ppermute(array, "tp", [(i, i ^ 1) for i in range(tp_size)])

    def along_z(array, k):
        return lax.ppermute(array, "req", [(i, i ^ (2 * k)) for i in range(req_size)])

    def across_core(array):
        return lax.ppermute(array, "req", [(i, i ^ 1) for i in range(req_size)])

    def along_y(array, k):
        return lax.ppermute(array, "req", [(i, i ^ (2 * z_size * k)) for i in range(req_size)])

    order = (2, 1, 3)

    fold = jnp.asarray(fold_matrix(feat_dim, feats), BF16)
    def in_hbm(array):
        return pltpu.with_memory_space_constraint(array, pltpu.HBM)

    state_in = jnp.transpose(node_state[0], (1, 0, 2))
    own = stream.T
    hbm = pl.BlockSpec(memory_space=pltpu.HBM)
    fold_in = (fold, state_in, node_norm[0], node_tail[0], own)
    payload, own_near = pl.pallas_call(
        fold_kernel,
        out_shape=[sds((heads, ROWS, LANES), BF16), sds(own.shape, BF16)],
        in_specs=[hbm] * len(fold_in),
        out_specs=[VMEM] * 2,
        scratch_shapes=[pltpu.VMEM(a.shape, BF16) for a in fold_in[:4]] + [pltpu.SemaphoreType.DMA((len(fold_in),))],
        compiler_params=PARAMS,
        name="fold",
    )(*[in_hbm(a) for a in fold_in])
    gain_rows = model // LANES

    def gain_block(gain):
        return jnp.pad(gain.reshape(gain_rows, LANES), ((0, -gain_rows % 8), (0, 0)))

    narrow = (query_weight.T, key_weight.T, value_weight.T, conv_gate_weight.T)
    ready_in = (out_weight, request_leaf, parent, owner_map, *narrow, gain_block(mixer_gain))
    out_turned, slots, wide_weight = pl.pallas_call(
        functools.partial(mixer_weights_kernel, y_size, z_size),
        out_shape=[
            sds(out_weight.shape[::-1], BF16),
            sds((y_size * per * 3,), jnp.int32),
            sds((sum(a.shape[0] for a in narrow), model), BF16),
        ],
        in_specs=[hbm] * len(ready_in),
        out_specs=[VMEM, SMEM, VMEM],
        scratch_shapes=[
            pltpu.SMEM(a.shape, a.dtype) if a.dtype == jnp.int32 else pltpu.VMEM(a.shape, a.dtype) for a in ready_in
        ]
        + [pltpu.SemaphoreType.DMA((len(ready_in),))],
        compiler_params=PARAMS,
        name="mixer_weights",
    )(*[in_hbm(a) for a in ready_in])
    from_z = {k: along_z(payload, k) for k in order}

    pair = call(stack_kernel, sds((2, width, tokens), BF16), [VMEM] * 2, (own_near, across_z(own)), name="stack_pair")
    rows = {k: along_x(pair, k) for k in order}

    held_pair, out_turned, *arrived = lax.optimization_barrier(
        (pair, out_turned, from_z[1], from_z[2], from_z[3])
    )
    mine = jnp.stack([payload, *arrived])
    other = across_core(mine)
    def select(shifts, held, name):
        return call(
            functools.partial(select_kernel, shifts),
            [sds((per, heads, ROWS, LANES), BF16)] * len(shifts),
            [SMEM] + [VMEM] * 2,
            (slots, *held),
            scratch=[pltpu.VMEM((2 * z_size + 1, heads, ROWS, LANES), BF16)],
            name=name,
        )

    sent = dict(zip(order, select(order, (mine, other), "select_sent")))
    mine, other, sent = lax.optimization_barrier((mine, other, sent))
    [kept] = select((0,), (mine, other), "select_kept")
    from_y = {k: along_y(sent[k], k) for k in order}

    local = call(
        functools.partial(local_kernel, request_leaf.shape[0]),
        [
            sds((width, tokens), F32),
            sds((width, tokens), F32),
            sds((heads, tokens, tokens), BF16),
            sds((heads, 1, tokens), F32),
            sds((heads, per * ROWS, 3 * tokens), BF16),
            sds((width, 8), F32),
        ],
        [VMEM] * 6 + [pl.BlockSpec(memory_space=pl.ANY), VMEM],
        (
            pair, rows[1], rows[3], rows[2], token_req.reshape(1, tokens), wide_weight, kept, conv_kernel,
        ),
        scratch=[pltpu.VMEM((model, tokens), BF16)],
        name="local",
    )
    parts = call(
        mix_kernel,
        [sds((2, width, tokens), F32)] + [sds((2, width, tokens), BF16)] * 3,
        [VMEM] * 11,
        (*local, kept, from_y[2], from_y[1], from_y[3], out_turned),
        scratch=[pltpu.VMEM((width, tokens), BF16)],
        name="mix",
    )
    got = {k: along_x(parts[k], k) for k in order}
    share = parts[0] + got[2].astype(F32) + got[1].astype(F32) + got[3].astype(F32)
    crossing, down_in = lax.optimization_barrier((jnp.stack([share[1], share[0]]).astype(BF16), ffn_down))
    share_peer = across_z(crossing)
    ffn_shape = ffn_gate.shape[::-1]
    ready = call(
        ffn_weights_kernel,
        [sds(down_in.shape[::-1], BF16), sds(ffn_shape, BF16), sds(ffn_shape, BF16)],
        [VMEM] * 4,
        (down_in, ffn_gate.T, ffn_up.T, gain_block(ffn_gain)),
        name="ffn_weights",
    )
    updated = (held_pair.astype(F32) + share + share_peer.astype(F32)).astype(BF16)
    updated, down_turned, gate_scaled, up_scaled = lax.optimization_barrier((updated, *ready))

    wide = {k: along_x(updated, k) for k in order}
    downs = call(
        ffn_kernel,
        [sds((2, width, tokens), F32)] + [sds((2, width, tokens), BF16)] * 3,
        [VMEM] * 7,
        (updated, wide[1], wide[3], wide[2], gate_scaled, up_scaled, down_turned),
        scratch=[pltpu.VMEM((model, tokens), BF16), pltpu.VMEM((ffn_shape[0], tokens), BF16)],
        name="ffn",
    )
    back = {k: along_x(downs[k], k) for k in order}
    down_share = downs[0] + back[2].astype(F32) + back[1].astype(F32) + back[3].astype(F32)
    down_peer = across_z(down_share[1].astype(BF16))
    result = updated[0].astype(F32) + down_share[0] + down_peer.astype(F32)
    return result.astype(BF16).T


def solution(mesh):
    in_specs = (
        P("req", "tp"), P("req"), P(), P(), P(), P("req", "tp", None, None), P("req", "tp", None), P("req", None, "tp"),
        P(), P(), P(None, "tp"), P(None, "tp"), P(None, "tp"), P(None, "tp"), P(None, "tp"), P("tp", None),
        P(None, "tp"), P(None, "tp"), P("tp", None),
    )
    return jax.shard_map(shards, mesh=mesh, in_specs=in_specs, out_specs=P("req", "tp"), check_vma=False)
```

```python
import functools

import jax
import jax.numpy as jnp
import numpy as np
from jax import lax
from jax.experimental import pallas as pl
from jax.experimental.pallas import tpu as pltpu
from jax.sharding import PartitionSpec as P

EPSILON = 1e-05
ROWS = 160
LANES = 128
TAIL_ROW = 153
F32 = jnp.float32
BF16 = jnp.bfloat16

VMEM = pl.BlockSpec(memory_space=pltpu.VMEM)
SMEM = pl.BlockSpec(memory_space=pltpu.SMEM)
PARAMS = pltpu.CompilerParams(vmem_limit_bytes=12 * 1024 * 1024)


def call(kernel, out_shape, specs, args, scratch=(), name=None):
    single = not isinstance(out_shape, (list, tuple))
    return pl.pallas_call(
        kernel,
        out_shape=out_shape,
        in_specs=specs,
        out_specs=VMEM if single else [VMEM] * len(out_shape),
        scratch_shapes=list(scratch),
        compiler_params=PARAMS,
        name=name,
    )(*args)


def sds(shape, dtype):
    return jax.ShapeDtypeStruct(shape, dtype)


def fold_matrix(feat_dim, feat_count):
    fold = np.zeros((ROWS, feat_count), np.float32)
    row = 0
    for i in range(feat_dim):
        fold[row, 1 + i] = 1
        row += 1
    for gap in range(feat_dim // 2 + 1):
        for i in range(feat_dim if gap < feat_dim // 2 else feat_dim // 2):
            j = (i + gap) % feat_dim
            fold[row, 1 + feat_dim + feat_dim * i + j] = 1
            fold[row, 1 + feat_dim + feat_dim * j + i] = 1
            row += 1
    fold[row, 0] = 1
    return fold


def split_norm(total, head_dim):
    rounded = total.astype(BF16).astype(F32)
    lost = pltpu.roll(total - rounded, 1, axis=1)
    lane = lax.broadcasted_iota(jnp.int32, total.shape, 1)
    return jnp.where(lane == head_dim + 1, total + lost, total).astype(BF16)


def fetch(pairs, sems):
    copies = [pltpu.make_async_copy(a, b, sems.at[i]) for i, (a, b) in enumerate(pairs)]
    for copy in copies:
        copy.start()
    return copies


def fold_kernel(
    fold_hbm, state_hbm, norm_hbm, tail_hbm, own_hbm, out_ref, own_ref, fold_ref, state_ref, norm_ref, tail_ref, sems
):
    copies = fetch(
        (
            (state_hbm, state_ref), (fold_hbm, fold_ref), (norm_hbm, norm_ref), (tail_hbm, tail_ref),
            (own_hbm, own_ref),
        ),
        sems,
    )
    for copy in copies[:4]:
        copy.wait()
    feats, heads, head_dim = state_ref.shape
    fold = fold_ref[...]
    norms = lax.dot_general(fold, norm_ref[...], (((1,), (1,)), ((), ())), preferred_element_type=F32)
    lane = lax.broadcasted_iota(jnp.int32, (ROWS, LANES), 1)
    for h in range(heads):
        state = jnp.dot(fold, state_ref[:, h, :], preferred_element_type=F32)
        norm = jnp.broadcast_to(norms[:, h : h + 1], (ROWS, LANES))
        hi = norm.astype(BF16).astype(F32)
        cols = jnp.where(lane == head_dim, hi, jnp.where(lane == head_dim + 1, norm - hi, 0.0))
        out_ref[h] = cols.astype(BF16)
        out_ref[h, :, :head_dim] = state.astype(BF16)
        out_ref[h, TAIL_ROW : TAIL_ROW + 2, :head_dim] = tail_ref[:, h * head_dim : (h + 1) * head_dim]
    copies[4].wait()


def turn_block(in_ref, out_ref):
    for j in range(out_ref.shape[0] // LANES):
        at = slice(j * LANES, (j + 1) * LANES)
        out_ref[at, :] = in_ref[:, at].T


def scale_block(in_ref, gain_ref, out_ref):
    for j in range(in_ref.shape[1] // LANES):
        at = slice(j * LANES, (j + 1) * LANES)
        out_ref[:, at] = (in_ref[:, at].astype(F32) * gain_ref[j : j + 1, :]).astype(BF16)


def ready_ffn_weights(down_ref, gate_ref, up_ref, gain_ref, turned_ref, gate_out_ref, up_out_ref):
    turn_block(down_ref, turned_ref)
    scale_block(gate_ref, gain_ref, gate_out_ref)
    scale_block(up_ref, gain_ref, up_out_ref)


def early_weights_kernel(*refs):
    @pl.when((lax.axis_index("req") & 1) == 1)
    def _():
        ready_ffn_weights(*refs)


def late_weights_kernel(*refs):
    core = lax.axis_index("req") & 1

    @pl.when(core == 0)
    def _():
        ready_ffn_weights(*refs[:4], *refs[7:])

    @pl.when(core == 1)
    def _():
        for have, out in zip(refs[4:7], refs[7:]):
            out[...] = have[...]


def mixer_weights_kernel(groups, held, *refs):
    out_ref, slot_ref, wide_ref = refs[9:12]
    copies = fetch(tuple(zip(refs[:9], refs[12:21])), refs[21])
    in_ref, leaf_ref, parent_ref, owner_ref, query_ref, key_ref, value_ref, gate_ref, gain_ref = refs[12:21]
    for copy in copies:
        copy.wait()
    row = 0
    for part in (query_ref, key_ref, value_ref, gate_ref):
        scale_block(part, gain_ref, wide_ref.at[row : row + part.shape[0]])
        row += part.shape[0]
    dev = lax.axis_index("req")
    count = 2 * held
    total_dev = groups * count
    column = dev // count
    place = (dev % count) // 2
    core = dev % 2
    per = leaf_ref.shape[0] // total_dev

    def slot(row):
        k = (place ^ ((row % count) // 2)) + jnp.where((row % 2) == core, 0, held)
        return jnp.where((row // count) == column, k, count)

    for k in range(groups):
        target = dev ^ (k * count)
        for s in range(per):
            leaf = leaf_ref[target * per + s]
            middle = parent_ref[leaf]
            root = parent_ref[middle]
            for i, node in enumerate((leaf, middle, root)):
                slot_ref[(k * per + s) * 3 + i] = slot(owner_ref[node])
    turn_block(in_ref, out_ref)


def select_kernel(shifts, slot_ref, mine_ref, other_ref, *rest):
    outs, pool = rest[:-1], rest[-1]
    held, heads = mine_ref.shape[:2]
    per = outs[0].shape[0]
    for n in range(held):
        pool[n] = mine_ref[n]
        pool[held + n] = other_ref[n]
    pool[2 * held] = jnp.zeros(pool.shape[1:], BF16)
    rows = lax.broadcasted_iota(jnp.int32, (ROWS, LANES), 0)
    is_tail = (rows >= TAIL_ROW) & (rows < TAIL_ROW + 2)
    for out, k in zip(outs, shifts):
        for s in range(per):
            at = [slot_ref[(k * per + s) * 3 + i] for i in range(3)]
            for h in range(heads):
                first, second, third = [pool[a, h].astype(F32) for a in at]
                total = first + jnp.where(is_tail, 0.0, second + third)
                out[s, h] = split_norm(total, 112)


def tp_place():
    index = lax.axis_index("tp")
    return index >> 1, index & 1


def place_blocks(scratch, blocks):
    x, z = tp_place()
    rows = blocks[0].shape[1]
    for k, block in enumerate(blocks):
        source = x ^ k
        scratch[pl.ds(pl.multiple_of((2 * source + z) * rows, 32), rows), :] = block[0]
        scratch[pl.ds(pl.multiple_of((2 * source + 1 - z) * rows, 32), rows), :] = block[1]


def row_scale(scratch):
    squares = jnp.zeros((LANES, scratch.shape[1]), F32)
    for j in range(scratch.shape[0] // LANES):
        rows = scratch[j * LANES : (j + 1) * LANES, :].astype(F32)
        squares = squares + rows * rows
    mean = jnp.sum(squares, axis=0, keepdims=True) / scratch.shape[0]
    return lax.rsqrt(mean + EPSILON)


def silu(v):
    return v / (1.0 + jnp.exp(-v))


def local_kernel(
    total_req, own_ref, r1_ref, r3_ref, r2_ref, token_ref, weight_ref, kept_ref,
    taps_ref, conv_ref, silu_ref, scores_ref, den_ref, right_ref, turned_ref, scratch,
):
    place_blocks(scratch, [own_ref, r1_ref, r2_ref, r3_ref])
    del kept_ref
    scale = row_scale(scratch)
    heads = scores_ref.shape[0]
    proj = jnp.dot(weight_ref[...], scratch[...], preferred_element_type=F32) * scale
    value_dim = conv_ref.shape[0]
    narrow = (proj.shape[0] - 2 * value_dim) // 2
    queries = proj[:narrow]
    keys = proj[narrow : 2 * narrow]
    values = proj[2 * narrow : 2 * narrow + value_dim].astype(BF16).astype(F32)
    gates = proj[2 * narrow + value_dim :]
    per = right_ref.shape[1] // ROWS
    feat_dim = queries.shape[0] // heads
    tokens = token_ref.shape[1]
    ids = token_ref[...]
    slot = jnp.where(ids >= total_req, per, ids - lax.axis_index("req") * per)
    lane = lax.broadcasted_iota(jnp.int32, (1, tokens), 1)
    start = jnp.zeros((1, tokens), jnp.int32)
    for s in range(per):
        amount = jnp.sum((slot == s).astype(jnp.int32), axis=1, keepdims=True)
        start = start + jnp.where(slot > s, amount, 0)
    position = lane - start
    source = lax.broadcasted_iota(jnp.int32, (tokens, tokens), 0)
    target = lax.broadcasted_iota(jnp.int32, (tokens, tokens), 1)
    allowed = (source >= start) & (source <= target)
    turned = jnp.concatenate([taps_ref[...], jnp.zeros((5, taps_ref.shape[1]), F32)], axis=0).T
    turned_ref[...] = turned
    taps = turned
    conv_ref[...] = (
        taps[:, 0:1] * values
        + taps[:, 1:2] * jnp.where(position >= 1, pltpu.roll(values, 1, axis=1), 0.0)
        + taps[:, 2:3] * jnp.where(position >= 2, pltpu.roll(values, 2, axis=1), 0.0)
    )
    silu_ref[...] = silu(gates)
    payload_row = lax.broadcasted_iota(jnp.int32, (ROWS, tokens), 0)
    lag_one = (position == 0) & (payload_row == TAIL_ROW + 1)
    lag_two = ((position == 0) & (payload_row == TAIL_ROW)) | ((position == 1) & (payload_row == TAIL_ROW + 1))
    half = feat_dim // 2
    one = (lax.broadcasted_iota(jnp.int32, (half, tokens), 0) == 0).astype(F32)
    for h in range(heads):
        query = queries[h * feat_dim : (h + 1) * feat_dim]
        key = keys[h * feat_dim : (h + 1) * feat_dim]
        blocks = [query * feat_dim ** (-0.25)]
        for gap in range(half):
            other = query if gap == 0 else pltpu.roll(query, feat_dim - gap, axis=0)
            blocks.append(query * other * (2.0 * feat_dim) ** (-0.5))
        blocks.append(query[:half] * query[half:] * (2.0 * feat_dim) ** (-0.5))
        blocks.append(one)
        feature = jnp.concatenate(blocks, axis=0)
        for s in range(per):
            member = slot == s
            at = slice(s * ROWS, (s + 1) * ROWS)
            right_ref[h, at, :tokens] = jnp.where(member, feature, 0.0).astype(BF16)
            right_ref[h, at, tokens : 2 * tokens] = (member & lag_one).astype(F32).astype(BF16)
            right_ref[h, at, 2 * tokens :] = (member & lag_two).astype(F32).astype(BF16)
        dots = lax.dot_general(
            key, query, (((0,), (0,)), ((), ())), preferred_element_type=F32, precision=lax.Precision.HIGHEST
        )
        scores = jnp.where(allowed, 1.0 + dots * feat_dim ** (-0.5) + dots * dots * (1.0 / (2.0 * feat_dim)), 0.0)
        den_ref[h] = jnp.sum(scores, axis=0, keepdims=True)
        scores_ref[h] = scores.astype(BF16)


def stack_kernel(first_ref, second_ref, out_ref):
    out_ref[0] = first_ref[...]
    out_ref[1] = second_ref[...]


def mix_kernel(
    conv_ref, silu_ref, scores_ref, den_ref, right_ref, taps_ref, p0_ref, p1_ref, p2_ref, p3_ref,
    out_weight_ref, *rest,
):
    outs, attended_ref = rest[:4], rest[4]
    per, heads = p0_ref.shape[:2]
    head_dim = attended_ref.shape[0] // heads
    tokens = attended_ref.shape[1]
    for h in range(heads):
        states = []
        for s in range(per):
            total = (
                p0_ref[s, h].astype(F32) + p1_ref[s, h].astype(F32) + p2_ref[s, h].astype(F32) + p3_ref[s, h].astype(F32)
            )
            states.append(split_norm(total, head_dim))
        reached = lax.dot_general(
            jnp.concatenate(states, axis=0), right_ref[h], (((0,), (0,)), ((), ())), preferred_element_type=F32
        )
        prefix_num = reached[:head_dim, :tokens]
        prefix_den = reached[head_dim : head_dim + 1, :tokens] + reached[head_dim + 1 : head_dim + 2, :tokens]
        at = slice(h * head_dim, (h + 1) * head_dim)
        taps = taps_ref[at, :]
        conv = (
            conv_ref[at, :]
            + taps[:, 1:2] * reached[:head_dim, tokens : 2 * tokens]
            + taps[:, 2:3] * reached[:head_dim, 2 * tokens :]
        )
        mixed = (conv * silu_ref[at, :]).astype(BF16)
        local_num = jnp.dot(mixed, scores_ref[h], preferred_element_type=F32)
        attended_ref[at, :] = ((local_num + prefix_num) / (den_ref[h] + prefix_den)).astype(BF16)
    spread_blocks(outs, out_weight_ref, attended_ref[...])


def spread_blocks(outs, weight_ref, right):
    x, z = tp_place()
    rows = outs[0].shape[1]
    for k, out in enumerate(outs):
        to = x ^ k
        for half, at in ((0, 2 * to + z), (1, 2 * to + 1 - z)):
            block = weight_ref[pl.ds(pl.multiple_of(at * rows, 32), rows), :]
            out[half] = jnp.dot(block, right, preferred_element_type=F32).astype(out.dtype)


def ffn_kernel(own_ref, r1_ref, r3_ref, r2_ref, gate_ref, up_ref, down_ref, *rest):
    outs, scratch = rest[:4], rest[4]
    place_blocks(scratch, [own_ref, r1_ref, r2_ref, r3_ref])
    scale = row_scale(scratch)
    gate = jnp.dot(gate_ref[...], scratch[...], preferred_element_type=F32) * scale
    up = jnp.dot(up_ref[...], scratch[...], preferred_element_type=F32) * scale
    spread_blocks(outs, down_ref, (silu(gate) * up).astype(BF16))


def shards(
    stream, token_req, request_leaf, parent, owner_map, node_state, node_norm, node_tail, mixer_gain, ffn_gain,
    query_weight, key_weight, value_weight, conv_gate_weight, conv_kernel, out_weight, ffn_gate, ffn_up, ffn_down,
):
    tokens, width = stream.shape
    heads, feats, head_dim = node_state.shape[1:]
    feat_dim = query_weight.shape[1] // heads
    model = value_weight.shape[0]
    req_size = lax.axis_size("req")
    tp_size = lax.axis_size("tp")
    y_size, z_size = 4, req_size // 8
    per = request_leaf.shape[0] // req_size

    def along_x(array, k):
        return lax.ppermute(array, "tp", [(i, i ^ (2 * k)) for i in range(tp_size)])

    def across_z(array):
        return lax.ppermute(array, "tp", [(i, i ^ 1) for i in range(tp_size)])

    def along_z(array, k):
        return lax.ppermute(array, "req", [(i, i ^ (2 * k)) for i in range(req_size)])

    def across_core(array):
        return lax.ppermute(array, "req", [(i, i ^ 1) for i in range(req_size)])

    def along_y(array, k):
        return lax.ppermute(array, "req", [(i, i ^ (2 * z_size * k)) for i in range(req_size)])

    order = (2, 1, 3)

    fold = jnp.asarray(fold_matrix(feat_dim, feats), BF16)
    def in_hbm(array):
        return pltpu.with_memory_space_constraint(array, pltpu.HBM)

    state_in = jnp.transpose(node_state[0], (1, 0, 2))
    own = stream.T
    hbm = pl.BlockSpec(memory_space=pltpu.HBM)
    fold_in = (fold, state_in, node_norm[0], node_tail[0], own)
    payload, own_near = pl.pallas_call(
        fold_kernel,
        out_shape=[sds((heads, ROWS, LANES), BF16), sds(own.shape, BF16)],
        in_specs=[hbm] * len(fold_in),
        out_specs=[VMEM] * 2,
        scratch_shapes=[pltpu.VMEM(a.shape, BF16) for a in fold_in[:4]] + [pltpu.SemaphoreType.DMA((len(fold_in),))],
        compiler_params=PARAMS,
        name="fold",
    )(*[in_hbm(a) for a in fold_in])
    gain_rows = model // LANES

    def gain_block(gain):
        return jnp.pad(gain.reshape(gain_rows, LANES), ((0, -gain_rows % 8), (0, 0)))

    narrow = (query_weight.T, key_weight.T, value_weight.T, conv_gate_weight.T)
    ready_in = (out_weight, request_leaf, parent, owner_map, *narrow, gain_block(mixer_gain))
    out_turned, slots, wide_weight = pl.pallas_call(
        functools.partial(mixer_weights_kernel, y_size, z_size),
        out_shape=[
            sds(out_weight.shape[::-1], BF16),
            sds((y_size * per * 3,), jnp.int32),
            sds((sum(a.shape[0] for a in narrow), model), BF16),
        ],
        in_specs=[hbm] * len(ready_in),
        out_specs=[VMEM, SMEM, VMEM],
        scratch_shapes=[
            pltpu.SMEM(a.shape, a.dtype) if a.dtype == jnp.int32 else pltpu.VMEM(a.shape, a.dtype) for a in ready_in
        ]
        + [pltpu.SemaphoreType.DMA((len(ready_in),))],
        compiler_params=PARAMS,
        name="mixer_weights",
    )(*[in_hbm(a) for a in ready_in])
    from_z = {k: along_z(payload, k) for k in order}

    pair = call(stack_kernel, sds((2, width, tokens), BF16), [VMEM] * 2, (own_near, across_z(own)), name="stack_pair")
    rows = {k: along_x(pair, k) for k in order}

    held_pair, out_turned, *arrived = lax.optimization_barrier(
        (pair, out_turned, from_z[1], from_z[2], from_z[3])
    )
    mine = jnp.stack([payload, *arrived])
    other = across_core(mine)
    def select(shifts, held, name):
        return call(
            functools.partial(select_kernel, shifts),
            [sds((per, heads, ROWS, LANES), BF16)] * len(shifts),
            [SMEM] + [VMEM] * 2,
            (slots, *held),
            scratch=[pltpu.VMEM((2 * z_size + 1, heads, ROWS, LANES), BF16)],
            name=name,
        )

    sent = dict(zip(order, select(order, (mine, other), "select_sent")))
    mine, other, sent = lax.optimization_barrier((mine, other, sent))
    [kept] = select((0,), (mine, other), "select_kept")
    from_y = {k: along_y(sent[k], k) for k in order}

    local = call(
        functools.partial(local_kernel, request_leaf.shape[0]),
        [
            sds((width, tokens), F32),
            sds((width, tokens), F32),
            sds((heads, tokens, tokens), BF16),
            sds((heads, 1, tokens), F32),
            sds((heads, per * ROWS, 3 * tokens), BF16),
            sds((width, 8), F32),
        ],
        [VMEM] * 6 + [pl.BlockSpec(memory_space=pl.ANY), VMEM],
        (
            pair, rows[1], rows[3], rows[2], token_req.reshape(1, tokens), wide_weight, kept, conv_kernel,
        ),
        scratch=[pltpu.VMEM((model, tokens), BF16)],
        name="local",
    )
    parts = call(
        mix_kernel,
        [sds((2, width, tokens), F32)] + [sds((2, width, tokens), BF16)] * 3,
        [VMEM] * 11,
        (*local, kept, from_y[2], from_y[1], from_y[3], out_turned),
        scratch=[pltpu.VMEM((width, tokens), BF16)],
        name="mix",
    )
    got = {k: along_x(parts[k], k) for k in order}
    share = parts[0] + got[2].astype(F32) + got[1].astype(F32) + got[3].astype(F32)
    crossing, down_in = lax.optimization_barrier((jnp.stack([share[1], share[0]]).astype(BF16), ffn_down))
    ffn_shape = ffn_gate.shape[::-1]
    ready_shape = [sds(down_in.shape[::-1], BF16), sds(ffn_shape, BF16), sds(ffn_shape, BF16)]
    raw = (down_in, ffn_gate.T, ffn_up.T, gain_block(ffn_gain))
    early = call(early_weights_kernel, ready_shape, [VMEM] * 4, raw, name="early_weights")
    crossing, *early = lax.optimization_barrier((crossing, *early))
    share_peer = across_z(crossing)
    ready = call(late_weights_kernel, ready_shape, [VMEM] * 7, (*raw, *early), name="late_weights")
    updated = (held_pair.astype(F32) + share + share_peer.astype(F32)).astype(BF16)
    updated, down_turned, gate_scaled, up_scaled = lax.optimization_barrier((updated, *ready))

    wide = {k: along_x(updated, k) for k in order}
    downs = call(
        ffn_kernel,
        [sds((2, width, tokens), F32)] + [sds((2, width, tokens), BF16)] * 3,
        [VMEM] * 7,
        (updated, wide[1], wide[3], wide[2], gate_scaled, up_scaled, down_turned),
        scratch=[pltpu.VMEM((model, tokens), BF16)],
        name="ffn",
    )
    back = {k: along_x(downs[k], k) for k in order}
    down_share = downs[0] + back[2].astype(F32) + back[1].astype(F32) + back[3].astype(F32)
    down_peer = across_z(down_share[1].astype(BF16))
    result = updated[0].astype(F32) + down_share[0] + down_peer.astype(F32)
    return result.astype(BF16).T


def solution(mesh):
    in_specs = (
        P("req", "tp"), P("req"), P(), P(), P(), P("req", "tp", None, None), P("req", "tp", None), P("req", None, "tp"),
        P(), P(), P(None, "tp"), P(None, "tp"), P(None, "tp"), P(None, "tp"), P(None, "tp"), P("tp", None),
        P(None, "tp"), P(None, "tp"), P("tp", None),
    )
    return jax.shard_map(shards, mesh=mesh, in_specs=in_specs, out_specs=P("req", "tp"), check_vma=False)
```

```python
import functools

import jax
import jax.numpy as jnp
import numpy as np
from jax import lax
from jax.experimental import pallas as pl
from jax.experimental.pallas import tpu as pltpu
from jax.sharding import PartitionSpec as P

EPSILON = 1e-05
ROWS = 160
LANES = 128
TAIL_ROW = 153
F32 = jnp.float32
BF16 = jnp.bfloat16

VMEM = pl.BlockSpec(memory_space=pltpu.VMEM)
SMEM = pl.BlockSpec(memory_space=pltpu.SMEM)
PARAMS = pltpu.CompilerParams(vmem_limit_bytes=12 * 1024 * 1024)


def call(kernel, out_shape, specs, args, scratch=(), name=None):
    single = not isinstance(out_shape, (list, tuple))
    return pl.pallas_call(
        kernel,
        out_shape=out_shape,
        in_specs=specs,
        out_specs=VMEM if single else [VMEM] * len(out_shape),
        scratch_shapes=list(scratch),
        compiler_params=PARAMS,
        name=name,
    )(*args)


def sds(shape, dtype):
    return jax.ShapeDtypeStruct(shape, dtype)


def fold_matrix(feat_dim, feat_count):
    fold = np.zeros((ROWS, feat_count), np.float32)
    row = 0
    for i in range(feat_dim):
        fold[row, 1 + i] = 1
        row += 1
    for gap in range(feat_dim // 2 + 1):
        for i in range(feat_dim if gap < feat_dim // 2 else feat_dim // 2):
            j = (i + gap) % feat_dim
            fold[row, 1 + feat_dim + feat_dim * i + j] = 1
            fold[row, 1 + feat_dim + feat_dim * j + i] = 1
            row += 1
    fold[row, 0] = 1
    return fold


def split_norm(total, head_dim):
    rounded = total.astype(BF16).astype(F32)
    lost = pltpu.roll(total - rounded, 1, axis=1)
    lane = lax.broadcasted_iota(jnp.int32, total.shape, 1)
    return jnp.where(lane == head_dim + 1, total + lost, total).astype(BF16)


def fetch(pairs, sems):
    copies = [pltpu.make_async_copy(a, b, sems.at[i]) for i, (a, b) in enumerate(pairs)]
    for copy in copies:
        copy.start()
    return copies


def fold_kernel(
    fold_hbm, state_hbm, norm_hbm, tail_hbm, own_hbm, out_ref, own_ref, fold_ref, state_ref, norm_ref, tail_ref, sems
):
    copies = fetch(
        (
            (state_hbm, state_ref), (fold_hbm, fold_ref), (norm_hbm, norm_ref), (tail_hbm, tail_ref),
            (own_hbm, own_ref),
        ),
        sems,
    )
    for copy in copies[:4]:
        copy.wait()
    feats, heads, head_dim = state_ref.shape
    fold = fold_ref[...]
    norms = lax.dot_general(fold, norm_ref[...], (((1,), (1,)), ((), ())), preferred_element_type=F32)
    lane = lax.broadcasted_iota(jnp.int32, (ROWS, LANES), 1)
    for h in range(heads):
        state = jnp.dot(fold, state_ref[:, h, :], preferred_element_type=F32)
        norm = jnp.broadcast_to(norms[:, h : h + 1], (ROWS, LANES))
        hi = norm.astype(BF16).astype(F32)
        cols = jnp.where(lane == head_dim, hi, jnp.where(lane == head_dim + 1, norm - hi, 0.0))
        out_ref[h] = cols.astype(BF16)
        out_ref[h, :, :head_dim] = state.astype(BF16)
        out_ref[h, TAIL_ROW : TAIL_ROW + 2, :head_dim] = tail_ref[:, h * head_dim : (h + 1) * head_dim]
    copies[4].wait()


def turn_block(in_ref, out_ref):
    for j in range(out_ref.shape[0] // LANES):
        at = slice(j * LANES, (j + 1) * LANES)
        out_ref[at, :] = in_ref[:, at].T


def scale_block(in_ref, gain_ref, out_ref):
    for j in range(in_ref.shape[1] // LANES):
        at = slice(j * LANES, (j + 1) * LANES)
        out_ref[:, at] = (in_ref[:, at].astype(F32) * gain_ref[j : j + 1, :]).astype(BF16)


def ffn_weights_kernel(down_ref, gate_ref, up_ref, gain_ref, turned_ref, gate_out_ref, up_out_ref):
    turn_block(down_ref, turned_ref)
    scale_block(gate_ref, gain_ref, gate_out_ref)
    scale_block(up_ref, gain_ref, up_out_ref)


def mixer_weights_kernel(groups, held, *refs):
    out_ref, slot_ref, wide_ref = refs[9:12]
    copies = fetch(tuple(zip(refs[:9], refs[12:21])), refs[21])
    in_ref, leaf_ref, parent_ref, owner_ref, query_ref, key_ref, value_ref, gate_ref, gain_ref = refs[12:21]
    for copy in copies:
        copy.wait()
    row = 0
    for part in (query_ref, key_ref, value_ref, gate_ref):
        scale_block(part, gain_ref, wide_ref.at[row : row + part.shape[0]])
        row += part.shape[0]
    dev = lax.axis_index("req")
    count = 2 * held
    total_dev = groups * count
    column = dev // count
    place = (dev % count) // 2
    core = dev % 2
    per = leaf_ref.shape[0] // total_dev

    def slot(row):
        k = (place ^ ((row % count) // 2)) + jnp.where((row % 2) == core, 0, held)
        return jnp.where((row // count) == column, k, count)

    for k in range(groups):
        target = dev ^ (k * count)
        for s in range(per):
            leaf = leaf_ref[target * per + s]
            middle = parent_ref[leaf]
            root = parent_ref[middle]
            for i, node in enumerate((leaf, middle, root)):
                slot_ref[(k * per + s) * 3 + i] = slot(owner_ref[node])
    turn_block(in_ref, out_ref)


def select_kernel(shifts, slot_ref, mine_ref, other_ref, *rest):
    outs, pool = rest[:-1], rest[-1]
    held, heads = mine_ref.shape[:2]
    per = outs[0].shape[0]
    for n in range(held):
        pool[n] = mine_ref[n]
        pool[held + n] = other_ref[n]
    pool[2 * held] = jnp.zeros(pool.shape[1:], BF16)
    rows = lax.broadcasted_iota(jnp.int32, (ROWS, LANES), 0)
    is_tail = (rows >= TAIL_ROW) & (rows < TAIL_ROW + 2)
    for out, k in zip(outs, shifts):
        for s in range(per):
            at = [slot_ref[(k * per + s) * 3 + i] for i in range(3)]
            for h in range(heads):
                first, second, third = [pool[a, h].astype(F32) for a in at]
                total = first + jnp.where(is_tail, 0.0, second + third)
                out[s, h] = split_norm(total, 112)


def tp_place():
    index = lax.axis_index("tp")
    return index >> 1, index & 1


OTHER_CORE = {0: 0, 1: 3, 2: 1, 3: 2}


def partner(k):
    return jnp.where((lax.axis_index("req") & 1) == 1, OTHER_CORE[k], k)


def place_blocks(scratch, blocks):
    x, z = tp_place()
    rows = blocks[0].shape[1]
    for k, block in enumerate(blocks):
        source = x ^ partner(k)
        scratch[pl.ds(pl.multiple_of((2 * source + z) * rows, 32), rows), :] = block[0]
        scratch[pl.ds(pl.multiple_of((2 * source + 1 - z) * rows, 32), rows), :] = block[1]


def row_scale(scratch):
    squares = jnp.zeros((LANES, scratch.shape[1]), F32)
    for j in range(scratch.shape[0] // LANES):
        rows = scratch[j * LANES : (j + 1) * LANES, :].astype(F32)
        squares = squares + rows * rows
    mean = jnp.sum(squares, axis=0, keepdims=True) / scratch.shape[0]
    return lax.rsqrt(mean + EPSILON)


def silu(v):
    return v / (1.0 + jnp.exp(-v))


def local_kernel(
    total_req, own_ref, r1_ref, r3_ref, r2_ref, token_ref, weight_ref, kept_ref,
    taps_ref, conv_ref, silu_ref, scores_ref, den_ref, right_ref, turned_ref, scratch,
):
    place_blocks(scratch, [own_ref, r1_ref, r2_ref, r3_ref])
    del kept_ref
    scale = row_scale(scratch)
    heads = scores_ref.shape[0]
    proj = jnp.dot(weight_ref[...], scratch[...], preferred_element_type=F32) * scale
    value_dim = conv_ref.shape[0]
    narrow = (proj.shape[0] - 2 * value_dim) // 2
    queries = proj[:narrow]
    keys = proj[narrow : 2 * narrow]
    values = proj[2 * narrow : 2 * narrow + value_dim].astype(BF16).astype(F32)
    gates = proj[2 * narrow + value_dim :]
    per = right_ref.shape[1] // ROWS
    feat_dim = queries.shape[0] // heads
    tokens = token_ref.shape[1]
    ids = token_ref[...]
    slot = jnp.where(ids >= total_req, per, ids - lax.axis_index("req") * per)
    lane = lax.broadcasted_iota(jnp.int32, (1, tokens), 1)
    start = jnp.zeros((1, tokens), jnp.int32)
    for s in range(per):
        amount = jnp.sum((slot == s).astype(jnp.int32), axis=1, keepdims=True)
        start = start + jnp.where(slot > s, amount, 0)
    position = lane - start
    source = lax.broadcasted_iota(jnp.int32, (tokens, tokens), 0)
    target = lax.broadcasted_iota(jnp.int32, (tokens, tokens), 1)
    allowed = (source >= start) & (source <= target)
    turned = jnp.concatenate([taps_ref[...], jnp.zeros((5, taps_ref.shape[1]), F32)], axis=0).T
    turned_ref[...] = turned
    taps = turned
    conv_ref[...] = (
        taps[:, 0:1] * values
        + taps[:, 1:2] * jnp.where(position >= 1, pltpu.roll(values, 1, axis=1), 0.0)
        + taps[:, 2:3] * jnp.where(position >= 2, pltpu.roll(values, 2, axis=1), 0.0)
    )
    silu_ref[...] = silu(gates)
    payload_row = lax.broadcasted_iota(jnp.int32, (ROWS, tokens), 0)
    lag_one = (position == 0) & (payload_row == TAIL_ROW + 1)
    lag_two = ((position == 0) & (payload_row == TAIL_ROW)) | ((position == 1) & (payload_row == TAIL_ROW + 1))
    half = feat_dim // 2
    one = (lax.broadcasted_iota(jnp.int32, (half, tokens), 0) == 0).astype(F32)
    for h in range(heads):
        query = queries[h * feat_dim : (h + 1) * feat_dim]
        key = keys[h * feat_dim : (h + 1) * feat_dim]
        blocks = [query * feat_dim ** (-0.25)]
        for gap in range(half):
            other = query if gap == 0 else pltpu.roll(query, feat_dim - gap, axis=0)
            blocks.append(query * other * (2.0 * feat_dim) ** (-0.5))
        blocks.append(query[:half] * query[half:] * (2.0 * feat_dim) ** (-0.5))
        blocks.append(one)
        feature = jnp.concatenate(blocks, axis=0)
        for s in range(per):
            member = slot == s
            at = slice(s * ROWS, (s + 1) * ROWS)
            right_ref[h, at, :tokens] = jnp.where(member, feature, 0.0).astype(BF16)
            right_ref[h, at, tokens : 2 * tokens] = (member & lag_one).astype(F32).astype(BF16)
            right_ref[h, at, 2 * tokens :] = (member & lag_two).astype(F32).astype(BF16)
        dots = lax.dot_general(
            key, query, (((0,), (0,)), ((), ())), preferred_element_type=F32, precision=lax.Precision.HIGHEST
        )
        scores = jnp.where(allowed, 1.0 + dots * feat_dim ** (-0.5) + dots * dots * (1.0 / (2.0 * feat_dim)), 0.0)
        den_ref[h] = jnp.sum(scores, axis=0, keepdims=True)
        scores_ref[h] = scores.astype(BF16)


def stack_kernel(first_ref, second_ref, out_ref):
    out_ref[0] = first_ref[...]
    out_ref[1] = second_ref[...]


def mix_kernel(
    conv_ref, silu_ref, scores_ref, den_ref, right_ref, taps_ref, p0_ref, p1_ref, p2_ref, p3_ref,
    out_weight_ref, *rest,
):
    outs, attended_ref = rest[:4], rest[4]
    per, heads = p0_ref.shape[:2]
    head_dim = attended_ref.shape[0] // heads
    tokens = attended_ref.shape[1]
    for h in range(heads):
        states = []
        for s in range(per):
            total = (
                p0_ref[s, h].astype(F32) + p1_ref[s, h].astype(F32) + p2_ref[s, h].astype(F32) + p3_ref[s, h].astype(F32)
            )
            states.append(split_norm(total, head_dim))
        reached = lax.dot_general(
            jnp.concatenate(states, axis=0), right_ref[h], (((0,), (0,)), ((), ())), preferred_element_type=F32
        )
        prefix_num = reached[:head_dim, :tokens]
        prefix_den = reached[head_dim : head_dim + 1, :tokens] + reached[head_dim + 1 : head_dim + 2, :tokens]
        at = slice(h * head_dim, (h + 1) * head_dim)
        taps = taps_ref[at, :]
        conv = (
            conv_ref[at, :]
            + taps[:, 1:2] * reached[:head_dim, tokens : 2 * tokens]
            + taps[:, 2:3] * reached[:head_dim, 2 * tokens :]
        )
        mixed = (conv * silu_ref[at, :]).astype(BF16)
        local_num = jnp.dot(mixed, scores_ref[h], preferred_element_type=F32)
        attended_ref[at, :] = ((local_num + prefix_num) / (den_ref[h] + prefix_den)).astype(BF16)
    spread_blocks(outs, out_weight_ref, attended_ref[...])


def spread_blocks(outs, weight_ref, right):
    x, z = tp_place()
    rows = outs[0].shape[1]
    for k, out in enumerate(outs):
        to = x ^ partner(k)
        for half, at in ((0, 2 * to + z), (1, 2 * to + 1 - z)):
            block = weight_ref[pl.ds(pl.multiple_of(at * rows, 32), rows), :]
            out[half] = jnp.dot(block, right, preferred_element_type=F32).astype(out.dtype)


def ffn_kernel(own_ref, r1_ref, r3_ref, r2_ref, gate_ref, up_ref, down_ref, *rest):
    outs, scratch = rest[:4], rest[4]
    place_blocks(scratch, [own_ref, r1_ref, r2_ref, r3_ref])
    scale = row_scale(scratch)
    gate = jnp.dot(gate_ref[...], scratch[...], preferred_element_type=F32) * scale
    up = jnp.dot(up_ref[...], scratch[...], preferred_element_type=F32) * scale
    spread_blocks(outs, down_ref, (silu(gate) * up).astype(BF16))


def shards(
    stream, token_req, request_leaf, parent, owner_map, node_state, node_norm, node_tail, mixer_gain, ffn_gain,
    query_weight, key_weight, value_weight, conv_gate_weight, conv_kernel, out_weight, ffn_gate, ffn_up, ffn_down,
):
    tokens, width = stream.shape
    heads, feats, head_dim = node_state.shape[1:]
    feat_dim = query_weight.shape[1] // heads
    model = value_weight.shape[0]
    req_size = lax.axis_size("req")
    tp_size = lax.axis_size("tp")
    y_size, z_size = 4, req_size // 8
    per = request_leaf.shape[0] // req_size

    def along_x(array, k):
        pairs = [
            (r * tp_size + i, r * tp_size + (i ^ (2 * (OTHER_CORE[k] if r % 2 else k))))
            for r in range(req_size)
            for i in range(tp_size)
        ]
        return lax.ppermute(array, ("req", "tp"), pairs)

    def across_z(array):
        return lax.ppermute(array, "tp", [(i, i ^ 1) for i in range(tp_size)])

    def along_z(array, k):
        return lax.ppermute(array, "req", [(i, i ^ (2 * k)) for i in range(req_size)])

    def across_core(array):
        return lax.ppermute(array, "req", [(i, i ^ 1) for i in range(req_size)])

    def along_y(array, k):
        return lax.ppermute(array, "req", [(i, i ^ (2 * z_size * k)) for i in range(req_size)])

    order = (2, 1, 3)

    fold = jnp.asarray(fold_matrix(feat_dim, feats), BF16)
    def in_hbm(array):
        return pltpu.with_memory_space_constraint(array, pltpu.HBM)

    state_in = jnp.transpose(node_state[0], (1, 0, 2))
    own = stream.T
    hbm = pl.BlockSpec(memory_space=pltpu.HBM)
    fold_in = (fold, state_in, node_norm[0], node_tail[0], own)
    payload, own_near = pl.pallas_call(
        fold_kernel,
        out_shape=[sds((heads, ROWS, LANES), BF16), sds(own.shape, BF16)],
        in_specs=[hbm] * len(fold_in),
        out_specs=[VMEM] * 2,
        scratch_shapes=[pltpu.VMEM(a.shape, BF16) for a in fold_in[:4]] + [pltpu.SemaphoreType.DMA((len(fold_in),))],
        compiler_params=PARAMS,
        name="fold",
    )(*[in_hbm(a) for a in fold_in])
    gain_rows = model // LANES

    def gain_block(gain):
        return jnp.pad(gain.reshape(gain_rows, LANES), ((0, -gain_rows % 8), (0, 0)))

    narrow = (query_weight.T, key_weight.T, value_weight.T, conv_gate_weight.T)
    ready_in = (out_weight, request_leaf, parent, owner_map, *narrow, gain_block(mixer_gain))
    out_turned, slots, wide_weight = pl.pallas_call(
        functools.partial(mixer_weights_kernel, y_size, z_size),
        out_shape=[
            sds(out_weight.shape[::-1], BF16),
            sds((y_size * per * 3,), jnp.int32),
            sds((sum(a.shape[0] for a in narrow), model), BF16),
        ],
        in_specs=[hbm] * len(ready_in),
        out_specs=[VMEM, SMEM, VMEM],
        scratch_shapes=[
            pltpu.SMEM(a.shape, a.dtype) if a.dtype == jnp.int32 else pltpu.VMEM(a.shape, a.dtype) for a in ready_in
        ]
        + [pltpu.SemaphoreType.DMA((len(ready_in),))],
        compiler_params=PARAMS,
        name="mixer_weights",
    )(*[in_hbm(a) for a in ready_in])
    from_z = {k: along_z(payload, k) for k in order}

    pair = call(stack_kernel, sds((2, width, tokens), BF16), [VMEM] * 2, (own_near, across_z(own)), name="stack_pair")
    rows = {k: along_x(pair, k) for k in order}

    held_pair, out_turned, *arrived = lax.optimization_barrier(
        (pair, out_turned, from_z[1], from_z[2], from_z[3])
    )
    mine = jnp.stack([payload, *arrived])
    other = across_core(mine)
    def select(shifts, held, name):
        return call(
            functools.partial(select_kernel, shifts),
            [sds((per, heads, ROWS, LANES), BF16)] * len(shifts),
            [SMEM] + [VMEM] * 2,
            (slots, *held),
            scratch=[pltpu.VMEM((2 * z_size + 1, heads, ROWS, LANES), BF16)],
            name=name,
        )

    sent = dict(zip(order, select(order, (mine, other), "select_sent")))
    mine, other, sent = lax.optimization_barrier((mine, other, sent))
    [kept] = select((0,), (mine, other), "select_kept")
    from_y = {k: along_y(sent[k], k) for k in order}

    local = call(
        functools.partial(local_kernel, request_leaf.shape[0]),
        [
            sds((width, tokens), F32),
            sds((width, tokens), F32),
            sds((heads, tokens, tokens), BF16),
            sds((heads, 1, tokens), F32),
            sds((heads, per * ROWS, 3 * tokens), BF16),
            sds((width, 8), F32),
        ],
        [VMEM] * 6 + [pl.BlockSpec(memory_space=pl.ANY), VMEM],
        (
            pair, rows[1], rows[3], rows[2], token_req.reshape(1, tokens), wide_weight, kept, conv_kernel,
        ),
        scratch=[pltpu.VMEM((model, tokens), BF16)],
        name="local",
    )
    parts = call(
        mix_kernel,
        [sds((2, width, tokens), F32)] + [sds((2, width, tokens), BF16)] * 3,
        [VMEM] * 11,
        (*local, kept, from_y[2], from_y[1], from_y[3], out_turned),
        scratch=[pltpu.VMEM((width, tokens), BF16)],
        name="mix",
    )
    got = {k: along_x(parts[k], k) for k in order}
    share = parts[0] + got[2].astype(F32) + got[1].astype(F32) + got[3].astype(F32)
    crossing, down_in = lax.optimization_barrier((jnp.stack([share[1], share[0]]).astype(BF16), ffn_down))
    share_peer = across_z(crossing)
    ffn_shape = ffn_gate.shape[::-1]
    ready = call(
        ffn_weights_kernel,
        [sds(down_in.shape[::-1], BF16), sds(ffn_shape, BF16), sds(ffn_shape, BF16)],
        [VMEM] * 4,
        (down_in, ffn_gate.T, ffn_up.T, gain_block(ffn_gain)),
        name="ffn_weights",
    )
    updated = (held_pair.astype(F32) + share + share_peer.astype(F32)).astype(BF16)
    updated, down_turned, gate_scaled, up_scaled = lax.optimization_barrier((updated, *ready))

    wide = {k: along_x(updated, k) for k in order}
    downs = call(
        ffn_kernel,
        [sds((2, width, tokens), F32)] + [sds((2, width, tokens), BF16)] * 3,
        [VMEM] * 7,
        (updated, wide[1], wide[3], wide[2], gate_scaled, up_scaled, down_turned),
        scratch=[pltpu.VMEM((model, tokens), BF16)],
        name="ffn",
    )
    back = {k: along_x(downs[k], k) for k in order}
    down_share = downs[0] + back[2].astype(F32) + back[1].astype(F32) + back[3].astype(F32)
    down_peer = across_z(down_share[1].astype(BF16))
    result = updated[0].astype(F32) + down_share[0] + down_peer.astype(F32)
    return result.astype(BF16).T


def solution(mesh):
    in_specs = (
        P("req", "tp"), P("req"), P(), P(), P(), P("req", "tp", None, None), P("req", "tp", None), P("req", None, "tp"),
        P(), P(), P(None, "tp"), P(None, "tp"), P(None, "tp"), P(None, "tp"), P(None, "tp"), P("tp", None),
        P(None, "tp"), P(None, "tp"), P("tp", None),
    )
    return jax.shard_map(shards, mesh=mesh, in_specs=in_specs, out_specs=P("req", "tp"), check_vma=False)
```
